32 devices in a mesh: groups: 2 (over y), seq: 4 (over z), chan: 4 (over x, core).
Axes of the slice: x: 2, y: 2, z: 4, core: 2. Of those that a mesh axis runs over, the one named last changes fastest.
Arguments:
- dna_bases: int32 [4096], P(('groups', 'seq')), parts along dimension 0, may hold values from 0 to 3
- w_stem: bfloat16 [768, 5, 4], P('chan'), may hold values from -2.5 to 2.5
- w_enc: bfloat16 [1536, 5, 768], P(None, None, 'chan'), may hold values from -0.09375 to 0.09375
- w_dec: bfloat16 [768, 5, 1536], P(None, None, 'chan'), may hold values from -0.0625 to 0.0625
- targets: bfloat16 [4096, 768], P(('groups', 'seq'), 'chan'), parts along dimension 0, may hold values from -6 to 6
Outputs:
- pred: bfloat16 [4096, 768], P(('groups', 'seq'), 'chan'), parts along dimension 0
- g_enc: float32 [3072, 5, 768], P(('groups', 'seq'), None, 'chan'), parts along dimension 0
- g_dec: float32 [1536, 5, 1536], P(('groups', 'seq'), None, 'chan'), parts along dimension 0
The draws below stay inside these ranges and needn't reach their ends.
There are 2 independent parts, one for each index of `groups`. The reference program is written for one: setup_inputs(seed, part) draws one part's arguments, and reference() takes and returns one part's arrays. A program takes and returns all parts, laid end to end along the dimension named above; an argument that names none is the same for every part. Nothing has to cross between parts.
Inputs may be any that keep to these rules, and one draw needn't show every extreme that they name: `dna_bases`: each entry is one of the four bases.
All inputs are finite; a program needn't handle non-finite values.
Results may differ from the reference program's by a relative error of at most 0.009.
Values may be sent and summed in bfloat16 or wider, within the bound.
A program may use at most 192 MiB of HBM per device.

```python
import math
import jax
import jax.numpy as jnp
from jax import lax

C1 = 768
C2 = 1536
KW = 5
LENGTH = 2048
N_SEQ = 4


def set_ends(drawn, stream_key, least, largest):
    spot = [jax.random.randint(jax.random.fold_in(stream_key, axis), (), 0, length) for axis, length in enumerate(drawn.shape)]
    widest = drawn.shape.index(max(drawn.shape))
    beside = spot[:widest] + [(spot[widest] + 1) % drawn.shape[widest]] + spot[widest + 1:]
    return drawn.at[tuple(spot)].set(least).at[tuple(beside)].set(largest)


def strengthened(values, key, source, target, shards_of, factor):
    def block_of(position):
        return (jnp.arange(values.shape[position]) // (values.shape[position] // shards_of)).reshape((-1,) + (1,) * (values.ndim - 1 - position))

    one_side = jax.random.permutation(key, shards_of)[block_of(target)]
    far = (block_of(target) + shards_of // 2) % shards_of
    return jnp.where((block_of(source) == one_side) | (block_of(source) == far), factor * values, values)


def shard_levels(own_key, shape, shards, least, high):
    def one(position, shards_of):
        steps = jax.random.uniform(jax.random.fold_in(jax.random.fold_in(own_key, 6), position), (shards_of,), jnp.float32, least / len(shards), high / len(shards))
        return jnp.repeat(jnp.exp(steps), shape[position] // shards_of).reshape((-1,) + (1,) * (len(shape) - position - 1))

    factor_of = one(*shards[0])
    for cut in shards[1:]:
        factor_of = factor_of * one(*cut)
    return factor_of


def noise(key, extent, spread, limit, cuts=(), kind=jnp.bfloat16):
    drawn = jax.random.normal(key, extent, jnp.float32) * spread
    if len(cuts) > 0:
        drawn = shard_levels(key, extent, cuts, -0.22, 0.18) * drawn
    return jnp.clip(drawn, min=-limit, max=limit).astype(kind)


def bell_draw_with(stream_key, dims, spread, reach, shards, heavy, kind=jnp.bfloat16):
    values = spread * jax.random.normal(stream_key, dims, jnp.float32)
    if shards:
        values = values * shard_levels(stream_key, dims, shards, -0.22, 0.18)
    return jnp.clip(strengthened(values, jax.random.fold_in(stream_key, 3), *heavy), -reach, reach).astype(kind)


def setup_inputs(seed: int = 0, part: int = 0) -> dict:
    splits = jax.random.split(jax.random.key(seed), 6)
    part_keys = jax.random.split(jax.random.fold_in(splits[5], part), 6)
    dna_bases = set_ends(jax.random.randint(part_keys[0], (LENGTH,), 0, 4), jax.random.fold_in(part_keys[0], 1), 0, 3).astype(jnp.int32)
    w_stem = noise(splits[1], (C1, KW, 4), KW ** -0.5, 2.5, ((0, 4),))
    w_enc = noise(splits[2], (C2, KW, C1), (KW * C1) ** -0.5, 0.09375, ((2, 4),))
    w_dec = noise(splits[3], (C1, KW, C2), (KW * C2) ** -0.5, 0.0625, ((2, 4),))
    targets = bell_draw_with(part_keys[4], (LENGTH, C1), 1.0, 6.0, ((0, 4), (1, 4)), (0, 1, 4, 2.0))
    return dict(dna_bases=dna_bases, w_stem=w_stem, w_enc=w_enc, w_dec=w_dec, targets=targets)


SQRT_TWO_PI = 0.7978845608028654
CUBIC = 0.044715

def gelu_value(value):
    inner = jnp.tanh(SQRT_TWO_PI * (value + CUBIC * value * value * value))
    return 0.5 * value * (1.0 + inner)

def gelu_slope(value):
    inner = jnp.tanh(SQRT_TWO_PI * (value + CUBIC * value * value * value))
    return 0.5 * (1.0 + inner) + 0.5 * value * (1.0 - inner * inner) * SQRT_TWO_PI * (1.0 + 3.0 * CUBIC * value * value)

def pad_rows(array, margin):
    return jnp.pad(array, ((margin, margin), (0, 0)))

def conv_rows(padded, weight):
    row_count = padded.shape[0] - 4
    total = jnp.zeros((row_count, weight.shape[0]), jnp.float32)
    for k in range(KW):
        total = total + jnp.dot(padded[k:k + row_count].astype(jnp.float32), weight[:, k, :].astype(jnp.float32).T)
    return total

def block_grad(cotangent, padded):
    row_count = cotangent.shape[0] // N_SEQ
    width = cotangent.shape[1]

    def one_block(total, index):
        first = index * row_count
        part = lax.dynamic_slice_in_dim(cotangent, first, row_count, 0).astype(jnp.float32)
        window = lax.dynamic_slice_in_dim(padded, first, row_count + 4, 0).astype(jnp.float32)
        pieces = [jnp.dot(part.T, window[k:k + row_count]) for k in range(KW)]
        piece = jnp.stack(pieces, axis=1).astype(jnp.bfloat16)
        return (total + lax.optimization_barrier(piece).astype(jnp.float32), None)
    start_total = jnp.zeros((width, KW, padded.shape[1]), jnp.float32)
    total, _ = lax.scan(one_block, start_total, jnp.arange(N_SEQ, dtype=jnp.int32))
    return total

def reference(dna_bases, w_stem, w_enc, w_dec, targets):
    length = dna_bases.shape[0]
    onehot = (dna_bases[:, None] == jnp.arange(4, dtype=jnp.int32)[None, :]).astype(jnp.bfloat16)
    stem_out = gelu_value(conv_rows(pad_rows(onehot, 2), w_stem)).astype(jnp.bfloat16)
    stem_pad = pad_rows(stem_out, 2)
    enc_pre = conv_rows(stem_pad, w_enc)
    active = gelu_value(enc_pre).astype(jnp.bfloat16).astype(jnp.float32)
    pooled = (0.5 * (active[0::2] + active[1::2])).astype(jnp.bfloat16)
    up_pad = pad_rows(jnp.repeat(pooled, 2, axis=0), 2)
    output = conv_rows(up_pad, w_dec) + stem_out.astype(jnp.float32)
    pred = output.astype(jnp.bfloat16)
    scale = 1.0 / math.sqrt(length)
    slope_out = ((output - targets.astype(jnp.float32)) * scale).astype(jnp.bfloat16)
    g_dec = block_grad(slope_out, up_pad)
    slope_pad = pad_rows(slope_out, 2).astype(jnp.float32)
    up_grad = jnp.zeros((length, w_dec.shape[2]), jnp.float32)
    for k in range(KW):
        up_grad = up_grad + jnp.dot(slope_pad[4 - k:4 - k + length], w_dec[:, k, :].astype(jnp.float32))
    pool_grad = up_grad[0::2] + up_grad[1::2]
    act_grad = 0.5 * jnp.repeat(pool_grad, 2, axis=0)
    pre_grad = (act_grad * gelu_slope(enc_pre)).astype(jnp.bfloat16)
    g_enc = block_grad(pre_grad, stem_pad)
    return (pred, g_enc, g_dec)
```

```python
import functools
import math

import jax
import jax.numpy as jnp
import numpy as np
from jax import lax
from jax.experimental import pallas as pl
from jax.experimental.pallas import tpu as pltpu
from jax.sharding import PartitionSpec as P

KW = 5


SQRT_TWO_PI = 0.7978845608028654
CUBIC = 0.044715


def extended(block, sides, width):
    for axis, dim in sides:
        count = lax.axis_size(axis)
        forward = [(i, i + 1) for i in range(count - 1)]
        backward = [(target, source) for source, target in forward]
        low = lax.ppermute(
            lax.slice_in_dim(block, block.shape[dim] - width, None, axis=dim), axis, forward
        )
        high = lax.ppermute(lax.slice_in_dim(block, 0, width, axis=dim), axis, backward)
        block = jnp.concatenate([low, block, high], axis=dim)
    return block


def gelu_value(value):
    inner = jnp.tanh(SQRT_TWO_PI * (value + CUBIC * value * value * value))
    return 0.5 * value * (1.0 + inner)


def gelu_slope(value):
    inner = jnp.tanh(SQRT_TWO_PI * (value + CUBIC * value * value * value))
    return 0.5 * (1.0 + inner) + 0.5 * value * (1.0 - inner * inner) * SQRT_TWO_PI * (
        1.0 + 3.0 * CUBIC * value * value
    )


def rim_cells(block, margin):
    return extended(block, (("seq", 0),), margin)


def channel_sum(partial_value):
    return lax.psum_scatter(partial_value, "chan", scatter_dimension=1, tiled=True)


def channel_gather(block):
    return lax.all_gather(block, "chan", axis=1, tiled=True)


def conv_rows(padded, weight):
    row_count = padded.shape[0] - 4
    total = jnp.zeros((row_count, weight.shape[0]), jnp.float32)
    for k in range(KW):
        total = total + lax.dot_general(
            padded[k : k + row_count],
            weight[:, k, :],
            (((1,), (1,)), ((), ())),
            preferred_element_type=jnp.float32,
        )
    return total


def grad_taps(picked, padded):
    row_count = picked.shape[0]
    pieces = [
        lax.dot_general(
            picked,
            padded[k : k + row_count],
            (((0,), (0,)), ((), ())),
            preferred_element_type=jnp.float32,
        )
        for k in range(KW)
    ]
    return jnp.stack(pieces, axis=1)


def weight_grad(cotangent, padded):
    rounded = grad_taps(cotangent, padded).astype(jnp.bfloat16)
    return lax.psum_scatter(
        lax.optimization_barrier(rounded).astype(jnp.float32),
        "seq",
        scatter_dimension=0,
        tiled=True,
    )


def general_shards(dna_bases, w_stem, w_enc, w_dec, targets):
    row_count = dna_bases.shape[0]
    devices = lax.axis_size("seq")
    length = row_count * devices
    onehot = (dna_bases[:, None] == jnp.arange(4, dtype=jnp.int32)[None, :]).astype(jnp.bfloat16)
    onehot_pad = rim_cells(onehot, 2)
    stem_out = gelu_value(conv_rows(onehot_pad, w_stem)).astype(jnp.bfloat16)
    stem_pad = rim_cells(stem_out, 2)
    enc_pre = channel_sum(conv_rows(stem_pad, w_enc))
    active = gelu_value(enc_pre).astype(jnp.bfloat16).astype(jnp.float32)
    pooled = (0.5 * active.reshape(row_count // 2, 2, -1).sum(axis=1)).astype(jnp.bfloat16)
    pooled_pad = rim_cells(pooled, 1)
    up_pad = jnp.repeat(pooled_pad, 2, axis=0)
    output = channel_sum(conv_rows(up_pad, w_dec)) + stem_out.astype(jnp.float32)
    pred = output.astype(jnp.bfloat16)
    scale = 1.0 / math.sqrt(length)
    slope_out = ((output - targets.astype(jnp.float32)) * scale).astype(jnp.bfloat16)
    slope_all = channel_gather(slope_out)
    g_dec = weight_grad(slope_all, up_pad)
    slope_pad = rim_cells(slope_all, 2)
    up_grad = jnp.zeros((row_count, w_dec.shape[2]), jnp.float32)
    for k in range(KW):
        up_grad = up_grad + jnp.dot(
            slope_pad[4 - k : 4 - k + row_count], w_dec[:, k, :], preferred_element_type=jnp.float32
        )
    pool_grad = up_grad.reshape(row_count // 2, 2, -1).sum(axis=1)
    act_grad = 0.5 * jnp.repeat(pool_grad, 2, axis=0)
    pre_grad = (act_grad * gelu_slope(enc_pre)).astype(jnp.bfloat16)
    pre_all = channel_gather(pre_grad)
    g_enc = weight_grad(pre_all, stem_pad)
    return (pred, g_enc, g_dec)


MESH_ID = pl.DeviceIdType.MESH
BF16 = jnp.bfloat16
F32 = jnp.float32
TILE = 16
SIDE = 8
VMEM_BYTES = 36 * 1024 * 1024


def send(src, dst, send_sem, recv_sem, seq, chan):
    return pltpu.make_async_remote_copy(
        src_ref=src,
        dst_ref=dst,
        send_sem=send_sem,
        recv_sem=recv_sem,
        device_id={"seq": seq, "chan": chan},
        device_id_type=MESH_ID,
    )


def greet(targets):
    barrier = pltpu.get_barrier_semaphore()
    for seq, chan in targets:
        pl.semaphore_signal(
            barrier, inc=1, device_id={"seq": seq, "chan": chan}, device_id_type=MESH_ID
        )
    pl.semaphore_wait(barrier, len(targets))


def whole_group(n, s, c):
    others = []
    for ds in range(n):
        for dc in range(n):
            if ds or dc:
                others.append((lax.rem(s + ds, n), lax.rem(c + dc, n)))
    return others


def bases_kernel(n, own_ref, all_ref, local_sem, send_sem, recv_sem):
    s, c = lax.axis_index("seq"), lax.axis_index("chan")
    peers = [lax.rem(s + d, n) for d in range(1, n)]
    greet([(p, c) for p in peers])
    copies = [
        send(own_ref, all_ref.at[s], send_sem.at[d], recv_sem.at[d], p, c)
        for d, p in enumerate(peers)
    ]
    for copy in copies:
        copy.start()
    mine = pltpu.make_async_copy(own_ref, all_ref.at[s], local_sem)
    mine.start()
    mine.wait()
    for copy in copies:
        copy.wait()


def partners(c):
    mate = c + 1 - 2 * lax.rem(c, 2)
    across = lax.rem(c + 2, 4)
    return mate, across, lax.rem(mate + 2, 4)


def span(first, count):
    return pl.ds(first, count)


def tiles(first, count, body):
    @pl.loop(0, count // TILE)
    def _(i):
        body(pl.ds(pl.multiple_of(first + i * TILE, TILE), TILE))


class Turn:
    def __init__(self, n, s, c, own, out, sems):
        self.n, self.s, self.c, self.own, self.out = n, s, c, own, out
        self.quarter_send, self.quarter_recv, self.share_send, self.share_recv, self.local = sems
        self.piece = own.shape[1] // n

    def rows(self, index):
        return pl.ds(pl.multiple_of(index * self.piece, self.piece), self.piece)

    def keep(self):
        at = self.rows(self.c)
        return pltpu.make_async_copy(self.own.at[:, at], self.out.at[self.s, :, at], self.local)

    def quarter(self, q, slot):
        at = self.rows(q)
        return send(self.own.at[:, at], self.out.at[self.s, :, at], self.quarter_send.at[q],
                    self.quarter_recv.at[slot], self.c, q)

    def itself(self, q):
        return jnp.logical_and(self.s == self.c, self.c == q)

    def start(self, q):
        pl.when(jnp.logical_not(self.itself(q)))(lambda: self.quarter(q, self.s).start())

    def share(self, slot, kind, part, to):
        at = self.rows(part)
        index = slot * 3 + kind
        return send(self.out.at[slot, :, at], self.out.at[slot, :, at], self.share_send.at[index],
                    self.share_recv.at[index], self.s, to)

    def slots(self):
        return [lax.rem(self.s + d, self.n) for d in range(self.n)]

    def forward(self, d):
        mate, across, _ = partners(self.c)
        slot = self.slots()[d]
        if d == 0:
            pl.when(self.s == self.c)(lambda: self.keep().wait())
            pl.when(self.s != self.c)(lambda: self.quarter(self.c, slot).wait_recv())
        else:
            self.quarter(self.c, slot).wait_recv()
        self.share(slot, 1, self.c, across).start()
        self.share(slot, 0, self.c, mate).start()

    def relay(self, d):
        mate, across, _ = partners(self.c)
        slot = self.slots()[d]
        self.share(slot, 1, across, across).wait_recv()
        self.share(slot, 2, across, mate).start()

    def finish(self, slot):
        mate, across, far = partners(self.c)
        self.share(slot, 0, mate, mate).wait_recv()
        self.share(slot, 2, far, mate).wait_recv()

    def end(self):
        mate, across, _ = partners(self.c)
        for slot in self.slots():
            self.share(slot, 0, self.c, mate).wait_send()
            self.share(slot, 1, self.c, across).wait_send()
            self.share(slot, 2, across, mate).wait_send()
        for q in range(self.n):
            pl.when(jnp.logical_not(self.itself(q)))(
                functools.partial(lambda q: self.quarter(q, self.s).wait_send(), q)
            )


class PairSum:
    def __init__(self, block, held, pair, s, c, chunks, sems):
        self.block, self.held, self.pair, self.s, self.c = block, held, pair, s, c
        self.chunks = chunks
        self.send_sem, self.recv_sem = sems

    def hop(self, kind, q):
        mate, across, far = partners(self.c)
        source = (lambda: self.block(mate), lambda: self.block(far), lambda: self.pair)[kind]()
        target = (mate, mate, across)[kind]
        at = span(*self.chunks[q])
        index = kind * len(self.chunks) + q
        return send(source.at[:, at], self.held.at[kind, :, at], self.send_sem.at[index],
                    self.recv_sem.at[index], self.s, target)

    def start(self, kind):
        for q in range(len(self.chunks)):
            self.hop(kind, q).start()

    def cross(self, q):
        _, across, _ = partners(self.c)
        self.hop(1, q).wait_recv()
        block = self.block(across)

        def body(at):
            self.pair[:, at, :] = (
                block[:, at, :].astype(F32) + self.held[1, :, at, :].astype(F32)
            ).astype(BF16)

        tiles(*self.chunks[q], body)
        self.hop(2, q).start()

    def arrive(self, q):
        self.hop(0, q).wait_recv()
        self.hop(2, q).wait_recv()

    def total(self, at):
        mine = self.block(self.c)[:, at, :].astype(F32)
        return mine + self.held[0, :, at, :].astype(F32) + self.held[2, :, at, :].astype(F32)

    def end(self):
        for kind in range(3):
            for q in range(len(self.chunks)):
                self.hop(kind, q).wait_send()


class PoolRelay:
    def __init__(self, n, s, c, out, right_send, left_send, recv):
        self.n, self.s, self.c, self.out = n, s, c, out
        self.right_send, self.left_send, self.recv = right_send, left_send, recv

    def hop(self, slot, step):
        sems = self.right_send if step > 0 else self.left_send
        return send(self.out.at[slot], self.out.at[slot], sems.at[slot], self.recv.at[slot],
                    self.s + step, self.c)

    def start(self):
        pl.when(self.s < self.n - 1)(lambda: self.hop(self.s, 1).start())
        pl.when(self.s > 0)(lambda: self.hop(self.s, -1).start())

    def arrive(self, d):
        low, high = self.s - d, self.s + d

        @pl.when(low >= 0)
        def _():
            self.hop(low, 1).wait_recv()
            pl.when(self.s < self.n - 1)(lambda: self.hop(low, 1).start())

        @pl.when(high < self.n)
        def _():
            self.hop(high, -1).wait_recv()
            pl.when(self.s > 0)(lambda: self.hop(high, -1).start())

    def end(self):
        for slot in range(self.n):
            pl.when(jnp.logical_and(slot <= self.s, self.s < self.n - 1))(
                functools.partial(lambda slot: self.hop(slot, 1).wait_send(), slot)
            )
            pl.when(jnp.logical_and(slot >= self.s, self.s > 0))(
                functools.partial(lambda slot: self.hop(slot, -1).wait_send(), slot)
            )


class SlopeTurn:
    def __init__(self, n, s, c, chan, out, sems):
        self.n, self.s, self.c, self.chan, self.out = n, s, c, chan, out
        self.send_sem, self.recv_sem, self.share_send, self.share_recv, self.local = sems
        self.plane = lax.rem(c, 2)

    def hop(self, to, slot):
        return send(self.chan.at[to, self.plane], self.out.at[self.s, self.plane],
                    self.send_sem.at[to], self.recv_sem.at[slot], to, self.c)

    def start(self, block):
        pl.when(block != self.s)(lambda: self.hop(block, self.s).start())

    def keep(self):
        return pltpu.make_async_copy(self.chan.at[self.s], self.out.at[self.s], self.local)

    def share(self, slot, plane):
        mate, _, _ = partners(self.c)
        spot = self.out.at[slot, plane]
        return send(spot, spot, self.share_send.at[slot], self.share_recv.at[slot], self.s, mate)

    def others(self):
        return [lax.rem(self.s + d, self.n) for d in range(1, self.n)]

    def forward(self):
        for slot in self.others():
            self.hop(self.s, slot).wait_recv()
            self.share(slot, self.plane).start()

    def finish(self):
        self.keep().wait()
        for slot in self.others():
            self.share(slot, 1 - self.plane).wait_recv()

    def end(self):
        for slot in self.others():
            self.share(slot, self.plane).wait_send()
            self.hop(slot, self.s).wait_send()


def across_rows(left, right):
    return lax.dot_general(left, right, (((0,), (0,)), ((), ())), preferred_element_type=F32)


def by_channels(left, right):
    return lax.dot_general(left, right, (((1,), (1,)), ((), ())), preferred_element_type=F32)


def train_kernel(
    n, scale, enc_chunks, dec_chunks, part_ref, stem_ref, target_ref, w_ref, stem_all_ref,
    pred_ref, g_enc_ref, g_dec_ref,
    enc_held, enc_pair, bend, pool_wide, pool_near, dec_part, dec_held, dec_pair, q_wide,
    edge, slope, chan, up, pre_own, pre_seq, ab_seq, ab_wide, pools, stems,
    enc_send, enc_recv, dec_send, dec_recv, edge_send, edge_recv, row_send, row_recv,
    right_send, left_send, pool_recv, *turn_sems,
):
    s, c = lax.axis_index("seq"), lax.axis_index("chan")
    mate, across, far = partners(c)
    rows, c2 = pool_near.shape[0], pool_wide.shape[1]
    own = rows - TILE
    c1 = stem_ref.shape[2]
    greet(whole_group(n, s, c))

    enc = PairSum(
        lambda j: part_ref.at[:, :, pl.ds(pl.multiple_of(j * c2, 128), c2)],
        enc_held, enc_pair, s, c, enc_chunks, (enc_send, enc_recv),
    )
    dec = PairSum(
        lambda j: dec_part.at[j], dec_held, dec_pair, s, c, dec_chunks, (dec_send, dec_recv)
    )
    relay = PoolRelay(n, s, c, pools, right_send, left_send, pool_recv)
    turn = Turn(n, s, c, pre_own, pre_seq, turn_sems[:5])
    slopes = SlopeTurn(n, s, c, chan, ab_seq, turn_sems[5:])

    enc.start(1)
    enc.start(0)
    edges = [
        send(target_ref.at[:, pl.ds(own - TILE, TILE)], edge.at[0], edge_send.at[0],
             edge_recv.at[0], lax.rem(s + 1, n), c),
        send(target_ref.at[:, pl.ds(0, TILE)], edge.at[1], edge_send.at[1], edge_recv.at[1],
             lax.rem(s + n - 1, n), c),
    ]
    for q in range(len(enc_chunks)):
        enc.cross(q)
    for copy in edges:
        copy.start()

    row = lax.broadcasted_iota(jnp.int32, (TILE, 1), 0)
    inside = jnp.logical_or(
        jnp.logical_and(row < SIDE, s < n - 1), jnp.logical_and(row >= SIDE, s > 0)
    )

    @pl.loop(0, stem_all_ref.shape[1] // 64)
    def _(i):
        at = pl.ds(pl.multiple_of(i * 64, 64), 64)
        for parity in range(2):
            wide = stem_all_ref[parity, pl.ds(pl.multiple_of(i * 64, TILE), 64 + TILE), :].astype(F32)
            for shift in range(3):
                first = SIDE - 1 + shift
                stems[2 * shift + parity, at, :] = wide[first : first + 64].astype(BF16)

    def enc_rows(at):
        total = enc.total(at)
        square = total * total
        inner = jnp.tanh(SQRT_TWO_PI * (total + CUBIC * square * total))
        active = (0.5 * total * (1.0 + inner)).astype(BF16).astype(F32)
        pooled = (0.5 * (active[0] + active[1])).astype(BF16).astype(F32)
        pool_wide[pl.ds(pl.multiple_of(at.start + SIDE, SIDE), TILE), :] = pooled
        bend[:, at, :] = 0.5 * (
            0.5 * (1.0 + inner)
            + 0.5 * total * (1.0 - inner * inner) * SQRT_TWO_PI * (1.0 + 3.0 * CUBIC * square)
        )

    for q in range(len(enc_chunks)):
        enc.arrive(q)
        tiles(*enc_chunks[q], enc_rows)
    pool_wide[SIDE : SIDE + TILE, :] = jnp.where(inside, pool_wide[SIDE : SIDE + TILE, :], 0.0)
    pool_wide[0:SIDE, :] = pool_wide[rows : rows + SIDE, :]
    pool_wide[rows + SIDE :, :] = pool_wide[SIDE : 2 * SIDE, :]
    for first in range(0, rows, TILE):
        for shift in range(3):
            value = pool_wide[first + SIDE - 1 + shift : first + SIDE - 1 + shift + TILE, :]
            pool_near[first : first + TILE, shift * c2 : (shift + 1) * c2] = value.astype(BF16)
    pools[s, :, :] = pool_near[TILE:, c2 : 2 * c2]

    def conv_block(j):
        at = pl.ds(pl.multiple_of(j * c1, TILE), c1)
        before, here, after = (pool_near[:, i * c2 : (i + 1) * c2] for i in range(3))
        both = by_channels(before, w_ref[0, at, :]) + by_channels(here, w_ref[2, at, :])
        both = both + by_channels(after, w_ref[4, at, :])
        single = by_channels(before, w_ref[1, at, :]) + by_channels(here, w_ref[3, at, :])
        q_wide[0:rows, :] = single
        q_wide[rows:, :] = single[0:SIDE]
        dec_part[j, 0, :, :] = (both + single).astype(BF16)
        dec_part[j, 1, :, :] = (both + q_wide[1 : rows + 1, :]).astype(BF16)

    conv_block(far)
    dec.start(1)
    relay.start()
    conv_block(across)
    for q in range(len(dec_chunks)):
        dec.cross(q)
    conv_block(mate)
    dec.start(0)
    conv_block(c)

    def slope_tile(at, target, keep=None):
        output = dec.total(at) + stem_ref[:, at, :].astype(F32)
        value = (output - target) * scale
        if keep is None:
            own_at = pl.ds(pl.multiple_of(at.start - TILE, TILE), TILE)
            pred_ref[:, own_at, :] = output.astype(BF16)
        else:
            value = jnp.where(keep[None], value, 0.0)
        slope[:, at, :] = value

    def slope_rows(at):
        own_at = pl.ds(pl.multiple_of(at.start - TILE, TILE), TILE)
        slope_tile(at, target_ref[:, own_at, :].astype(F32))

    def pair_slopes(first, count):
        for start in range(first, first + count, TILE):
            even = slope[0, start : start + TILE, :]
            odd = slope[1, start : start + TILE, :]
            following = slope[0, start + 1 : start + 1 + TILE, :]
            chan[c, 0, start : start + TILE, :] = (even + odd).astype(BF16)
            chan[c, 1, start : start + TILE, :] = (odd + following).astype(BF16)

    cut = dec_chunks[1][0] - TILE
    row_chunks = ((0, cut), (cut, rows - cut))

    def row_copy(kind, q, owner, to):
        spot = chan.at[owner, :, span(*row_chunks[q])]
        index = kind * len(row_chunks) + q
        return send(spot, spot, row_send.at[index], row_recv.at[index], s, to)

    for copy in edges:
        copy.wait()
    dec.arrive(0)
    high, low = edge[1].astype(F32), edge[0].astype(F32)
    slope_tile(pl.ds(0, TILE), jnp.where(row[None] < SIDE, high, low), inside)
    slope[:, rows:, :] = slope[:, 0:SIDE, :]
    tiles(TILE, dec_chunks[0][1] - TILE, slope_rows)
    pair_slopes(*row_chunks[0])
    row_copy(1, 0, c, across).start()
    row_copy(0, 0, c, mate).start()
    dec.arrive(1)
    tiles(*dec_chunks[1], slope_rows)
    pair_slopes(*row_chunks[1])
    row_copy(1, 1, c, across).start()
    row_copy(0, 1, c, mate).start()
    slopes.start(c)

    def up_block(j, first):
        at = pl.ds(pl.multiple_of(j * c1, TILE), c1)
        for place, terms in enumerate((((0, 0),), ((1, 1), (0, 2)), ((1, 3), (0, 4)))):
            total = None
            for plane, k in terms:
                term = jnp.dot(chan[j, plane], w_ref[k, at, :], preferred_element_type=F32)
                total = term if total is None else total + term
            if not first:
                total = total + up[place, SIDE : SIDE + rows, :]
            up[place, SIDE : SIDE + rows, :] = total

    up_block(c, True)
    relay.arrive(1)
    for q in range(2):
        row_copy(0, q, mate, mate).wait_recv()
    slopes.start(mate)
    for q in range(2):
        row_copy(1, q, across, across).wait_recv()
        row_copy(2, q, across, mate).start()
    slopes.start(across)
    up_block(mate, False)
    up_block(across, False)
    for q in range(2):
        row_copy(2, q, far, mate).wait_recv()
    slopes.start(far)
    slopes.keep().start()
    up_block(far, False)
    up[0, SIDE + rows :, :] = up[0, SIDE : 2 * SIDE, :]
    for q in range(n):
        for first in range(q * turn.piece, (q + 1) * turn.piece, TILE):
            spot = first + TILE + SIDE
            grad = (
                up[0, spot + 1 : spot + 1 + TILE, :]
                + up[1, spot : spot + TILE, :]
                + up[2, spot - 1 : spot - 1 + TILE, :]
            )
            pre_own[:, first : first + TILE, :] = (
                grad[None] * bend[:, first + TILE : first + 2 * TILE, :]
            ).astype(BF16)
        turn.start(q)
    pl.when(s == c)(lambda: turn.keep().start())

    g_enc_ref[...] = jnp.zeros_like(g_enc_ref)
    g_dec_ref[...] = jnp.zeros_like(g_dec_ref)
    relay.arrive(2)
    turn.forward(0)
    relay.arrive(3)
    for d in range(1, n):
        turn.forward(d)
    slopes.forward()
    for d in range(n):
        turn.relay(d)
    slopes.finish()

    @pl.loop(0, n)
    def _(slot):
        for plane in range(2):
            value = ab_seq[slot, plane].astype(F32)
            ab_wide[plane, 0:rows, :] = value
            ab_wide[plane, rows:, :] = value[0:SIDE]
        terms = (
            ab_wide[0, TILE + 1 : rows + 1, :].astype(BF16),
            ab_seq[slot, 1, TILE:, :],
            ab_seq[slot, 0, TILE:, :],
            ab_wide[1, TILE - 1 : rows - 1, :].astype(BF16),
            ab_wide[0, TILE - 1 : rows - 1, :].astype(BF16),
        )
        for k in range(KW):
            g_dec_ref[k, :, :] += across_rows(terms[k], pools[slot])

    @pl.loop(0, n)
    def _(d):
        slot = lax.rem(s + d, n)
        turn.finish(slot)
        at = pl.ds(pl.multiple_of(slot * own, TILE), own)
        for k in range(KW):
            g_enc_ref[k, :, :] += across_rows(stems[k, at, :], pre_seq[slot, 0]) + across_rows(
                stems[k + 1, at, :], pre_seq[slot, 1]
            )

    enc.end()
    dec.end()
    for q in range(2):
        row_copy(0, q, c, mate).wait_send()
        row_copy(1, q, c, across).wait_send()
        row_copy(2, q, across, mate).wait_send()
    relay.end()
    slopes.end()
    turn.end()


def call(kernel, ident, outs, scratch, *operands):
    vmem = pl.BlockSpec(memory_space=pltpu.VMEM)
    return pl.pallas_call(
        kernel,
        out_shape=outs,
        in_specs=[vmem] * len(operands),
        out_specs=jax.tree.map(lambda _: vmem, outs),
        scratch_shapes=scratch,
        compiler_params=pltpu.CompilerParams(
            collective_id=ident, has_side_effects=True, vmem_limit_bytes=VMEM_BYTES
        ),
    )(*operands)


def dma(count):
    return pltpu.SemaphoreType.DMA((count,))


def square_shards(dna_bases, w_stem, w_enc, w_dec, targets):
    rows = dna_bases.shape[0]
    n = lax.axis_size("seq")
    half = rows // 2
    length, pairs = rows * n, half * n
    held = half + TILE
    s = lax.axis_index("seq")
    c1, c2 = w_stem.shape[0], w_dec.shape[2]
    struct = jax.ShapeDtypeStruct

    split = np.zeros((rows, rows), np.float32)
    split[np.arange(half), 2 * np.arange(half)] = 1
    split[half + np.arange(half), 2 * np.arange(half) + 1] = 1
    split = jnp.asarray(split, BF16)
    target_pair = jnp.dot(split, targets, preferred_element_type=F32).astype(BF16)

    own_bases = dna_bases.reshape(half, 2).T.reshape(rows // 128, 128)
    bases = call(
        functools.partial(bases_kernel, n), 0, struct((n, rows // 128, 128), jnp.int32),
        [pltpu.SemaphoreType.DMA, dma(n - 1), dma(n - 1)], own_bases,
    )
    bases = bases.reshape(n, 2, half).transpose(1, 0, 2).reshape(2, pairs)
    bases = jnp.pad(bases, ((0, 0), (1, 1)), constant_values=-1)
    near = jnp.stack([bases[i % 2, i // 2 : i // 2 + pairs] for i in range(6)])
    onehot = (near[:, None, :] == jnp.arange(4, dtype=jnp.int32)[None, :, None]).astype(BF16)
    weight = w_stem.reshape(c1, KW * 4)
    stem_pair = [
        gelu_value(
            lax.dot_general(
                onehot[i : i + KW].reshape(KW * 4, pairs), weight, (((0,), (1,)), ((), ())),
                preferred_element_type=F32,
            )
        ).astype(BF16)
        for i in range(2)
    ]
    padded = [jnp.pad(value, ((TILE, TILE), (0, 0))) for value in stem_pair]
    stem_all = jnp.stack([value[TILE - SIDE : TILE + pairs + SIDE] for value in padded])

    def local(i):
        first = s * half + TILE - SIDE - 1 + i // 2
        value = lax.dynamic_slice_in_dim(padded[i % 2], first, held, 0)
        return jnp.concatenate([value[half + SIDE :], value[: half + SIDE]], axis=0)

    near_stem = [local(i) for i in range(6)]
    windows = jnp.stack(
        [jnp.concatenate([near_stem[k], near_stem[k + 1]], axis=0) for k in range(KW)]
    )
    part = lax.dot_general(
        windows, w_enc, (((0, 2), (1, 2)), ((), ())), preferred_element_type=F32
    ).astype(BF16)

    tile_count = held // TILE
    step = tile_count // 4 * TILE
    first = held - 3 * step
    enc_chunks = ((0, first), (first, step), (first + step, step), (first + 2 * step, step))
    middle = half // 2 + TILE
    dec_chunks = ((0, middle), (middle, held - middle))
    wide = held + SIDE
    pred, g_enc, g_dec = call(
        functools.partial(train_kernel, n, 1.0 / math.sqrt(length), enc_chunks, dec_chunks), 1,
        (
            struct((2, half, c1), BF16),
            struct((KW, c1, c2), F32),
            struct((KW, c1, c2), F32),
        ),
        [
            pltpu.VMEM((3, 2, held, c2), BF16),
            pltpu.VMEM((2, held, c2), BF16),
            pltpu.VMEM((2, held, c2), F32),
            pltpu.VMEM((held + 2 * SIDE, c2), F32),
            pltpu.VMEM((held, 3 * c2), BF16),
            pltpu.VMEM((n, 2, held, c1), BF16),
            pltpu.VMEM((3, 2, held, c1), BF16),
            pltpu.VMEM((2, held, c1), BF16),
            pltpu.VMEM((wide, c1), F32),
            pltpu.VMEM((2, 2, TILE, c1), BF16),
            pltpu.VMEM((2, wide, c1), F32),
            pltpu.VMEM((n, 2, held, c1), BF16),
            pltpu.VMEM((3, held + 2 * SIDE, c2), F32),
            pltpu.VMEM((2, half, c2), BF16),
            pltpu.VMEM((n, 2, half, c2), BF16),
            pltpu.VMEM((n, 2, held, c1), BF16),
            pltpu.VMEM((2, wide, c1), F32),
            pltpu.VMEM((n, half, c2), BF16),
            pltpu.VMEM((6, pairs, c1), BF16),
            dma(12), dma(12), dma(6), dma(6), dma(2), dma(2), dma(6), dma(6),
            dma(n), dma(n), dma(n),
            dma(n), dma(n), dma(3 * n), dma(3 * n), pltpu.SemaphoreType.DMA,
            dma(n), dma(n), dma(n), dma(n), pltpu.SemaphoreType.DMA,
        ],
        part.reshape(2, held, n * c2),
        jnp.stack([near_stem[2], near_stem[3]]),
        target_pair.reshape(2, half, c1),
        w_dec.transpose(1, 0, 2),
        stem_all,
    )
    pred = lax.dot_general(
        split, pred.reshape(rows, c1), (((0,), (0,)), ((), ())), preferred_element_type=F32
    ).astype(BF16)
    return (pred, g_enc.transpose(2, 0, 1), g_dec.transpose(1, 0, 2))


def shards(dna_bases, w_stem, w_enc, w_dec, targets):
    args = (dna_bases, w_stem, w_enc, w_dec, targets)
    rows, c1, c2 = dna_bases.shape[0], w_stem.shape[0], w_dec.shape[2]
    n = lax.axis_size("seq")
    square = n == 4 and lax.axis_size("chan") == 4
    if square and rows % 512 == 0 and c2 % 128 == 0 and c1 % 64 == 0:
        return square_shards(*args)
    return general_shards(*args)


def solution(mesh):
    return jax.shard_map(
        shards,
        mesh=mesh,
        in_specs=(
            P(("groups", "seq")),
            P("chan", None, None),
            P(None, None, "chan"),
            P(None, None, "chan"),
            P(("groups", "seq"), "chan"),
        ),
        out_specs=(
            P(("groups", "seq"), "chan"),
            P(("groups", "seq"), None, "chan"),
            P(("groups", "seq"), None, "chan"),
        ),
        check_vma=False,
    )
```

```python
import functools
import math

import jax
import jax.numpy as jnp
import numpy as np
from jax import lax
from jax.experimental import pallas as pl
from jax.experimental.pallas import tpu as pltpu
from jax.sharding import PartitionSpec as P

KW = 5


SQRT_TWO_PI = 0.7978845608028654
CUBIC = 0.044715


def extended(block, sides, width):
    for axis, dim in sides:
        count = lax.axis_size(axis)
        forward = [(i, i + 1) for i in range(count - 1)]
        backward = [(target, source) for source, target in forward]
        low = lax.ppermute(
            lax.slice_in_dim(block, block.shape[dim] - width, None, axis=dim), axis, forward
        )
        high = lax.ppermute(lax.slice_in_dim(block, 0, width, axis=dim), axis, backward)
        block = jnp.concatenate([low, block, high], axis=dim)
    return block


def gelu_value(value):
    inner = jnp.tanh(SQRT_TWO_PI * (value + CUBIC * value * value * value))
    return 0.5 * value * (1.0 + inner)


def gelu_slope(value):
    inner = jnp.tanh(SQRT_TWO_PI * (value + CUBIC * value * value * value))
    return 0.5 * (1.0 + inner) + 0.5 * value * (1.0 - inner * inner) * SQRT_TWO_PI * (
        1.0 + 3.0 * CUBIC * value * value
    )


def rim_cells(block, margin):
    return extended(block, (("seq", 0),), margin)


def channel_sum(partial_value):
    return lax.psum_scatter(partial_value, "chan", scatter_dimension=1, tiled=True)


def channel_gather(block):
    return lax.all_gather(block, "chan", axis=1, tiled=True)


def conv_rows(padded, weight):
    row_count = padded.shape[0] - 4
    total = jnp.zeros((row_count, weight.shape[0]), jnp.float32)
    for k in range(KW):
        total = total + lax.dot_general(
            padded[k : k + row_count],
            weight[:, k, :],
            (((1,), (1,)), ((), ())),
            preferred_element_type=jnp.float32,
        )
    return total


def grad_taps(picked, padded):
    row_count = picked.shape[0]
    pieces = [
        lax.dot_general(
            picked,
            padded[k : k + row_count],
            (((0,), (0,)), ((), ())),
            preferred_element_type=jnp.float32,
        )
        for k in range(KW)
    ]
    return jnp.stack(pieces, axis=1)


def weight_grad(cotangent, padded):
    rounded = grad_taps(cotangent, padded).astype(jnp.bfloat16)
    return lax.psum_scatter(
        lax.optimization_barrier(rounded).astype(jnp.float32),
        "seq",
        scatter_dimension=0,
        tiled=True,
    )


def general_shards(dna_bases, w_stem, w_enc, w_dec, targets):
    row_count = dna_bases.shape[0]
    devices = lax.axis_size("seq")
    length = row_count * devices
    onehot = (dna_bases[:, None] == jnp.arange(4, dtype=jnp.int32)[None, :]).astype(jnp.bfloat16)
    onehot_pad = rim_cells(onehot, 2)
    stem_out = gelu_value(conv_rows(onehot_pad, w_stem)).astype(jnp.bfloat16)
    stem_pad = rim_cells(stem_out, 2)
    enc_pre = channel_sum(conv_rows(stem_pad, w_enc))
    active = gelu_value(enc_pre).astype(jnp.bfloat16).astype(jnp.float32)
    pooled = (0.5 * active.reshape(row_count // 2, 2, -1).sum(axis=1)).astype(jnp.bfloat16)
    pooled_pad = rim_cells(pooled, 1)
    up_pad = jnp.repeat(pooled_pad, 2, axis=0)
    output = channel_sum(conv_rows(up_pad, w_dec)) + stem_out.astype(jnp.float32)
    pred = output.astype(jnp.bfloat16)
    scale = 1.0 / math.sqrt(length)
    slope_out = ((output - targets.astype(jnp.float32)) * scale).astype(jnp.bfloat16)
    slope_all = channel_gather(slope_out)
    g_dec = weight_grad(slope_all, up_pad)
    slope_pad = rim_cells(slope_all, 2)
    up_grad = jnp.zeros((row_count, w_dec.shape[2]), jnp.float32)
    for k in range(KW):
        up_grad = up_grad + jnp.dot(
            slope_pad[4 - k : 4 - k + row_count], w_dec[:, k, :], preferred_element_type=jnp.float32
        )
    pool_grad = up_grad.reshape(row_count // 2, 2, -1).sum(axis=1)
    act_grad = 0.5 * jnp.repeat(pool_grad, 2, axis=0)
    pre_grad = (act_grad * gelu_slope(enc_pre)).astype(jnp.bfloat16)
    pre_all = channel_gather(pre_grad)
    g_enc = weight_grad(pre_all, stem_pad)
    return (pred, g_enc, g_dec)


MESH_ID = pl.DeviceIdType.MESH
BF16 = jnp.bfloat16
F32 = jnp.float32
TILE = 16
SIDE = 8
HALVES = 2
VMEM_BYTES = 36 * 1024 * 1024


def send(src, dst, send_sem, recv_sem, seq, chan):
    return pltpu.make_async_remote_copy(
        src_ref=src,
        dst_ref=dst,
        send_sem=send_sem,
        recv_sem=recv_sem,
        device_id={"seq": seq, "chan": chan},
        device_id_type=MESH_ID,
    )


def greet(targets):
    barrier = pltpu.get_barrier_semaphore()
    for seq, chan in targets:
        pl.semaphore_signal(
            barrier, inc=1, device_id={"seq": seq, "chan": chan}, device_id_type=MESH_ID
        )
    pl.semaphore_wait(barrier, len(targets))


def whole_group(n, s, c):
    others = []
    for ds in range(n):
        for dc in range(n):
            if ds or dc:
                others.append((lax.rem(s + ds, n), lax.rem(c + dc, n)))
    return others


def bases_kernel(n, own_ref, all_ref, local_sem, send_sem, recv_sem):
    s, c = lax.axis_index("seq"), lax.axis_index("chan")
    peers = [lax.rem(s + d, n) for d in range(1, n)]
    greet([(p, c) for p in peers])
    copies = [
        send(own_ref, all_ref.at[s], send_sem.at[d], recv_sem.at[d], p, c)
        for d, p in enumerate(peers)
    ]
    for copy in copies:
        copy.start()
    mine = pltpu.make_async_copy(own_ref, all_ref.at[s], local_sem)
    mine.start()
    mine.wait()
    for copy in copies:
        copy.wait()


def partners(c):
    mate = c + 1 - 2 * lax.rem(c, 2)
    across = lax.rem(c + 2, 4)
    return mate, across, lax.rem(mate + 2, 4)


def span(first, count):
    return pl.ds(first, count)


def tiles(first, count, body):
    @pl.loop(0, count // TILE)
    def _(i):
        body(pl.ds(pl.multiple_of(first + i * TILE, TILE), TILE))


class Part:
    def __init__(self, sem, base):
        self.sem, self.base = sem, base

    @property
    def at(self):
        return self

    def __getitem__(self, index):
        return self.sem.at[self.base + index]


class Turn:
    def __init__(self, n, s, c, h, own, mid, out, sems):
        self.n, self.s, self.c, self.h, self.own, self.mid, self.out = n, s, c, h, own, mid, out
        (self.cross_send, self.cross_recv, self.along_send, self.along_recv,
         self.share_send, self.share_recv, self.local) = sems
        self.count = own.shape[1]
        self.piece = self.count // n
        self.side = c // 2

    def out_rows(self, index):
        first = self.h * self.count + index * self.piece
        return pl.ds(pl.multiple_of(first, self.piece), self.piece)

    def cross(self):
        wide = 2 * self.piece
        at = pl.ds(pl.multiple_of((1 - self.side) * wide, wide), wide)
        return send(self.own.at[:, at], self.mid, self.cross_send.at[0], self.cross_recv.at[0],
                    self.s, partners(self.c)[1])

    def source(self, plane, q):
        if plane:
            first = (q - 2 * self.side) * self.piece
            return self.mid.at[:, pl.ds(pl.multiple_of(first, self.piece), self.piece)]
        return self.own.at[:, pl.ds(pl.multiple_of(q * self.piece, self.piece), self.piece)]

    def along(self, plane, kind, slot):
        mate, across, _ = partners(self.c)
        q = mate if kind else self.c
        return send(self.source(plane, q), self.out.at[self.s, :, self.out_rows(q)],
                    self.along_send.at[2 * plane + kind], self.along_recv.at[slot],
                    across if plane else self.c, q)

    def keep(self, plane):
        return pltpu.make_async_copy(
            self.source(plane, self.c), self.out.at[self.s, :, self.out_rows(self.c)], self.local
        )

    def home(self, plane):
        return self.s == (partners(self.c)[1] if plane else self.c)

    def start(self, plane):
        home = self.home(plane)
        pl.when(jnp.logical_not(home))(lambda: self.along(plane, 0, self.s).start())
        pl.when(home)(lambda: self.keep(plane).start())
        self.along(plane, 1, self.s).start()

    def share(self, slot, kind, part, to):
        spot = self.out.at[slot, :, self.out_rows(part)]
        index = slot * 3 + kind
        return send(spot, spot, self.share_send.at[index], self.share_recv.at[index], self.s, to)

    def forward(self, slot, mine):
        mate, across, _ = partners(self.c)
        if mine:
            pl.when(self.home(0))(lambda: self.keep(0).wait())
            pl.when(self.home(1))(lambda: self.keep(1).wait())
            other = jnp.logical_not(jnp.logical_or(self.home(0), self.home(1)))
            pl.when(other)(lambda: self.along(0, 0, slot).wait_recv())
        else:
            self.along(0, 0, slot).wait_recv()
        self.share(slot, 1, self.c, across).start()
        self.share(slot, 0, self.c, mate).start()

    def relay(self, slot):
        mate, across, _ = partners(self.c)
        self.share(slot, 1, across, across).wait_recv()
        self.share(slot, 2, across, mate).start()

    def finish(self, slot):
        mate, across, far = partners(self.c)
        self.share(slot, 0, mate, mate).wait_recv()
        self.share(slot, 2, far, mate).wait_recv()

    def end(self):
        mate, across, _ = partners(self.c)
        for slot in range(self.n):
            self.share(slot, 0, self.c, mate).wait_send()
            self.share(slot, 1, self.c, across).wait_send()
            self.share(slot, 2, across, mate).wait_send()
        self.cross().wait_send()
        for plane in range(2):
            pl.when(jnp.logical_not(self.home(plane)))(
                functools.partial(lambda plane: self.along(plane, 0, self.s).wait_send(), plane)
            )
            self.along(plane, 1, self.s).wait_send()


class PairSum:
    def __init__(self, block, held, pair, s, c, chunks, sems):
        self.block, self.held, self.pair, self.s, self.c = block, held, pair, s, c
        self.chunks = chunks
        self.send_sem, self.recv_sem = sems

    def hop(self, kind, q):
        mate, across, far = partners(self.c)
        source = (lambda: self.block(mate), lambda: self.block(far), lambda: self.pair)[kind]()
        target = (mate, mate, across)[kind]
        at = span(*self.chunks[q])
        index = kind * len(self.chunks) + q
        return send(source.at[:, at], self.held.at[kind, :, at], self.send_sem.at[index],
                    self.recv_sem.at[index], self.s, target)

    def start(self, kind):
        for q in range(len(self.chunks)):
            self.hop(kind, q).start()

    def cross(self, q):
        _, across, _ = partners(self.c)
        self.hop(1, q).wait_recv()
        block = self.block(across)

        def body(at):
            self.pair[:, at, :] = (
                block[:, at, :].astype(F32) + self.held[1, :, at, :].astype(F32)
            ).astype(BF16)

        tiles(*self.chunks[q], body)
        self.hop(2, q).start()

    def arrive(self, q):
        self.hop(0, q).wait_recv()
        self.hop(2, q).wait_recv()

    def total(self, at):
        mine = self.block(self.c)[:, at, :].astype(F32)
        return mine + self.held[0, :, at, :].astype(F32) + self.held[2, :, at, :].astype(F32)

    def end(self):
        for kind in range(3):
            for q in range(len(self.chunks)):
                self.hop(kind, q).wait_send()


class PoolRelay:
    def __init__(self, n, s, c, h, out, right_send, left_send, recv):
        self.n, self.s, self.c, self.out = n, s, c, out
        self.right_send, self.left_send, self.recv = right_send, left_send, recv
        self.at = span(h * (out.shape[1] // HALVES), out.shape[1] // HALVES)

    def hop(self, slot, step):
        sems = self.right_send if step > 0 else self.left_send
        spot = self.out.at[slot, self.at]
        return send(spot, spot, sems.at[slot], self.recv.at[slot], self.s + step, self.c)

    def start(self):
        pl.when(self.s < self.n - 1)(lambda: self.hop(self.s, 1).start())
        pl.when(self.s > 0)(lambda: self.hop(self.s, -1).start())

    def arrive(self, d):
        low, high = self.s - d, self.s + d

        @pl.when(low >= 0)
        def _():
            self.hop(low, 1).wait_recv()
            pl.when(self.s < self.n - 1)(lambda: self.hop(low, 1).start())

        @pl.when(high < self.n)
        def _():
            self.hop(high, -1).wait_recv()
            pl.when(self.s > 0)(lambda: self.hop(high, -1).start())

    def end(self):
        for slot in range(self.n):
            pl.when(jnp.logical_and(slot <= self.s, self.s < self.n - 1))(
                functools.partial(lambda slot: self.hop(slot, 1).wait_send(), slot)
            )
            pl.when(jnp.logical_and(slot >= self.s, self.s > 0))(
                functools.partial(lambda slot: self.hop(slot, -1).wait_send(), slot)
            )


class SlopeTurn:
    def __init__(self, n, s, c, chan, out, sems):
        self.n, self.s, self.c, self.chan, self.out = n, s, c, chan, out
        self.send_sem, self.recv_sem, self.share_send, self.share_recv, self.local = sems
        self.plane = lax.rem(c, 2)

    def hop(self, to, slot):
        return send(self.chan.at[to, self.plane], self.out.at[self.s, self.plane],
                    self.send_sem.at[to], self.recv_sem.at[slot], to, self.c)

    def start(self, block):
        pl.when(block != self.s)(lambda: self.hop(block, self.s).start())

    def keep(self):
        return pltpu.make_async_copy(self.chan.at[self.s], self.out.at[self.s], self.local)

    def share(self, slot, plane):
        mate, _, _ = partners(self.c)
        spot = self.out.at[slot, plane]
        return send(spot, spot, self.share_send.at[slot], self.share_recv.at[slot], self.s, mate)

    def forward(self, slot):
        self.hop(self.s, slot).wait_recv()
        self.share(slot, self.plane).start()

    def finish(self, slot):
        self.share(slot, 1 - self.plane).wait_recv()

    def end(self, others):
        for slot in others:
            self.share(slot, self.plane).wait_send()
            self.hop(slot, self.s).wait_send()


def across_rows(left, right):
    return lax.dot_general(left, right, (((0,), (0,)), ((), ())), preferred_element_type=F32)


def by_channels(left, right):
    return lax.dot_general(left, right, (((1,), (1,)), ((), ())), preferred_element_type=F32)


def train_kernel(
    n, scale, enc_chunks, part_ref, stem_ref, target_ref, w_ref, stem_all_ref,
    pred_ref, g_enc_ref, g_dec_ref,
    enc_held, enc_pair, bend, pool_wide, pool_near, dec_part, dec_held, dec_pair, q_wide,
    edge, slope, chan, up, pre_own, pre_mid, pre_seq, ab_seq, ab_wide, ab_near, pools, stems,
    enc_send, enc_recv, dec_send, dec_recv, edge_send, edge_recv, row_send, row_recv,
    right_send, left_send, pool_recv, *turn_sems,
):
    s, c = lax.axis_index("seq"), lax.axis_index("chan")
    mate, across, far = partners(c)
    rows, c2 = pool_near.shape[0], pool_wide.shape[1]
    own = rows - TILE
    pairs = HALVES * own
    c1 = stem_ref.shape[3]
    upper = s // 2
    slots = (s, 1 - s + 4 * upper, 2 - upper, 3 - 3 * upper)
    both_halves = range(HALVES)
    greet(whole_group(n, s, c))

    def column_block(h, j):
        return part_ref.at[h, :, :, pl.ds(pl.multiple_of(j * c2, 128), c2)]

    counts = 3 * len(enc_chunks)
    enc = [
        PairSum(functools.partial(column_block, h), enc_held.at[h], enc_pair.at[h], s, c,
                enc_chunks, (Part(enc_send, h * counts), Part(enc_recv, h * counts)))
        for h in both_halves
    ]
    dec = [
        PairSum(functools.partial(lambda h, j: dec_part.at[h, j], h), dec_held.at[h],
                dec_pair.at[h], s, c, ((0, rows),), (Part(dec_send, h * 3), Part(dec_recv, h * 3)))
        for h in both_halves
    ]
    relay = [
        PoolRelay(n, s, c, h, pools, *[Part(sem, h * n) for sem in (right_send, left_send, pool_recv)])
        for h in both_halves
    ]
    turn = [
        Turn(n, s, c, h, pre_own.at[h], pre_mid.at[h], pre_seq,
             [Part(sem, h * size) for sem, size in zip(turn_sems[:6], (1, 1, n, n, 3 * n, 3 * n))]
             + [turn_sems[6].at[h]])
        for h in both_halves
    ]
    slopes = [
        SlopeTurn(n, s, c, chan.at[h], ab_seq.at[h],
                  [Part(sem, h * n) for sem in turn_sems[7:11]] + [turn_sems[11].at[h]])
        for h in both_halves
    ]

    for h in both_halves:
        enc[h].start(1)
        enc[h].start(0)
    edges = [
        send(target_ref.at[:, pl.ds(pairs - TILE, TILE)], edge.at[0], edge_send.at[0],
             edge_recv.at[0], lax.rem(s + 1, n), c),
        send(target_ref.at[:, pl.ds(0, TILE)], edge.at[1], edge_send.at[1], edge_recv.at[1],
             lax.rem(s + n - 1, n), c),
    ]
    for h in both_halves:
        for q in range(len(enc_chunks)):
            enc[h].cross(q)
    for copy in edges:
        copy.start()

    row = lax.broadcasted_iota(jnp.int32, (TILE, 1), 0)
    inside = (
        jnp.logical_or(row < SIDE, s > 0),
        jnp.logical_or(row >= SIDE, s < n - 1),
    )

    @pl.loop(0, n * pairs // 64)
    def _(i):
        at = pl.ds(pl.multiple_of(i * 64, 64), 64)
        for parity in range(2):
            wide = stem_all_ref[parity, pl.ds(pl.multiple_of(i * 64, TILE), 64 + TILE), :].astype(F32)
            for shift in range(3):
                first = SIDE - 1 + shift
                stems[2 * shift + parity, at, :] = wide[first : first + 64].astype(BF16)

    def enc_rows(h, at):
        total = enc[h].total(at)
        square = total * total
        inner = jnp.tanh(SQRT_TWO_PI * (total + CUBIC * square * total))
        active = (0.5 * total * (1.0 + inner)).astype(BF16).astype(F32)
        pooled = (0.5 * (active[0] + active[1])).astype(BF16).astype(F32)
        pool_wide[pl.ds(pl.multiple_of(at.start + SIDE, SIDE), TILE), :] = pooled
        bend[h, :, at, :] = 0.5 * (
            0.5 * (1.0 + inner)
            + 0.5 * total * (1.0 - inner * inner) * SQRT_TWO_PI * (1.0 + 3.0 * CUBIC * square)
        )

    def conv_block(h, j):
        at = pl.ds(pl.multiple_of(j * c1, TILE), c1)
        before, here, after = (pool_near[:, i * c2 : (i + 1) * c2] for i in range(3))
        shared = by_channels(before, w_ref[0, at, :]) + by_channels(here, w_ref[2, at, :])
        shared = shared + by_channels(after, w_ref[4, at, :])
        single = by_channels(before, w_ref[1, at, :]) + by_channels(here, w_ref[3, at, :])
        q_wide[0:rows, :] = single
        q_wide[rows:, :] = single[0:SIDE]
        dec_part[h, j, 0, :, :] = (shared + single).astype(BF16)
        dec_part[h, j, 1, :, :] = (shared + q_wide[1 : rows + 1, :]).astype(BF16)

    def encode(h):
        for q in range(len(enc_chunks)):
            enc[h].arrive(q)
            tiles(*enc_chunks[q], functools.partial(enc_rows, h))
        halo = pool_wide[SIDE : SIDE + TILE, :]
        pool_wide[SIDE : SIDE + TILE, :] = jnp.where(inside[h], halo, 0.0)
        pool_wide[0:SIDE, :] = pool_wide[rows : rows + SIDE, :]
        pool_wide[rows + SIDE :, :] = pool_wide[SIDE : 2 * SIDE, :]
        for first in range(0, rows, TILE):
            for shift in range(3):
                value = pool_wide[first + SIDE - 1 + shift : first + SIDE - 1 + shift + TILE, :]
                pool_near[first : first + TILE, shift * c2 : (shift + 1) * c2] = value.astype(BF16)
        conv_block(h, far)
        dec[h].start(1)
        pools[s, h * own : (h + 1) * own, :] = pool_near[TILE:, c2 : 2 * c2]
        relay[h].start()
        conv_block(h, across)
        dec[h].cross(0)
        conv_block(h, mate)
        dec[h].start(0)
        conv_block(h, c)

    def slope_tile(h, at, target, keep=None):
        output = dec[h].total(at) + stem_ref[h, :, at, :].astype(F32)
        value = (output - target) * scale
        if keep is None:
            own_at = pl.ds(pl.multiple_of(at.start - TILE + h * own, TILE), TILE)
            pred_ref[:, own_at, :] = output.astype(BF16)
        else:
            value = jnp.where(keep[None], value, 0.0)
        slope[:, at, :] = value

    def slope_rows(h, at):
        own_at = pl.ds(pl.multiple_of(at.start - TILE + h * own, TILE), TILE)
        slope_tile(h, at, target_ref[:, own_at, :].astype(F32))

    def row_copy(h, kind, owner, to):
        spot = chan.at[h, owner]
        return send(spot, spot, row_send.at[h * 3 + kind], row_recv.at[h * 3 + kind], s, to)

    def decode(h):
        dec[h].arrive(0)
        high = target_ref[:, own : own + TILE, :] if h == 0 else edge[1]
        low = edge[0] if h == 0 else target_ref[:, own - TILE : own, :]
        target = jnp.where(row[None] < SIDE, high.astype(F32), low.astype(F32))
        slope_tile(h, pl.ds(0, TILE), target, inside[h])
        slope[:, rows:, :] = slope[:, 0:SIDE, :]
        tiles(TILE, own, functools.partial(slope_rows, h))
        for start in range(0, rows, TILE):
            even = slope[0, start : start + TILE, :]
            odd = slope[1, start : start + TILE, :]
            following = slope[0, start + 1 : start + 1 + TILE, :]
            chan[h, c, 0, start : start + TILE, :] = (even + odd).astype(BF16)
            chan[h, c, 1, start : start + TILE, :] = (odd + following).astype(BF16)
        row_copy(h, 1, c, across).start()
        row_copy(h, 0, c, mate).start()

    def up_block(h, j, first):
        at = pl.ds(pl.multiple_of(j * c1, TILE), c1)
        for place, terms in enumerate((((0, 0),), ((1, 1), (0, 2)), ((1, 3), (0, 4)))):
            total = None
            for plane, k in terms:
                term = jnp.dot(chan[h, j, plane], w_ref[k, at, :], preferred_element_type=F32)
                total = term if total is None else total + term
            if not first:
                total = total + up[place, SIDE : SIDE + rows, :]
            up[place, SIDE : SIDE + rows, :] = total

    def bend_back(h):
        up[0, SIDE + rows :, :] = up[0, SIDE : 2 * SIDE, :]
        for first in range(0, own, TILE):
            spot = first + TILE + SIDE
            grad = (
                up[0, spot + 1 : spot + 1 + TILE, :]
                + up[1, spot : spot + TILE, :]
                + up[2, spot - 1 : spot - 1 + TILE, :]
            )
            pre_own[h, :, first : first + TILE, :] = (
                grad[None] * bend[h, :, first + TILE : first + 2 * TILE, :]
            ).astype(BF16)
        turn[h].cross().start()
        turn[h].start(0)

    def back(h):
        up_block(h, c, True)
        row_copy(h, 0, mate, mate).wait_recv()
        up_block(h, mate, False)
        row_copy(h, 1, across, across).wait_recv()
        row_copy(h, 2, across, mate).start()
        up_block(h, across, False)
        row_copy(h, 2, far, mate).wait_recv()
        up_block(h, far, False)
        bend_back(h)

    def pass_on(h):
        turn[h].cross().wait_recv()
        turn[h].start(1)

    def turn_slopes(h):
        for block in (c, mate, across, far):
            slopes[h].start(block)
        slopes[h].keep().start()

    def decoder_grad(slot):
        for h in both_halves:
            for plane in range(2):
                value = ab_seq[h, slot, plane].astype(F32)
                ab_wide[plane, 0:rows, :] = value
                ab_wide[plane, rows:, :] = value[0:SIDE]
            for k, (plane, shift) in enumerate(((0, 1), (1, 0), (0, 0), (1, -1), (0, -1))):
                ab_near[k, h * own : (h + 1) * own, :] = ab_wide[
                    plane, TILE + shift : rows + shift, :
                ].astype(BF16)
        for k in range(KW):
            g_dec_ref[k, :, :] += across_rows(ab_near[k], pools[slot])

    def encoder_grad(slot):
        at = pl.ds(pl.multiple_of(slot * pairs, TILE), pairs)
        for k in range(KW):
            g_enc_ref[k, :, :] += across_rows(stems[k, at, :], pre_seq[slot, 0]) + across_rows(
                stems[k + 1, at, :], pre_seq[slot, 1]
            )

    encode(0)
    encode(1)
    for copy in edges:
        copy.wait()
    decode(0)
    relay[0].arrive(1)
    decode(1)
    relay[1].arrive(1)
    back(0)
    turn_slopes(0)
    relay[0].arrive(2)
    up_block(1, c, True)
    row_copy(1, 0, mate, mate).wait_recv()
    up_block(1, mate, False)
    row_copy(1, 1, across, across).wait_recv()
    row_copy(1, 2, across, mate).start()
    up_block(1, across, False)
    pass_on(0)
    row_copy(1, 2, far, mate).wait_recv()
    up_block(1, far, False)
    bend_back(1)
    g_enc_ref[...] = jnp.zeros_like(g_enc_ref)
    g_dec_ref[...] = jnp.zeros_like(g_dec_ref)
    relay[1].arrive(2)
    pass_on(1)
    turn_slopes(1)
    for i in range(n):
        turn[0].forward(slots[i], i == 0)
    relay[0].arrive(3)
    for i in range(n):
        turn[1].forward(slots[i], i == 0)
        turn[0].relay(slots[i])
    relay[1].arrive(3)
    for slot in slots[1:]:
        slopes[0].forward(slot)
    for i in range(n):
        turn[1].relay(slots[i])
        if i:
            slopes[1].forward(slots[i])
            for h in both_halves:
                turn[h].finish(slots[i - 1])
            encoder_grad(slots[i - 1])
    for h in both_halves:
        slopes[h].keep().wait()
        for slot in slots[1:]:
            slopes[h].finish(slot)

    @pl.loop(0, n)
    def _(slot):
        decoder_grad(slot)

    for h in both_halves:
        turn[h].finish(slots[n - 1])
    encoder_grad(slots[n - 1])

    for h in both_halves:
        enc[h].end()
        dec[h].end()
        row_copy(h, 0, c, mate).wait_send()
        row_copy(h, 1, c, across).wait_send()
        row_copy(h, 2, across, mate).wait_send()
        relay[h].end()
        slopes[h].end(slots[1:])
        turn[h].end()


def call(kernel, ident, outs, scratch, *operands):
    vmem = pl.BlockSpec(memory_space=pltpu.VMEM)
    return pl.pallas_call(
        kernel,
        out_shape=outs,
        in_specs=[vmem] * len(operands),
        out_specs=jax.tree.map(lambda _: vmem, outs),
        scratch_shapes=scratch,
        compiler_params=pltpu.CompilerParams(
            collective_id=ident, has_side_effects=True, vmem_limit_bytes=VMEM_BYTES
        ),
    )(*operands)


def dma(count):
    return pltpu.SemaphoreType.DMA((count,))


def square_shards(dna_bases, w_stem, w_enc, w_dec, targets):
    rows = dna_bases.shape[0]
    n = lax.axis_size("seq")
    half = rows // 2
    length, pairs = rows * n, half * n
    own = half // HALVES
    held = own + TILE
    s = lax.axis_index("seq")
    c1, c2 = w_stem.shape[0], w_dec.shape[2]
    struct = jax.ShapeDtypeStruct

    split = np.zeros((rows, rows), np.float32)
    split[np.arange(half), 2 * np.arange(half)] = 1
    split[half + np.arange(half), 2 * np.arange(half) + 1] = 1
    split = jnp.asarray(split, BF16)
    target_pair = jnp.dot(split, targets, preferred_element_type=F32).astype(BF16)

    own_bases = dna_bases.reshape(half, 2).T.reshape(rows // 128, 128)
    bases = call(
        functools.partial(bases_kernel, n), 0, struct((n, rows // 128, 128), jnp.int32),
        [pltpu.SemaphoreType.DMA, dma(n - 1), dma(n - 1)], own_bases,
    )
    bases = bases.reshape(n, 2, half).transpose(1, 0, 2).reshape(2, pairs)
    bases = jnp.pad(bases, ((0, 0), (1, 1)), constant_values=-1)
    near = jnp.stack([bases[i % 2, i // 2 : i // 2 + pairs] for i in range(6)])
    onehot = (near[:, None, :] == jnp.arange(4, dtype=jnp.int32)[None, :, None]).astype(BF16)
    weight = w_stem.reshape(c1, KW * 4)
    stem_pair = [
        gelu_value(
            lax.dot_general(
                onehot[i : i + KW].reshape(KW * 4, pairs), weight, (((0,), (1,)), ((), ())),
                preferred_element_type=F32,
            )
        ).astype(BF16)
        for i in range(2)
    ]
    padded = [jnp.pad(value, ((TILE, TILE), (0, 0))) for value in stem_pair]
    stem_all = jnp.stack([value[TILE - SIDE : TILE + pairs + SIDE] for value in padded])

    def local(h, i):
        first = s * half + h * own + TILE - SIDE - 1 + i // 2
        value = lax.dynamic_slice_in_dim(padded[i % 2], first, held, 0)
        return jnp.concatenate([value[own + SIDE :], value[: own + SIDE]], axis=0)

    near_stem = [[local(h, i) for i in range(6)] for h in range(HALVES)]
    windows = jnp.stack(
        [
            jnp.concatenate([near_stem[h][k + parity] for h in range(HALVES) for parity in range(2)])
            for k in range(KW)
        ]
    )
    part = lax.dot_general(
        windows, w_enc, (((0, 2), (1, 2)), ((), ())), preferred_element_type=F32
    ).astype(BF16)

    cut = held // TILE // 2 * TILE
    enc_chunks = ((0, cut), (cut, held - cut))
    wide = held + SIDE
    double = HALVES * n
    counts = HALVES * 3 * len(enc_chunks)
    pred, g_enc, g_dec = call(
        functools.partial(train_kernel, n, 1.0 / math.sqrt(length), enc_chunks), 1,
        (
            struct((2, half, c1), BF16),
            struct((KW, c1, c2), F32),
            struct((KW, c1, c2), F32),
        ),
        [
            pltpu.VMEM((HALVES, 3, 2, held, c2), BF16),
            pltpu.VMEM((HALVES, 2, held, c2), BF16),
            pltpu.VMEM((HALVES, 2, held, c2), F32),
            pltpu.VMEM((held + 2 * SIDE, c2), F32),
            pltpu.VMEM((held, 3 * c2), BF16),
            pltpu.VMEM((HALVES, n, 2, held, c1), BF16),
            pltpu.VMEM((HALVES, 3, 2, held, c1), BF16),
            pltpu.VMEM((HALVES, 2, held, c1), BF16),
            pltpu.VMEM((wide, c1), F32),
            pltpu.VMEM((2, 2, TILE, c1), BF16),
            pltpu.VMEM((2, wide, c1), F32),
            pltpu.VMEM((HALVES, n, 2, held, c1), BF16),
            pltpu.VMEM((3, held + 2 * SIDE, c2), F32),
            pltpu.VMEM((HALVES, 2, own, c2), BF16),
            pltpu.VMEM((HALVES, 2, own // 2, c2), BF16),
            pltpu.VMEM((n, 2, half, c2), BF16),
            pltpu.VMEM((HALVES, n, 2, held, c1), BF16),
            pltpu.VMEM((2, wide, c1), F32),
            pltpu.VMEM((KW, half, c1), BF16),
            pltpu.VMEM((n, half, c2), BF16),
            pltpu.VMEM((6, pairs, c1), BF16),
            dma(counts), dma(counts), dma(HALVES * 3), dma(HALVES * 3), dma(2), dma(2),
            dma(HALVES * 3), dma(HALVES * 3), dma(double), dma(double), dma(double),
            dma(HALVES), dma(HALVES), dma(double), dma(double), dma(3 * double), dma(3 * double),
            dma(HALVES),
            dma(double), dma(double), dma(double), dma(double), dma(HALVES),
        ],
        part.reshape(HALVES, 2, held, n * c2),
        jnp.stack([jnp.stack(near_stem[h][2:4]) for h in range(HALVES)]),
        target_pair.reshape(2, half, c1),
        w_dec.transpose(1, 0, 2),
        stem_all,
    )
    pred = lax.dot_general(
        split, pred.reshape(rows, c1), (((0,), (0,)), ((), ())), preferred_element_type=F32
    ).astype(BF16)
    return (pred, g_enc.transpose(2, 0, 1), g_dec.transpose(1, 0, 2))


def shards(dna_bases, w_stem, w_enc, w_dec, targets):
    args = (dna_bases, w_stem, w_enc, w_dec, targets)
    rows, c1, c2 = dna_bases.shape[0], w_stem.shape[0], w_dec.shape[2]
    n = lax.axis_size("seq")
    square = n == 4 and lax.axis_size("chan") == 4
    if square and rows % 512 == 0 and c2 % 128 == 0 and c1 % 64 == 0:
        return square_shards(*args)
    return general_shards(*args)


def solution(mesh):
    return jax.shard_map(
        shards,
        mesh=mesh,
        in_specs=(
            P(("groups", "seq")),
            P("chan", None, None),
            P(None, None, "chan"),
            P(None, None, "chan"),
            P(("groups", "seq"), "chan"),
        ),
        out_specs=(
            P(("groups", "seq"), "chan"),
            P(("groups", "seq"), None, "chan"),
            P(("groups", "seq"), None, "chan"),
        ),
        check_vma=False,
    )
```

```python
import functools
import math

import jax
import jax.numpy as jnp
from jax import lax
from jax.experimental import pallas as pl
from jax.experimental.pallas import tpu as pltpu
from jax.sharding import PartitionSpec as P

KW = 5


SQRT_TWO_PI = 0.7978845608028654
CUBIC = 0.044715


def extended(block, sides, width):
    for axis, dim in sides:
        count = lax.axis_size(axis)
        forward = [(i, i + 1) for i in range(count - 1)]
        backward = [(target, source) for source, target in forward]
        low = lax.ppermute(
            lax.slice_in_dim(block, block.shape[dim] - width, None, axis=dim), axis, forward
        )
        high = lax.ppermute(lax.slice_in_dim(block, 0, width, axis=dim), axis, backward)
        block = jnp.concatenate([low, block, high], axis=dim)
    return block


def gelu_value(value):
    inner = jnp.tanh(SQRT_TWO_PI * (value + CUBIC * value * value * value))
    return 0.5 * value * (1.0 + inner)


def gelu_slope(value):
    inner = jnp.tanh(SQRT_TWO_PI * (value + CUBIC * value * value * value))
    return 0.5 * (1.0 + inner) + 0.5 * value * (1.0 - inner * inner) * SQRT_TWO_PI * (
        1.0 + 3.0 * CUBIC * value * value
    )


def rim_cells(block, margin):
    return extended(block, (("seq", 0),), margin)


def channel_sum(partial_value):
    return lax.psum_scatter(partial_value, "chan", scatter_dimension=1, tiled=True)


def channel_gather(block):
    return lax.all_gather(block, "chan", axis=1, tiled=True)


def conv_rows(padded, weight):
    row_count = padded.shape[0] - 4
    total = jnp.zeros((row_count, weight.shape[0]), jnp.float32)
    for k in range(KW):
        total = total + lax.dot_general(
            padded[k : k + row_count],
            weight[:, k, :],
            (((1,), (1,)), ((), ())),
            preferred_element_type=jnp.float32,
        )
    return total


def grad_taps(picked, padded):
    row_count = picked.shape[0]
    pieces = [
        lax.dot_general(
            picked,
            padded[k : k + row_count],
            (((0,), (0,)), ((), ())),
            preferred_element_type=jnp.float32,
        )
        for k in range(KW)
    ]
    return jnp.stack(pieces, axis=1)


def weight_grad(cotangent, padded):
    rounded = grad_taps(cotangent, padded).astype(jnp.bfloat16)
    return lax.psum_scatter(
        lax.optimization_barrier(rounded).astype(jnp.float32),
        "seq",
        scatter_dimension=0,
        tiled=True,
    )


def general_shards(dna_bases, w_stem, w_enc, w_dec, targets):
    row_count = dna_bases.shape[0]
    devices = lax.axis_size("seq")
    length = row_count * devices
    onehot = (dna_bases[:, None] == jnp.arange(4, dtype=jnp.int32)[None, :]).astype(jnp.bfloat16)
    onehot_pad = rim_cells(onehot, 2)
    stem_out = gelu_value(conv_rows(onehot_pad, w_stem)).astype(jnp.bfloat16)
    stem_pad = rim_cells(stem_out, 2)
    enc_pre = channel_sum(conv_rows(stem_pad, w_enc))
    active = gelu_value(enc_pre).astype(jnp.bfloat16).astype(jnp.float32)
    pooled = (0.5 * active.reshape(row_count // 2, 2, -1).sum(axis=1)).astype(jnp.bfloat16)
    pooled_pad = rim_cells(pooled, 1)
    up_pad = jnp.repeat(pooled_pad, 2, axis=0)
    output = channel_sum(conv_rows(up_pad, w_dec)) + stem_out.astype(jnp.float32)
    pred = output.astype(jnp.bfloat16)
    scale = 1.0 / math.sqrt(length)
    slope_out = ((output - targets.astype(jnp.float32)) * scale).astype(jnp.bfloat16)
    slope_all = channel_gather(slope_out)
    g_dec = weight_grad(slope_all, up_pad)
    slope_pad = rim_cells(slope_all, 2)
    up_grad = jnp.zeros((row_count, w_dec.shape[2]), jnp.float32)
    for k in range(KW):
        up_grad = up_grad + jnp.dot(
            slope_pad[4 - k : 4 - k + row_count], w_dec[:, k, :], preferred_element_type=jnp.float32
        )
    pool_grad = up_grad.reshape(row_count // 2, 2, -1).sum(axis=1)
    act_grad = 0.5 * jnp.repeat(pool_grad, 2, axis=0)
    pre_grad = (act_grad * gelu_slope(enc_pre)).astype(jnp.bfloat16)
    pre_all = channel_gather(pre_grad)
    g_enc = weight_grad(pre_all, stem_pad)
    return (pred, g_enc, g_dec)


MESH_ID = pl.DeviceIdType.MESH
BF16 = jnp.bfloat16
F32 = jnp.float32
TILE = 16
SIDE = 8
RIM = 32
HALVES = 2
VMEM_BYTES = 48 * 1024 * 1024


def send(src, dst, send_sem, recv_sem, seq, chan):
    return pltpu.make_async_remote_copy(
        src_ref=src,
        dst_ref=dst,
        send_sem=send_sem,
        recv_sem=recv_sem,
        device_id={"seq": seq, "chan": chan},
        device_id_type=MESH_ID,
    )


def greet(targets):
    barrier = pltpu.get_barrier_semaphore()
    for seq, chan in targets:
        pl.semaphore_signal(
            barrier, inc=1, device_id={"seq": seq, "chan": chan}, device_id_type=MESH_ID
        )
    pl.semaphore_wait(barrier, len(targets))


def whole_group(n, s, c):
    others = []
    for ds in range(n):
        for dc in range(n):
            if ds or dc:
                others.append((lax.rem(s + ds, n), lax.rem(c + dc, n)))
    return others


def partners(c):
    mate = c + 1 - 2 * lax.rem(c, 2)
    across = lax.rem(c + 2, 4)
    return mate, across, lax.rem(mate + 2, 4)


def span(first, count):
    return pl.ds(first, count)


def tiles(first, count, body):
    @pl.loop(0, count // TILE)
    def _(i):
        body(pl.ds(pl.multiple_of(first + i * TILE, TILE), TILE))


class Part:
    def __init__(self, sem, base):
        self.sem, self.base = sem, base

    @property
    def at(self):
        return self

    def __getitem__(self, index):
        return self.sem.at[self.base + index]


class Turn:
    def __init__(self, n, s, c, h, own, mid, out, sems):
        self.n, self.s, self.c, self.h, self.own, self.mid, self.out = n, s, c, h, own, mid, out
        (self.cross_send, self.cross_recv, self.along_send, self.along_recv,
         self.share_send, self.share_recv, self.local) = sems
        self.count = own.shape[1]
        self.piece = self.count // n
        self.side = c // 2

    def out_rows(self, index):
        first = self.h * self.count + index * self.piece
        return pl.ds(pl.multiple_of(first, self.piece), self.piece)

    def cross(self):
        wide = 2 * self.piece
        at = pl.ds(pl.multiple_of((1 - self.side) * wide, wide), wide)
        return send(self.own.at[:, at], self.mid, self.cross_send.at[0], self.cross_recv.at[0],
                    self.s, partners(self.c)[1])

    def source(self, plane, q):
        if plane:
            first = (q - 2 * self.side) * self.piece
            return self.mid.at[:, pl.ds(pl.multiple_of(first, self.piece), self.piece)]
        return self.own.at[:, pl.ds(pl.multiple_of(q * self.piece, self.piece), self.piece)]

    def along(self, plane, kind, slot):
        mate, across, _ = partners(self.c)
        q = mate if kind else self.c
        return send(self.source(plane, q), self.out.at[self.s, :, self.out_rows(q)],
                    self.along_send.at[2 * plane + kind], self.along_recv.at[slot],
                    across if plane else self.c, q)

    def keep(self, plane):
        return pltpu.make_async_copy(
            self.source(plane, self.c), self.out.at[self.s, :, self.out_rows(self.c)], self.local
        )

    def home(self, plane):
        return self.s == (partners(self.c)[1] if plane else self.c)

    def start(self, plane):
        home = self.home(plane)
        pl.when(jnp.logical_not(home))(lambda: self.along(plane, 0, self.s).start())
        pl.when(home)(lambda: self.keep(plane).start())
        self.along(plane, 1, self.s).start()

    def share(self, slot, kind, part, to):
        spot = self.out.at[slot, :, self.out_rows(part)]
        index = slot * 3 + kind
        return send(spot, spot, self.share_send.at[index], self.share_recv.at[index], self.s, to)

    def forward(self, slot, mine):
        mate, across, _ = partners(self.c)
        if mine:
            pl.when(self.home(0))(lambda: self.keep(0).wait())
            pl.when(self.home(1))(lambda: self.keep(1).wait())
            other = jnp.logical_not(jnp.logical_or(self.home(0), self.home(1)))
            pl.when(other)(lambda: self.along(0, 0, slot).wait_recv())
        else:
            self.along(0, 0, slot).wait_recv()
        self.share(slot, 1, self.c, across).start()
        self.share(slot, 0, self.c, mate).start()

    def relay(self, slot):
        mate, across, _ = partners(self.c)
        self.share(slot, 1, across, across).wait_recv()
        self.share(slot, 2, across, mate).start()

    def finish(self, slot):
        mate, across, far = partners(self.c)
        self.share(slot, 0, mate, mate).wait_recv()
        self.share(slot, 2, far, mate).wait_recv()

    def end(self):
        mate, across, _ = partners(self.c)
        for slot in range(self.n):
            self.share(slot, 0, self.c, mate).wait_send()
            self.share(slot, 1, self.c, across).wait_send()
            self.share(slot, 2, across, mate).wait_send()
        self.cross().wait_send()
        for plane in range(2):
            pl.when(jnp.logical_not(self.home(plane)))(
                functools.partial(lambda plane: self.along(plane, 0, self.s).wait_send(), plane)
            )
            self.along(plane, 1, self.s).wait_send()


class PairSum:
    def __init__(self, block, held, pair, s, c, chunks, sems):
        self.block, self.held, self.pair, self.s, self.c = block, held, pair, s, c
        self.chunks = chunks
        self.send_sem, self.recv_sem = sems

    def hop(self, kind, q):
        mate, across, far = partners(self.c)
        source = (lambda: self.block(mate), lambda: self.block(far), lambda: self.pair)[kind]()
        target = (mate, mate, across)[kind]
        at = span(*self.chunks[q])
        index = kind * len(self.chunks) + q
        return send(source.at[:, at], self.held.at[kind, :, at], self.send_sem.at[index],
                    self.recv_sem.at[index], self.s, target)

    def start(self, kind):
        for q in range(len(self.chunks)):
            self.hop(kind, q).start()

    def cross(self, q):
        _, across, _ = partners(self.c)
        self.hop(1, q).wait_recv()
        block = self.block(across)

        def body(at):
            self.pair[:, at, :] = (
                block[:, at, :].astype(F32) + self.held[1, :, at, :].astype(F32)
            ).astype(BF16)

        tiles(*self.chunks[q], body)
        self.hop(2, q).start()

    def arrive(self, q):
        self.hop(0, q).wait_recv()
        self.hop(2, q).wait_recv()

    def total(self, at):
        mine = self.block(self.c)[:, at, :].astype(F32)
        return mine + self.held[0, :, at, :].astype(F32) + self.held[2, :, at, :].astype(F32)

    def end(self):
        for kind in range(3):
            for q in range(len(self.chunks)):
                self.hop(kind, q).wait_send()


class PoolRelay:
    def __init__(self, n, s, c, h, out, right_send, left_send, recv):
        self.n, self.s, self.c, self.out = n, s, c, out
        self.right_send, self.left_send, self.recv = right_send, left_send, recv
        self.at = span(h * (out.shape[1] // HALVES), out.shape[1] // HALVES)

    def hop(self, slot, step):
        sems = self.right_send if step > 0 else self.left_send
        spot = self.out.at[slot, self.at]
        return send(spot, spot, sems.at[slot], self.recv.at[slot], self.s + step, self.c)

    def start(self):
        pl.when(self.s < self.n - 1)(lambda: self.hop(self.s, 1).start())
        pl.when(self.s > 0)(lambda: self.hop(self.s, -1).start())

    def arrive(self, d):
        low, high = self.s - d, self.s + d

        @pl.when(low >= 0)
        def _():
            self.hop(low, 1).wait_recv()
            pl.when(self.s < self.n - 1)(lambda: self.hop(low, 1).start())

        @pl.when(high < self.n)
        def _():
            self.hop(high, -1).wait_recv()
            pl.when(self.s > 0)(lambda: self.hop(high, -1).start())

    def end(self):
        for slot in range(self.n):
            pl.when(jnp.logical_and(slot <= self.s, self.s < self.n - 1))(
                functools.partial(lambda slot: self.hop(slot, 1).wait_send(), slot)
            )
            pl.when(jnp.logical_and(slot >= self.s, self.s > 0))(
                functools.partial(lambda slot: self.hop(slot, -1).wait_send(), slot)
            )


class SlopeTurn:
    def __init__(self, n, s, c, chan, out, sems):
        self.n, self.s, self.c, self.chan, self.out = n, s, c, chan, out
        self.send_sem, self.recv_sem, self.share_send, self.share_recv, self.local = sems
        self.plane = lax.rem(c, 2)

    def hop(self, to, slot):
        return send(self.chan.at[to, self.plane], self.out.at[self.s, self.plane],
                    self.send_sem.at[to], self.recv_sem.at[slot], to, self.c)

    def start(self, block):
        pl.when(block != self.s)(lambda: self.hop(block, self.s).start())

    def keep(self):
        return pltpu.make_async_copy(self.chan.at[self.s], self.out.at[self.s], self.local)

    def share(self, slot, plane):
        mate, _, _ = partners(self.c)
        spot = self.out.at[slot, plane]
        return send(spot, spot, self.share_send.at[slot], self.share_recv.at[slot], self.s, mate)

    def forward(self, slot):
        self.hop(self.s, slot).wait_recv()
        self.share(slot, self.plane).start()

    def finish(self, slot):
        self.share(slot, 1 - self.plane).wait_recv()

    def end(self, others):
        for slot in others:
            self.share(slot, self.plane).wait_send()
            self.hop(slot, self.s).wait_send()


def across_rows(left, right):
    return lax.dot_general(left, right, (((0,), (0,)), ((), ())), preferred_element_type=F32)


def by_channels(left, right):
    return lax.dot_general(left, right, (((1,), (1,)), ((), ())), preferred_element_type=F32)


def train_kernel(
    n, scale, enc_chunks, bases_ref, w_stem_ref, target_in, w_enc_ref, w_dec_ref,
    pred_ref, g_enc_ref, g_dec_ref,
    bases, natural, near, w_enc, w_ref, part, target_ref, pred_pair, split,
    enc_held, enc_pair, bend, pool_wide, pool_near, dec_part, dec_held, dec_pair, q_wide,
    edge, slope, chan, up, pre_own, pre_mid, pre_seq, ab_seq, ab_wide, ab_near, pools, stems,
    enc_send, enc_recv, dec_send, dec_recv, edge_send, edge_recv, row_send, row_recv,
    right_send, left_send, pool_recv, bases_send, bases_recv, local_sem, *turn_sems,
):
    s, c = lax.axis_index("seq"), lax.axis_index("chan")
    mate, across, far = partners(c)
    rows, c2 = pool_near.shape[0], pool_wide.shape[1]
    own = rows - TILE
    pairs = HALVES * own
    c1 = near.shape[3]
    upper = s // 2
    slots = (s, 1 - s + 4 * upper, 2 - upper, 3 - 3 * upper)
    both_halves = range(HALVES)
    weight_copies = [
        pltpu.make_async_copy(w_enc_ref, w_enc, local_sem.at[0]),
        pltpu.make_async_copy(w_dec_ref, w_ref, local_sem.at[1]),
    ]
    for copy in weight_copies:
        copy.start()
    bases[s, :, :] = bases_ref[...]
    greet(whole_group(n, s, c))
    base_copies = [
        send(bases_ref, bases.at[s], bases_send.at[d - 1], bases_recv.at[d - 1],
             lax.rem(s + d, n), c)
        for d in range(1, n)
    ]
    for copy in base_copies:
        copy.start()

    def column_block(h, j):
        return part.at[h, :, :, pl.ds(pl.multiple_of(j * c2, 128), c2)]

    counts = 3 * len(enc_chunks)
    enc = [
        PairSum(functools.partial(column_block, h), enc_held.at[h], enc_pair.at[h], s, c,
                enc_chunks, (Part(enc_send, h * counts), Part(enc_recv, h * counts)))
        for h in both_halves
    ]
    dec = [
        PairSum(functools.partial(lambda h, j: dec_part.at[h, j], h), dec_held.at[h],
                dec_pair.at[h], s, c, ((0, rows),), (Part(dec_send, h * 3), Part(dec_recv, h * 3)))
        for h in both_halves
    ]
    relay = [
        PoolRelay(n, s, c, h, pools, *[Part(sem, h * n) for sem in (right_send, left_send, pool_recv)])
        for h in both_halves
    ]
    turn = [
        Turn(n, s, c, h, pre_own.at[h], pre_mid.at[h], pre_seq,
             [Part(sem, h * size) for sem, size in zip(turn_sems[:6], (1, 1, n, n, 3 * n, 3 * n))]
             + [turn_sems[6].at[h]])
        for h in both_halves
    ]
    slopes = [
        SlopeTurn(n, s, c, chan.at[h], ab_seq.at[h],
                  [Part(sem, h * n) for sem in turn_sems[7:11]] + [turn_sems[11].at[h]])
        for h in both_halves
    ]

    def stem_rows(slot):
        before = bases[lax.rem(slot + n - 1, n)]
        here = bases[slot]
        after = bases[lax.rem(slot + 1, n)]
        count = here.shape[0]
        lanes = [jnp.where(slot > 0, before[count - 1 :], -1)]
        lanes += [here[i : i + 1] for i in range(count)]
        lanes += [jnp.where(slot < n - 1, after[:1], -1)]
        line = jnp.concatenate(lanes, axis=1)
        total = line.shape[1]
        line = jnp.broadcast_to(line, (SIDE, total))
        kind = lax.broadcasted_iota(jnp.int32, (SIDE, total), 0)
        onehot = jnp.concatenate(
            [
                jnp.where(pltpu.roll(line, (2 - k) % total, 1) == kind, 1.0, 0.0)
                for k in range(KW)
            ],
            axis=0,
        ).astype(BF16)
        for i in range(count + 2):
            value = across_rows(onehot[:, i * 128 : (i + 1) * 128], w_stem_ref[...])
            first = 128 * (i - 1) + RIM
            if i == 0:
                first, value = 0, jnp.where(slot > 0, value[128 - RIM :], 0.0)
            if i == count + 1:
                value = jnp.where(slot < n - 1, value[:RIM], 0.0)
            value = gelu_value(value)
            for t in range(natural.shape[0]):
                natural[t, first : first + value.shape[0], :] = value[:, t * 128 : (t + 1) * 128]

    def every_other(t, first, count):
        return natural[t, pl.ds(first, count, stride=2), : min(128, c1 - t * 128)]

    def piece_start(i):
        return RIM + i % 2 + 2 * (i // 2 - 1)

    def lane_span(t):
        return slice(t * 128, min(c1, (t + 1) * 128))

    def near_rows():
        for h in both_halves:
            for i in range(6):
                first = piece_start(i) + 2 * own * h
                for t in range(natural.shape[0]):
                    halo = [every_other(t, first + 2 * own, SIDE), every_other(t, first - 2 * SIDE, SIDE)]
                    near[h, i, 0:TILE, lane_span(t)] = jnp.concatenate(halo, axis=0).astype(BF16)
                    near[h, i, TILE:, lane_span(t)] = every_other(t, first, own).astype(BF16)

    def keep_stems(slot):
        at = pl.ds(pl.multiple_of(slot * pairs, TILE), pairs)
        for i in range(6):
            for t in range(natural.shape[0]):
                stems[i, at, lane_span(t)] = every_other(t, piece_start(i), pairs).astype(BF16)

    def part_block(h, j):
        at = pl.ds(pl.multiple_of(j * c2, 128), c2)
        total = None
        for k in range(KW):
            window = near[h, k : k + 2].reshape(2 * rows, c1)
            term = jnp.dot(window, w_enc[k, :, at], preferred_element_type=F32)
            total = term if total is None else total + term
        part[h, :, :, at] = total.astype(BF16).reshape(2, rows, c2)

    edges = [
        send(target_ref.at[:, pl.ds(pairs - TILE, TILE)], edge.at[0], edge_send.at[0],
             edge_recv.at[0], lax.rem(s + 1, n), c),
        send(target_ref.at[:, pl.ds(0, TILE)], edge.at[1], edge_send.at[1], edge_recv.at[1],
             lax.rem(s + n - 1, n), c),
    ]

    def pair_targets():
        size = 2 * pairs
        for first in range(0, size, 128):
            place = lax.broadcasted_iota(jnp.int32, (128, size), 0) + first % pairs
            wanted = 2 * place + first // pairs
            column = lax.broadcasted_iota(jnp.int32, (128, size), 1)
            split[first : first + 128, :] = jnp.where(column == wanted, 1.0, 0.0).astype(BF16)
        for parity in range(2):
            value = by_channels(split[parity * pairs : (parity + 1) * pairs, :], target_in[...])
            target_ref[parity, :, :] = value.astype(BF16)

    for copy in base_copies:
        copy.wait()
    stem_rows(s)
    near_rows()
    weight_copies[0].wait()
    part_block(0, far)
    enc[0].start(1)
    part_block(0, across)
    part_block(1, far)
    enc[1].start(1)
    for q in range(len(enc_chunks)):
        enc[0].cross(q)
    part_block(1, across)
    for q in range(len(enc_chunks)):
        enc[1].cross(q)
    for h in both_halves:
        part_block(h, mate)
        enc[h].start(0)
        part_block(h, c)
    pair_targets()
    for copy in edges:
        copy.start()
    keep_stems(s)

    @pl.loop(1, n)
    def _(d):
        slot = lax.rem(s + d, n)
        stem_rows(slot)
        keep_stems(slot)

    weight_copies[1].wait()

    row = lax.broadcasted_iota(jnp.int32, (TILE, 1), 0)
    inside = (
        jnp.logical_or(row < SIDE, s > 0),
        jnp.logical_or(row >= SIDE, s < n - 1),
    )

    def enc_rows(h, at):
        total = enc[h].total(at)
        square = total * total
        inner = jnp.tanh(SQRT_TWO_PI * (total + CUBIC * square * total))
        active = (0.5 * total * (1.0 + inner)).astype(BF16).astype(F32)
        pooled = (0.5 * (active[0] + active[1])).astype(BF16).astype(F32)
        pool_wide[pl.ds(pl.multiple_of(at.start + SIDE, SIDE), TILE), :] = pooled
        bend[h, :, at, :] = 0.5 * (
            0.5 * (1.0 + inner)
            + 0.5 * total * (1.0 - inner * inner) * SQRT_TWO_PI * (1.0 + 3.0 * CUBIC * square)
        )

    def conv_block(h, j):
        at = pl.ds(pl.multiple_of(j * c1, TILE), c1)
        before, here, after = (pool_near[:, i * c2 : (i + 1) * c2] for i in range(3))
        shared = by_channels(before, w_ref[0, at, :]) + by_channels(here, w_ref[2, at, :])
        shared = shared + by_channels(after, w_ref[4, at, :])
        single = by_channels(before, w_ref[1, at, :]) + by_channels(here, w_ref[3, at, :])
        q_wide[0:rows, :] = single
        q_wide[rows:, :] = single[0:SIDE]
        dec_part[h, j, 0, :, :] = (shared + single).astype(BF16)
        dec_part[h, j, 1, :, :] = (shared + q_wide[1 : rows + 1, :]).astype(BF16)

    def encode(h):
        for q in range(len(enc_chunks)):
            enc[h].arrive(q)
            tiles(*enc_chunks[q], functools.partial(enc_rows, h))
        halo = pool_wide[SIDE : SIDE + TILE, :]
        pool_wide[SIDE : SIDE + TILE, :] = jnp.where(inside[h], halo, 0.0)
        pool_wide[0:SIDE, :] = pool_wide[rows : rows + SIDE, :]
        pool_wide[rows + SIDE :, :] = pool_wide[SIDE : 2 * SIDE, :]
        for first in range(0, rows, TILE):
            for shift in range(3):
                value = pool_wide[first + SIDE - 1 + shift : first + SIDE - 1 + shift + TILE, :]
                pool_near[first : first + TILE, shift * c2 : (shift + 1) * c2] = value.astype(BF16)
        conv_block(h, far)
        dec[h].start(1)
        pools[s, h * own : (h + 1) * own, :] = pool_near[TILE:, c2 : 2 * c2]
        relay[h].start()
        conv_block(h, across)
        dec[h].cross(0)
        conv_block(h, mate)
        dec[h].start(0)
        conv_block(h, c)

    def slope_tile(h, at, target, keep=None):
        output = dec[h].total(at) + near[h, 2:4, at, :].astype(F32)
        value = (output - target) * scale
        if keep is None:
            own_at = pl.ds(pl.multiple_of(at.start - TILE + h * own, TILE), TILE)
            pred_pair[:, own_at, :] = output.astype(BF16)
        else:
            value = jnp.where(keep[None], value, 0.0)
        slope[:, at, :] = value

    def slope_rows(h, at):
        own_at = pl.ds(pl.multiple_of(at.start - TILE + h * own, TILE), TILE)
        slope_tile(h, at, target_ref[:, own_at, :].astype(F32))

    def row_copy(h, kind, owner, to):
        spot = chan.at[h, owner]
        return send(spot, spot, row_send.at[h * 3 + kind], row_recv.at[h * 3 + kind], s, to)

    def decode(h):
        dec[h].arrive(0)
        high = target_ref[:, own : own + TILE, :] if h == 0 else edge[1]
        low = edge[0] if h == 0 else target_ref[:, own - TILE : own, :]
        target = jnp.where(row[None] < SIDE, high.astype(F32), low.astype(F32))
        slope_tile(h, pl.ds(0, TILE), target, inside[h])
        slope[:, rows:, :] = slope[:, 0:SIDE, :]
        tiles(TILE, own, functools.partial(slope_rows, h))
        for start in range(0, rows, TILE):
            even = slope[0, start : start + TILE, :]
            odd = slope[1, start : start + TILE, :]
            following = slope[0, start + 1 : start + 1 + TILE, :]
            chan[h, c, 0, start : start + TILE, :] = (even + odd).astype(BF16)
            chan[h, c, 1, start : start + TILE, :] = (odd + following).astype(BF16)
        row_copy(h, 1, c, across).start()
        row_copy(h, 0, c, mate).start()

    def up_block(h, j, first):
        at = pl.ds(pl.multiple_of(j * c1, TILE), c1)
        for place, terms in enumerate((((0, 0),), ((1, 1), (0, 2)), ((1, 3), (0, 4)))):
            total = None
            for plane, k in terms:
                term = jnp.dot(chan[h, j, plane], w_ref[k, at, :], preferred_element_type=F32)
                total = term if total is None else total + term
            if not first:
                total = total + up[place, SIDE : SIDE + rows, :]
            up[place, SIDE : SIDE + rows, :] = total

    def bend_back(h):
        up[0, SIDE + rows :, :] = up[0, SIDE : 2 * SIDE, :]
        for first in range(0, own, TILE):
            spot = first + TILE + SIDE
            grad = (
                up[0, spot + 1 : spot + 1 + TILE, :]
                + up[1, spot : spot + TILE, :]
                + up[2, spot - 1 : spot - 1 + TILE, :]
            )
            pre_own[h, :, first : first + TILE, :] = (
                grad[None] * bend[h, :, first + TILE : first + 2 * TILE, :]
            ).astype(BF16)
        turn[h].cross().start()
        turn[h].start(0)

    def back(h):
        up_block(h, c, True)
        row_copy(h, 0, mate, mate).wait_recv()
        up_block(h, mate, False)
        row_copy(h, 1, across, across).wait_recv()
        row_copy(h, 2, across, mate).start()
        up_block(h, across, False)
        row_copy(h, 2, far, mate).wait_recv()
        up_block(h, far, False)
        bend_back(h)

    def pass_on(h):
        turn[h].cross().wait_recv()
        turn[h].start(1)

    def turn_slopes(h):
        for block in (c, mate, across, far):
            slopes[h].start(block)
        slopes[h].keep().start()

    def decoder_grad(slot):
        for h in both_halves:
            for plane in range(2):
                value = ab_seq[h, slot, plane].astype(F32)
                ab_wide[plane, 0:rows, :] = value
                ab_wide[plane, rows:, :] = value[0:SIDE]
            for k, (plane, shift) in enumerate(((0, 1), (1, 0), (0, 0), (1, -1), (0, -1))):
                ab_near[k, h * own : (h + 1) * own, :] = ab_wide[
                    plane, TILE + shift : rows + shift, :
                ].astype(BF16)
        for k in range(KW):
            g_dec_ref[k, :, :] += across_rows(ab_near[k], pools[slot])

    def encoder_grad(slot):
        at = pl.ds(pl.multiple_of(slot * pairs, TILE), pairs)
        for k in range(KW):
            g_enc_ref[k, :, :] += across_rows(stems[k, at, :], pre_seq[slot, 0]) + across_rows(
                stems[k + 1, at, :], pre_seq[slot, 1]
            )

    encode(0)
    encode(1)
    for copy in edges:
        copy.wait()
    decode(0)
    relay[0].arrive(1)
    decode(1)
    relay[1].arrive(1)
    back(0)
    turn_slopes(0)
    relay[0].arrive(2)
    up_block(1, c, True)
    row_copy(1, 0, mate, mate).wait_recv()
    up_block(1, mate, False)
    row_copy(1, 1, across, across).wait_recv()
    row_copy(1, 2, across, mate).start()
    up_block(1, across, False)
    pass_on(0)
    row_copy(1, 2, far, mate).wait_recv()
    up_block(1, far, False)
    bend_back(1)
    g_enc_ref[...] = jnp.zeros_like(g_enc_ref)
    g_dec_ref[...] = jnp.zeros_like(g_dec_ref)
    merged = across_rows(pred_pair[0], split[0:pairs, :])
    pred_ref[...] = (merged + across_rows(pred_pair[1], split[pairs:, :])).astype(BF16)
    relay[1].arrive(2)
    pass_on(1)
    turn_slopes(1)
    for i in range(n):
        turn[0].forward(slots[i], i == 0)
    relay[0].arrive(3)
    for i in range(n):
        turn[1].forward(slots[i], i == 0)
        turn[0].relay(slots[i])
    relay[1].arrive(3)
    for slot in slots[1:]:
        slopes[0].forward(slot)
    for i in range(n):
        turn[1].relay(slots[i])
        if i:
            slopes[1].forward(slots[i])
            for h in both_halves:
                turn[h].finish(slots[i - 1])
            encoder_grad(slots[i - 1])
    for h in both_halves:
        slopes[h].keep().wait()
        for slot in slots[1:]:
            slopes[h].finish(slot)

    @pl.loop(0, n)
    def _(slot):
        decoder_grad(slot)

    for h in both_halves:
        turn[h].finish(slots[n - 1])
    encoder_grad(slots[n - 1])

    for h in both_halves:
        enc[h].end()
        dec[h].end()
        row_copy(h, 0, c, mate).wait_send()
        row_copy(h, 1, c, across).wait_send()
        row_copy(h, 2, across, mate).wait_send()
        relay[h].end()
        slopes[h].end(slots[1:])
        turn[h].end()


def dma(count):
    return pltpu.SemaphoreType.DMA((count,))


def square_shards(dna_bases, w_stem, w_enc, w_dec, targets):
    rows = dna_bases.shape[0]
    n = lax.axis_size("seq")
    half = rows // 2
    length, pairs = rows * n, half * n
    own = half // HALVES
    held = own + TILE
    c1, c2 = w_stem.shape[0], w_dec.shape[2]
    c1_wide = (c1 + 127) // 128 * 128
    struct = jax.ShapeDtypeStruct

    stem_weight = jnp.pad(w_stem, ((0, c1_wide - c1), (0, 0), (0, SIDE - 4)))
    stem_weight = stem_weight.transpose(1, 2, 0).reshape(KW * SIDE, c1_wide)
    cut = held // TILE // 2 * TILE
    enc_chunks = ((0, cut), (cut, held - cut))
    wide = held + SIDE
    double = HALVES * n
    counts = HALVES * 3 * len(enc_chunks)
    vmem = pl.BlockSpec(memory_space=pltpu.VMEM)
    anywhere = pl.BlockSpec(memory_space=pl.ANY)
    pred, g_enc, g_dec = pl.pallas_call(
        functools.partial(train_kernel, n, 1.0 / math.sqrt(length), enc_chunks),
        out_shape=(
            struct((c1, rows), BF16),
            struct((KW, c1, c2), F32),
            struct((KW, c1, c2), F32),
        ),
        in_specs=[vmem, vmem, vmem, anywhere, anywhere],
        out_specs=(vmem, vmem, vmem),
        scratch_shapes=[
            pltpu.VMEM((n, rows // 128, 128), jnp.int32),
            pltpu.VMEM((c1_wide // 128, rows + 2 * RIM, 128), F32),
            pltpu.VMEM((HALVES, 6, held, c1), BF16),
            pltpu.VMEM((KW, c1, n * c2), BF16),
            pltpu.VMEM((KW, n * c1, c2), BF16),
            pltpu.VMEM((HALVES, 2, held, n * c2), BF16),
            pltpu.VMEM((2, half, c1), BF16),
            pltpu.VMEM((2, half, c1), BF16),
            pltpu.VMEM((rows, rows), BF16),
            pltpu.VMEM((HALVES, 3, 2, held, c2), BF16),
            pltpu.VMEM((HALVES, 2, held, c2), BF16),
            pltpu.VMEM((HALVES, 2, held, c2), F32),
            pltpu.VMEM((held + 2 * SIDE, c2), F32),
            pltpu.VMEM((held, 3 * c2), BF16),
            pltpu.VMEM((HALVES, n, 2, held, c1), BF16),
            pltpu.VMEM((HALVES, 3, 2, held, c1), BF16),
            pltpu.VMEM((HALVES, 2, held, c1), BF16),
            pltpu.VMEM((wide, c1), F32),
            pltpu.VMEM((2, 2, TILE, c1), BF16),
            pltpu.VMEM((2, wide, c1), F32),
            pltpu.VMEM((HALVES, n, 2, held, c1), BF16),
            pltpu.VMEM((3, held + 2 * SIDE, c2), F32),
            pltpu.VMEM((HALVES, 2, own, c2), BF16),
            pltpu.VMEM((HALVES, 2, own // 2, c2), BF16),
            pltpu.VMEM((n, 2, half, c2), BF16),
            pltpu.VMEM((HALVES, n, 2, held, c1), BF16),
            pltpu.VMEM((2, wide, c1), F32),
            pltpu.VMEM((KW, half, c1), BF16),
            pltpu.VMEM((n, half, c2), BF16),
            pltpu.VMEM((6, pairs, c1), BF16),
            dma(counts), dma(counts), dma(HALVES * 3), dma(HALVES * 3), dma(2), dma(2),
            dma(HALVES * 3), dma(HALVES * 3), dma(double), dma(double), dma(double),
            dma(n - 1), dma(n - 1), dma(2),
            dma(HALVES), dma(HALVES), dma(double), dma(double), dma(3 * double), dma(3 * double),
            dma(HALVES),
            dma(double), dma(double), dma(double), dma(double), dma(HALVES),
        ],
        compiler_params=pltpu.CompilerParams(
            collective_id=0, has_side_effects=True, vmem_limit_bytes=VMEM_BYTES
        ),
    )(
        dna_bases.reshape(rows // 128, 128),
        stem_weight,
        targets.T,
        w_enc.transpose(1, 2, 0),
        w_dec.transpose(1, 0, 2),
    )
    return (pred.T, g_enc.transpose(2, 0, 1), g_dec.transpose(1, 0, 2))


def shards(dna_bases, w_stem, w_enc, w_dec, targets):
    args = (dna_bases, w_stem, w_enc, w_dec, targets)
    rows, c1, c2 = dna_bases.shape[0], w_stem.shape[0], w_dec.shape[2]
    n = lax.axis_size("seq")
    square = n == 4 and lax.axis_size("chan") == 4
    if square and rows % 512 == 0 and c2 % 128 == 0 and c1 % 64 == 0:
        return square_shards(*args)
    return general_shards(*args)


def solution(mesh):
    return jax.shard_map(
        shards,
        mesh=mesh,
        in_specs=(
            P(("groups", "seq")),
            P("chan", None, None),
            P(None, None, "chan"),
            P(None, None, "chan"),
            P(("groups", "seq"), "chan"),
        ),
        out_specs=(
            P(("groups", "seq"), "chan"),
            P(("groups", "seq"), None, "chan"),
            P(("groups", "seq"), None, "chan"),
        ),
        check_vma=False,
    )
```

```python
import functools
import math

import jax
import jax.numpy as jnp
from jax import lax
from jax.experimental import pallas as pl
from jax.experimental.pallas import tpu as pltpu
from jax.sharding import PartitionSpec as P

KW = 5


SQRT_TWO_PI = 0.7978845608028654
CUBIC = 0.044715


def extended(block, sides, width):
    for axis, dim in sides:
        count = lax.axis_size(axis)
        forward = [(i, i + 1) for i in range(count - 1)]
        backward = [(target, source) for source, target in forward]
        low = lax.ppermute(
            lax.slice_in_dim(block, block.shape[dim] - width, None, axis=dim), axis, forward
        )
        high = lax.ppermute(lax.slice_in_dim(block, 0, width, axis=dim), axis, backward)
        block = jnp.concatenate([low, block, high], axis=dim)
    return block


def gelu_value(value):
    inner = jnp.tanh(SQRT_TWO_PI * (value + CUBIC * value * value * value))
    return 0.5 * value * (1.0 + inner)


def gelu_slope(value):
    inner = jnp.tanh(SQRT_TWO_PI * (value + CUBIC * value * value * value))
    return 0.5 * (1.0 + inner) + 0.5 * value * (1.0 - inner * inner) * SQRT_TWO_PI * (
        1.0 + 3.0 * CUBIC * value * value
    )


def rim_cells(block, margin):
    return extended(block, (("seq", 0),), margin)


def channel_sum(partial_value):
    return lax.psum_scatter(partial_value, "chan", scatter_dimension=1, tiled=True)


def channel_gather(block):
    return lax.all_gather(block, "chan", axis=1, tiled=True)


def conv_rows(padded, weight):
    row_count = padded.shape[0] - 4
    total = jnp.zeros((row_count, weight.shape[0]), jnp.float32)
    for k in range(KW):
        total = total + lax.dot_general(
            padded[k : k + row_count],
            weight[:, k, :],
            (((1,), (1,)), ((), ())),
            preferred_element_type=jnp.float32,
        )
    return total


def grad_taps(picked, padded):
    row_count = picked.shape[0]
    pieces = [
        lax.dot_general(
            picked,
            padded[k : k + row_count],
            (((0,), (0,)), ((), ())),
            preferred_element_type=jnp.float32,
        )
        for k in range(KW)
    ]
    return jnp.stack(pieces, axis=1)


def weight_grad(cotangent, padded):
    rounded = grad_taps(cotangent, padded).astype(jnp.bfloat16)
    return lax.psum_scatter(
        lax.optimization_barrier(rounded).astype(jnp.float32),
        "seq",
        scatter_dimension=0,
        tiled=True,
    )


def general_shards(dna_bases, w_stem, w_enc, w_dec, targets):
    row_count = dna_bases.shape[0]
    devices = lax.axis_size("seq")
    length = row_count * devices
    onehot = (dna_bases[:, None] == jnp.arange(4, dtype=jnp.int32)[None, :]).astype(jnp.bfloat16)
    onehot_pad = rim_cells(onehot, 2)
    stem_out = gelu_value(conv_rows(onehot_pad, w_stem)).astype(jnp.bfloat16)
    stem_pad = rim_cells(stem_out, 2)
    enc_pre = channel_sum(conv_rows(stem_pad, w_enc))
    active = gelu_value(enc_pre).astype(jnp.bfloat16).astype(jnp.float32)
    pooled = (0.5 * active.reshape(row_count // 2, 2, -1).sum(axis=1)).astype(jnp.bfloat16)
    pooled_pad = rim_cells(pooled, 1)
    up_pad = jnp.repeat(pooled_pad, 2, axis=0)
    output = channel_sum(conv_rows(up_pad, w_dec)) + stem_out.astype(jnp.float32)
    pred = output.astype(jnp.bfloat16)
    scale = 1.0 / math.sqrt(length)
    slope_out = ((output - targets.astype(jnp.float32)) * scale).astype(jnp.bfloat16)
    slope_all = channel_gather(slope_out)
    g_dec = weight_grad(slope_all, up_pad)
    slope_pad = rim_cells(slope_all, 2)
    up_grad = jnp.zeros((row_count, w_dec.shape[2]), jnp.float32)
    for k in range(KW):
        up_grad = up_grad + jnp.dot(
            slope_pad[4 - k : 4 - k + row_count], w_dec[:, k, :], preferred_element_type=jnp.float32
        )
    pool_grad = up_grad.reshape(row_count // 2, 2, -1).sum(axis=1)
    act_grad = 0.5 * jnp.repeat(pool_grad, 2, axis=0)
    pre_grad = (act_grad * gelu_slope(enc_pre)).astype(jnp.bfloat16)
    pre_all = channel_gather(pre_grad)
    g_enc = weight_grad(pre_all, stem_pad)
    return (pred, g_enc, g_dec)


MESH_ID = pl.DeviceIdType.MESH
BF16 = jnp.bfloat16
F32 = jnp.float32
TILE = 16
SIDE = 8
RIM = 32
HALVES = 2
VMEM_BYTES = 48 * 1024 * 1024


def send(src, dst, send_sem, recv_sem, seq, chan):
    return pltpu.make_async_remote_copy(
        src_ref=src,
        dst_ref=dst,
        send_sem=send_sem,
        recv_sem=recv_sem,
        device_id={"seq": seq, "chan": chan},
        device_id_type=MESH_ID,
    )


def greet(targets):
    barrier = pltpu.get_barrier_semaphore()
    for seq, chan in targets:
        pl.semaphore_signal(
            barrier, inc=1, device_id={"seq": seq, "chan": chan}, device_id_type=MESH_ID
        )
    pl.semaphore_wait(barrier, len(targets))


def whole_group(n, s, c):
    others = []
    for ds in range(n):
        for dc in range(n):
            if ds or dc:
                others.append((lax.rem(s + ds, n), lax.rem(c + dc, n)))
    return others


def partners(c):
    mate = c + 1 - 2 * lax.rem(c, 2)
    across = lax.rem(c + 2, 4)
    return mate, across, lax.rem(mate + 2, 4)


def span(first, count):
    return pl.ds(first, count)


def tiles(first, count, body):
    @pl.loop(0, count // TILE)
    def _(i):
        body(pl.ds(pl.multiple_of(first + i * TILE, TILE), TILE))


class Part:
    def __init__(self, sem, base):
        self.sem, self.base = sem, base

    @property
    def at(self):
        return self

    def __getitem__(self, index):
        return self.sem.at[self.base + index]


class Turn:
    def __init__(self, n, s, c, h, own, mid, out, sems):
        self.n, self.s, self.c, self.h, self.own, self.mid, self.out = n, s, c, h, own, mid, out
        (self.cross_send, self.cross_recv, self.along_send, self.along_recv,
         self.share_send, self.share_recv, self.local) = sems
        self.count = own.shape[1]
        self.piece = self.count // n
        self.side = c // 2

    def out_rows(self, index):
        first = self.h * self.count + index * self.piece
        return pl.ds(pl.multiple_of(first, self.piece), self.piece)

    def cross(self):
        wide = 2 * self.piece
        at = pl.ds(pl.multiple_of((1 - self.side) * wide, wide), wide)
        return send(self.own.at[:, at], self.mid, self.cross_send.at[0], self.cross_recv.at[0],
                    self.s, partners(self.c)[1])

    def source(self, plane, q):
        if plane:
            first = (q - 2 * self.side) * self.piece
            return self.mid.at[:, pl.ds(pl.multiple_of(first, self.piece), self.piece)]
        return self.own.at[:, pl.ds(pl.multiple_of(q * self.piece, self.piece), self.piece)]

    def along(self, plane, kind, slot):
        mate, across, _ = partners(self.c)
        q = mate if kind else self.c
        return send(self.source(plane, q), self.out.at[self.s, :, self.out_rows(q)],
                    self.along_send.at[2 * plane + kind], self.along_recv.at[slot],
                    across if plane else self.c, q)

    def keep(self, plane):
        return pltpu.make_async_copy(
            self.source(plane, self.c), self.out.at[self.s, :, self.out_rows(self.c)], self.local
        )

    def home(self, plane):
        return self.s == (partners(self.c)[1] if plane else self.c)

    def start(self, plane):
        home = self.home(plane)
        pl.when(jnp.logical_not(home))(lambda: self.along(plane, 0, self.s).start())
        pl.when(home)(lambda: self.keep(plane).start())
        self.along(plane, 1, self.s).start()

    def share(self, slot, kind, part, to):
        spot = self.out.at[slot, :, self.out_rows(part)]
        index = slot * 3 + kind
        return send(spot, spot, self.share_send.at[index], self.share_recv.at[index], self.s, to)

    def forward(self, slot, mine):
        mate, across, _ = partners(self.c)
        if mine:
            pl.when(self.home(0))(lambda: self.keep(0).wait())
            pl.when(self.home(1))(lambda: self.keep(1).wait())
            other = jnp.logical_not(jnp.logical_or(self.home(0), self.home(1)))
            pl.when(other)(lambda: self.along(0, 0, slot).wait_recv())
        else:
            self.along(0, 0, slot).wait_recv()
        self.share(slot, 1, self.c, across).start()
        self.share(slot, 0, self.c, mate).start()

    def relay(self, slot):
        mate, across, _ = partners(self.c)
        self.share(slot, 1, across, across).wait_recv()
        self.share(slot, 2, across, mate).start()

    def finish(self, slot):
        mate, across, far = partners(self.c)
        self.share(slot, 0, mate, mate).wait_recv()
        self.share(slot, 2, far, mate).wait_recv()

    def end(self):
        mate, across, _ = partners(self.c)
        for slot in range(self.n):
            self.share(slot, 0, self.c, mate).wait_send()
            self.share(slot, 1, self.c, across).wait_send()
            self.share(slot, 2, across, mate).wait_send()
        self.cross().wait_send()
        for plane in range(2):
            pl.when(jnp.logical_not(self.home(plane)))(
                functools.partial(lambda plane: self.along(plane, 0, self.s).wait_send(), plane)
            )
            self.along(plane, 1, self.s).wait_send()


class PairSum:
    def __init__(self, block, held, pair, s, c, chunks, sems):
        self.block, self.held, self.pair, self.s, self.c = block, held, pair, s, c
        self.chunks = chunks
        self.send_sem, self.recv_sem = sems

    def hop(self, kind, q):
        mate, across, far = partners(self.c)
        source = (lambda: self.block(mate), lambda: self.block(far), lambda: self.pair)[kind]()
        target = (mate, mate, across)[kind]
        at = span(*self.chunks[q])
        index = kind * len(self.chunks) + q
        return send(source.at[:, at], self.held.at[kind, :, at], self.send_sem.at[index],
                    self.recv_sem.at[index], self.s, target)

    def start(self, kind):
        for q in range(len(self.chunks)):
            self.hop(kind, q).start()

    def cross(self, q):
        _, across, _ = partners(self.c)
        self.hop(1, q).wait_recv()
        block = self.block(across)

        def body(at):
            self.pair[:, at, :] = (
                block[:, at, :].astype(F32) + self.held[1, :, at, :].astype(F32)
            ).astype(BF16)

        tiles(*self.chunks[q], body)
        self.hop(2, q).start()

    def arrive(self, q):
        self.hop(0, q).wait_recv()
        self.hop(2, q).wait_recv()

    def total(self, at):
        mine = self.block(self.c)[:, at, :].astype(F32)
        return mine + self.held[0, :, at, :].astype(F32) + self.held[2, :, at, :].astype(F32)

    def end(self):
        for kind in range(3):
            for q in range(len(self.chunks)):
                self.hop(kind, q).wait_send()


class PoolRelay:
    def __init__(self, n, s, c, h, out, right_send, left_send, recv):
        self.n, self.s, self.c, self.out = n, s, c, out
        self.right_send, self.left_send, self.recv = right_send, left_send, recv
        self.at = span(h * (out.shape[1] // HALVES), out.shape[1] // HALVES)

    def hop(self, slot, step):
        sems = self.right_send if step > 0 else self.left_send
        spot = self.out.at[slot, self.at]
        return send(spot, spot, sems.at[slot], self.recv.at[slot], self.s + step, self.c)

    def start(self):
        pl.when(self.s < self.n - 1)(lambda: self.hop(self.s, 1).start())
        pl.when(self.s > 0)(lambda: self.hop(self.s, -1).start())

    def arrive(self, d):
        low, high = self.s - d, self.s + d

        @pl.when(low >= 0)
        def _():
            self.hop(low, 1).wait_recv()
            pl.when(self.s < self.n - 1)(lambda: self.hop(low, 1).start())

        @pl.when(high < self.n)
        def _():
            self.hop(high, -1).wait_recv()
            pl.when(self.s > 0)(lambda: self.hop(high, -1).start())

    def end(self):
        for slot in range(self.n):
            pl.when(jnp.logical_and(slot <= self.s, self.s < self.n - 1))(
                functools.partial(lambda slot: self.hop(slot, 1).wait_send(), slot)
            )
            pl.when(jnp.logical_and(slot >= self.s, self.s > 0))(
                functools.partial(lambda slot: self.hop(slot, -1).wait_send(), slot)
            )


class SlopeTurn:
    def __init__(self, n, s, c, chan, out, sems):
        self.n, self.s, self.c, self.chan, self.out = n, s, c, chan, out
        self.send_sem, self.recv_sem, self.share_send, self.share_recv, self.local = sems
        self.plane = lax.rem(c, 2)

    def hop(self, to, slot):
        return send(self.chan.at[to, self.plane], self.out.at[self.s, self.plane],
                    self.send_sem.at[to], self.recv_sem.at[slot], to, self.c)

    def start(self, block):
        pl.when(block != self.s)(lambda: self.hop(block, self.s).start())

    def keep(self):
        return pltpu.make_async_copy(self.chan.at[self.s], self.out.at[self.s], self.local)

    def share(self, slot, plane):
        mate, _, _ = partners(self.c)
        spot = self.out.at[slot, plane]
        return send(spot, spot, self.share_send.at[slot], self.share_recv.at[slot], self.s, mate)

    def forward(self, slot):
        self.hop(self.s, slot).wait_recv()
        self.share(slot, self.plane).start()

    def finish(self, slot):
        self.share(slot, 1 - self.plane).wait_recv()

    def end(self, others):
        for slot in others:
            self.share(slot, self.plane).wait_send()
            self.hop(slot, self.s).wait_send()


def across_rows(left, right):
    return lax.dot_general(left, right, (((0,), (0,)), ((), ())), preferred_element_type=F32)


def by_channels(left, right):
    return lax.dot_general(left, right, (((1,), (1,)), ((), ())), preferred_element_type=F32)


def train_kernel(
    n, scale, enc_chunks, bases_ref, w_stem_hbm, target_hbm, w_enc_ref, w_dec_ref,
    pred_ref, g_enc_ref, g_dec_ref,
    w_stem_small, w_stem_ref, target_in, bases, natural, near, w_enc, w_ref, part, target_ref, pred_pair, split,
    enc_held, enc_pair, bend, pool_wide, pool_near, dec_part, dec_held, dec_pair, q_wide,
    edge, slope, chan, up, pre_own, pre_mid, pre_seq, ab_seq, ab_wide, ab_near, pools, stems,
    enc_send, enc_recv, dec_send, dec_recv, edge_send, edge_recv, row_send, row_recv,
    right_send, left_send, pool_recv, bases_send, bases_recv, local_sem, *turn_sems,
):
    s, c = lax.axis_index("seq"), lax.axis_index("chan")
    mate, across, far = partners(c)
    rows, c2 = pool_near.shape[0], pool_wide.shape[1]
    own = rows - TILE
    pairs = HALVES * own
    c1 = near.shape[3]
    upper = s // 2
    slots = (s, 1 - s + 4 * upper, 2 - upper, 3 - 3 * upper)
    both_halves = range(HALVES)
    weight_copies = [
        pltpu.make_async_copy(w_enc_ref, w_enc, local_sem.at[0]),
        pltpu.make_async_copy(w_dec_ref, w_ref, local_sem.at[1]),
    ]
    small_copies = [
        pltpu.make_async_copy(bases_ref, bases.at[s], local_sem.at[2]),
        pltpu.make_async_copy(w_stem_hbm, w_stem_small, local_sem.at[3]),
        pltpu.make_async_copy(target_hbm, target_in, local_sem.at[4]),
    ]
    for copy in small_copies[:2] + weight_copies[:1] + small_copies[2:] + weight_copies[1:]:
        copy.start()
    greet(whole_group(n, s, c))
    small_copies[0].wait()
    base_copies = [
        send(bases.at[s], bases.at[s], bases_send.at[d - 1], bases_recv.at[d - 1],
             lax.rem(s + d, n), c)
        for d in range(1, n)
    ]
    for copy in base_copies:
        copy.start()

    def column_block(h, j):
        return part.at[h, :, :, pl.ds(pl.multiple_of(j * c2, 128), c2)]

    counts = 3 * len(enc_chunks)
    enc = [
        PairSum(functools.partial(column_block, h), enc_held.at[h], enc_pair.at[h], s, c,
                enc_chunks, (Part(enc_send, h * counts), Part(enc_recv, h * counts)))
        for h in both_halves
    ]
    dec = [
        PairSum(functools.partial(lambda h, j: dec_part.at[h, j], h), dec_held.at[h],
                dec_pair.at[h], s, c, ((0, rows),), (Part(dec_send, h * 3), Part(dec_recv, h * 3)))
        for h in both_halves
    ]
    relay = [
        PoolRelay(n, s, c, h, pools, *[Part(sem, h * n) for sem in (right_send, left_send, pool_recv)])
        for h in both_halves
    ]
    turn = [
        Turn(n, s, c, h, pre_own.at[h], pre_mid.at[h], pre_seq,
             [Part(sem, h * size) for sem, size in zip(turn_sems[:6], (1, 1, n, n, 3 * n, 3 * n))]
             + [turn_sems[6].at[h]])
        for h in both_halves
    ]
    slopes = [
        SlopeTurn(n, s, c, chan.at[h], ab_seq.at[h],
                  [Part(sem, h * n) for sem in turn_sems[7:11]] + [turn_sems[11].at[h]])
        for h in both_halves
    ]

    def stem_rows(slot):
        before = bases[lax.rem(slot + n - 1, n)]
        here = bases[slot]
        after = bases[lax.rem(slot + 1, n)]
        count = here.shape[0]
        lanes = [jnp.where(slot > 0, before[count - 1 :], -1)]
        lanes += [here[i : i + 1] for i in range(count)]
        lanes += [jnp.where(slot < n - 1, after[:1], -1)]
        line = jnp.concatenate(lanes, axis=1)
        total = line.shape[1]
        line = jnp.broadcast_to(line, (SIDE, total))
        kind = lax.broadcasted_iota(jnp.int32, (SIDE, total), 0)
        onehot = jnp.concatenate(
            [
                jnp.where(pltpu.roll(line, (2 - k) % total, 1) == kind, 1.0, 0.0)
                for k in range(KW)
            ],
            axis=0,
        ).astype(BF16)
        for i in range(count + 2):
            value = across_rows(onehot[:, i * 128 : (i + 1) * 128], w_stem_ref[...].astype(BF16))
            first = 128 * (i - 1) + RIM
            if i == 0:
                first, value = 0, jnp.where(slot > 0, value[128 - RIM :], 0.0)
            if i == count + 1:
                value = jnp.where(slot < n - 1, value[:RIM], 0.0)
            value = gelu_value(value)
            for t in range(natural.shape[0]):
                natural[t, first : first + value.shape[0], :] = value[:, t * 128 : (t + 1) * 128]

    def every_other(t, first, count):
        return natural[t, pl.ds(first, count, stride=2), : min(128, c1 - t * 128)]

    def piece_start(i):
        return RIM + i % 2 + 2 * (i // 2 - 1)

    def lane_span(t):
        return slice(t * 128, min(c1, (t + 1) * 128))

    def near_rows():
        for h in both_halves:
            for i in range(6):
                first = piece_start(i) + 2 * own * h
                for t in range(natural.shape[0]):
                    halo = [every_other(t, first + 2 * own, SIDE), every_other(t, first - 2 * SIDE, SIDE)]
                    near[h, i, 0:TILE, lane_span(t)] = jnp.concatenate(halo, axis=0).astype(BF16)
                    near[h, i, TILE:, lane_span(t)] = every_other(t, first, own).astype(BF16)

    def keep_stems(slot):
        at = pl.ds(pl.multiple_of(slot * pairs, TILE), pairs)
        for i in range(6):
            for t in range(natural.shape[0]):
                stems[i, at, lane_span(t)] = every_other(t, piece_start(i), pairs).astype(BF16)

    def part_block(h, j):
        at = pl.ds(pl.multiple_of(j * c2, 128), c2)
        total = None
        for k in range(KW):
            window = near[h, k : k + 2].reshape(2 * rows, c1)
            term = jnp.dot(window, w_enc[k, :, at], preferred_element_type=F32)
            total = term if total is None else total + term
        part[h, :, :, at] = total.astype(BF16).reshape(2, rows, c2)

    edges = [
        send(target_ref.at[:, pl.ds(pairs - TILE, TILE)], edge.at[0], edge_send.at[0],
             edge_recv.at[0], lax.rem(s + 1, n), c),
        send(target_ref.at[:, pl.ds(0, TILE)], edge.at[1], edge_send.at[1], edge_recv.at[1],
             lax.rem(s + n - 1, n), c),
    ]

    def pair_targets():
        size = 2 * pairs
        for first in range(0, size, 128):
            place = lax.broadcasted_iota(jnp.int32, (128, size), 0) + first % pairs
            wanted = 2 * place + first // pairs
            column = lax.broadcasted_iota(jnp.int32, (128, size), 1)
            split[first : first + 128, :] = jnp.where(column == wanted, 1.0, 0.0).astype(BF16)
        for parity in range(2):
            value = by_channels(split[parity * pairs : (parity + 1) * pairs, :], target_in[...])
            target_ref[parity, :, :] = value.astype(BF16)

    small_copies[1].wait()
    w_stem_ref[...] = jnp.zeros_like(w_stem_ref)
    for k in range(KW):
        w_stem_ref[k * SIDE : k * SIDE + 4, 0:c1] = w_stem_small[k].astype(F32)
    for copy in base_copies:
        copy.wait()
    stem_rows(s)
    near_rows()
    weight_copies[0].wait()
    part_block(0, far)
    enc[0].start(1)
    part_block(0, across)
    part_block(1, far)
    enc[1].start(1)
    for q in range(len(enc_chunks)):
        enc[0].cross(q)
    part_block(1, across)
    for q in range(len(enc_chunks)):
        enc[1].cross(q)
    for h in both_halves:
        part_block(h, mate)
        enc[h].start(0)
        part_block(h, c)
    small_copies[2].wait()
    pair_targets()
    for copy in edges:
        copy.start()
    keep_stems(s)

    @pl.loop(1, n)
    def _(d):
        slot = lax.rem(s + d, n)
        stem_rows(slot)
        keep_stems(slot)

    weight_copies[1].wait()

    row = lax.broadcasted_iota(jnp.int32, (TILE, 1), 0)
    inside = (
        jnp.logical_or(row < SIDE, s > 0),
        jnp.logical_or(row >= SIDE, s < n - 1),
    )

    def enc_rows(h, at):
        total = enc[h].total(at)
        square = total * total
        inner = jnp.tanh(SQRT_TWO_PI * (total + CUBIC * square * total))
        active = (0.5 * total * (1.0 + inner)).astype(BF16).astype(F32)
        pooled = (0.5 * (active[0] + active[1])).astype(BF16).astype(F32)
        pool_wide[pl.ds(pl.multiple_of(at.start + SIDE, SIDE), TILE), :] = pooled
        bend[h, :, at, :] = 0.5 * (
            0.5 * (1.0 + inner)
            + 0.5 * total * (1.0 - inner * inner) * SQRT_TWO_PI * (1.0 + 3.0 * CUBIC * square)
        )

    def conv_block(h, j):
        at = pl.ds(pl.multiple_of(j * c1, TILE), c1)
        before, here, after = (pool_near[:, i * c2 : (i + 1) * c2] for i in range(3))
        shared = by_channels(before, w_ref[0, at, :]) + by_channels(here, w_ref[2, at, :])
        shared = shared + by_channels(after, w_ref[4, at, :])
        single = by_channels(before, w_ref[1, at, :]) + by_channels(here, w_ref[3, at, :])
        q_wide[0:rows, :] = single
        q_wide[rows:, :] = single[0:SIDE]
        dec_part[h, j, 0, :, :] = (shared + single).astype(BF16)
        dec_part[h, j, 1, :, :] = (shared + q_wide[1 : rows + 1, :]).astype(BF16)

    def encode(h):
        for q in range(len(enc_chunks)):
            enc[h].arrive(q)
            tiles(*enc_chunks[q], functools.partial(enc_rows, h))
        halo = pool_wide[SIDE : SIDE + TILE, :]
        pool_wide[SIDE : SIDE + TILE, :] = jnp.where(inside[h], halo, 0.0)
        pool_wide[0:SIDE, :] = pool_wide[rows : rows + SIDE, :]
        pool_wide[rows + SIDE :, :] = pool_wide[SIDE : 2 * SIDE, :]
        for first in range(0, rows, TILE):
            for shift in range(3):
                value = pool_wide[first + SIDE - 1 + shift : first + SIDE - 1 + shift + TILE, :]
                pool_near[first : first + TILE, shift * c2 : (shift + 1) * c2] = value.astype(BF16)
        conv_block(h, far)
        dec[h].start(1)
        pools[s, h * own : (h + 1) * own, :] = pool_near[TILE:, c2 : 2 * c2]
        relay[h].start()
        conv_block(h, across)
        dec[h].cross(0)
        conv_block(h, mate)
        dec[h].start(0)
        conv_block(h, c)

    def slope_tile(h, at, target, keep=None):
        output = dec[h].total(at) + near[h, 2:4, at, :].astype(F32)
        value = (output - target) * scale
        if keep is None:
            own_at = pl.ds(pl.multiple_of(at.start - TILE + h * own, TILE), TILE)
            pred_pair[:, own_at, :] = output.astype(BF16)
        else:
            value = jnp.where(keep[None], value, 0.0)
        slope[:, at, :] = value

    def slope_rows(h, at):
        own_at = pl.ds(pl.multiple_of(at.start - TILE + h * own, TILE), TILE)
        slope_tile(h, at, target_ref[:, own_at, :].astype(F32))

    def row_copy(h, kind, owner, to):
        spot = chan.at[h, owner]
        return send(spot, spot, row_send.at[h * 3 + kind], row_recv.at[h * 3 + kind], s, to)

    def decode(h):
        dec[h].arrive(0)
        high = target_ref[:, own : own + TILE, :] if h == 0 else edge[1]
        low = edge[0] if h == 0 else target_ref[:, own - TILE : own, :]
        target = jnp.where(row[None] < SIDE, high.astype(F32), low.astype(F32))
        slope_tile(h, pl.ds(0, TILE), target, inside[h])
        slope[:, rows:, :] = slope[:, 0:SIDE, :]
        tiles(TILE, own, functools.partial(slope_rows, h))
        for start in range(0, rows, TILE):
            even = slope[0, start : start + TILE, :]
            odd = slope[1, start : start + TILE, :]
            following = slope[0, start + 1 : start + 1 + TILE, :]
            chan[h, c, 0, start : start + TILE, :] = (even + odd).astype(BF16)
            chan[h, c, 1, start : start + TILE, :] = (odd + following).astype(BF16)
        row_copy(h, 1, c, across).start()
        row_copy(h, 0, c, mate).start()

    def up_block(h, j, first):
        at = pl.ds(pl.multiple_of(j * c1, TILE), c1)
        for place, terms in enumerate((((0, 0),), ((1, 1), (0, 2)), ((1, 3), (0, 4)))):
            total = None
            for plane, k in terms:
                term = jnp.dot(chan[h, j, plane], w_ref[k, at, :], preferred_element_type=F32)
                total = term if total is None else total + term
            if not first:
                total = total + up[place, SIDE : SIDE + rows, :]
            up[place, SIDE : SIDE + rows, :] = total

    def bend_back(h):
        up[0, SIDE + rows :, :] = up[0, SIDE : 2 * SIDE, :]
        for first in range(0, own, TILE):
            spot = first + TILE + SIDE
            grad = (
                up[0, spot + 1 : spot + 1 + TILE, :]
                + up[1, spot : spot + TILE, :]
                + up[2, spot - 1 : spot - 1 + TILE, :]
            )
            pre_own[h, :, first : first + TILE, :] = (
                grad[None] * bend[h, :, first + TILE : first + 2 * TILE, :]
            ).astype(BF16)
        turn[h].cross().start()
        turn[h].start(0)

    def near_grad(h):
        slopes[h].start(c)
        up_block(h, c, True)
        row_copy(h, 0, mate, mate).wait_recv()
        slopes[h].start(mate)
        up_block(h, mate, False)

    def across_grad(h):
        row_copy(h, 1, across, across).wait_recv()
        row_copy(h, 2, across, mate).start()
        up_block(h, across, False)

    def far_grad(h):
        row_copy(h, 2, far, mate).wait_recv()
        up_block(h, far, False)
        bend_back(h)

    def pass_on(h):
        turn[h].cross().wait_recv()
        turn[h].start(1)

    def turn_slopes(h):
        for block in (across, far):
            slopes[h].start(block)
        slopes[h].keep().start()

    def decoder_grad(slot):
        for h in both_halves:
            for plane in range(2):
                value = ab_seq[h, slot, plane].astype(F32)
                ab_wide[plane, 0:rows, :] = value
                ab_wide[plane, rows:, :] = value[0:SIDE]
            for k, (plane, shift) in enumerate(((0, 1), (1, 0), (0, 0), (1, -1), (0, -1))):
                ab_near[k, h * own : (h + 1) * own, :] = ab_wide[
                    plane, TILE + shift : rows + shift, :
                ].astype(BF16)
        for k in range(KW):
            g_dec_ref[k, :, :] += across_rows(ab_near[k], pools[slot])

    def encoder_grad(slot):
        at = pl.ds(pl.multiple_of(slot * pairs, TILE), pairs)
        for k in range(KW):
            g_enc_ref[k, :, :] += across_rows(stems[k, at, :], pre_seq[slot, 0]) + across_rows(
                stems[k + 1, at, :], pre_seq[slot, 1]
            )

    encode(0)
    encode(1)
    for copy in edges:
        copy.wait()
    decode(0)
    relay[0].arrive(1)
    near_grad(0)
    decode(1)
    relay[1].arrive(1)
    across_grad(0)
    far_grad(0)
    turn_slopes(0)
    relay[0].arrive(2)
    near_grad(1)
    across_grad(1)
    pass_on(0)
    far_grad(1)
    g_enc_ref[...] = jnp.zeros_like(g_enc_ref)
    g_dec_ref[...] = jnp.zeros_like(g_dec_ref)
    merged = across_rows(pred_pair[0], split[0:pairs, :])
    pred_ref[...] = (merged + across_rows(pred_pair[1], split[pairs:, :])).astype(BF16)
    relay[1].arrive(2)
    pass_on(1)
    turn_slopes(1)
    for h in both_halves:
        slopes[h].keep().wait()
    decoder_grad(s)
    for i in range(n):
        turn[0].forward(slots[i], i == 0)
    relay[0].arrive(3)
    for slot in slots[1:]:
        slopes[0].forward(slot)
    for i in range(n):
        turn[1].forward(slots[i], i == 0)
        turn[0].relay(slots[i])
    relay[1].arrive(3)
    for slot in slots[1:]:
        slopes[1].forward(slot)
    for i in range(n):
        turn[1].relay(slots[i])
        if i:
            for h in both_halves:
                slopes[h].finish(slots[i])
            decoder_grad(slots[i])
            for h in both_halves:
                turn[h].finish(slots[i - 1])
            encoder_grad(slots[i - 1])
    for h in both_halves:
        turn[h].finish(slots[n - 1])
    encoder_grad(slots[n - 1])

    for h in both_halves:
        enc[h].end()
        dec[h].end()
        row_copy(h, 0, c, mate).wait_send()
        row_copy(h, 1, c, across).wait_send()
        row_copy(h, 2, across, mate).wait_send()
        relay[h].end()
        slopes[h].end(slots[1:])
        turn[h].end()


def store_kernel(*refs):
    count = (len(refs) - 1) // 2
    sems = refs[-1]
    copies = []
    for source, target in zip(refs[:count], refs[count:-1]):
        parts = source.shape[0] if len(source.shape) == 3 else 1
        for i in range(parts):
            pair = (source.at[i], target.at[i]) if len(source.shape) == 3 else (source, target)
            copies.append(pltpu.make_async_copy(*pair, sems.at[len(copies)]))
    for copy in copies:
        copy.start()
    for copy in copies:
        copy.wait()


def store(*values):
    return pl.pallas_call(
        store_kernel,
        out_shape=tuple(jax.ShapeDtypeStruct(value.shape, value.dtype) for value in values),
        in_specs=[pl.BlockSpec(memory_space=pl.ANY)] * len(values),
        out_specs=(pl.BlockSpec(memory_space=pltpu.HBM),) * len(values),
        scratch_shapes=[dma(2 * KW + len(values))],
        compiler_params=pltpu.CompilerParams(vmem_limit_bytes=1024 * 1024),
    )(*values)


def dma(count):
    return pltpu.SemaphoreType.DMA((count,))


def square_shards(dna_bases, w_stem, w_enc, w_dec, targets):
    rows = dna_bases.shape[0]
    n = lax.axis_size("seq")
    half = rows // 2
    length, pairs = rows * n, half * n
    own = half // HALVES
    held = own + TILE
    c1, c2 = w_stem.shape[0], w_dec.shape[2]
    c1_wide = (c1 + 127) // 128 * 128
    struct = jax.ShapeDtypeStruct

    cut = held // TILE // 2 * TILE
    enc_chunks = ((0, cut), (cut, held - cut))
    wide = held + SIDE
    double = HALVES * n
    counts = HALVES * 3 * len(enc_chunks)
    vmem = pl.BlockSpec(memory_space=pltpu.VMEM)
    anywhere = pl.BlockSpec(memory_space=pl.ANY)
    pred, g_enc, g_dec = pl.pallas_call(
        functools.partial(train_kernel, n, 1.0 / math.sqrt(length), enc_chunks),
        out_shape=(
            struct((c1, rows), BF16),
            struct((KW, c1, c2), F32),
            struct((KW, c1, c2), F32),
        ),
        in_specs=[anywhere] * 5,
        out_specs=(vmem, vmem, vmem),
        scratch_shapes=[
            pltpu.VMEM((KW, 4, c1), BF16),
            pltpu.VMEM((KW * SIDE, c1_wide), F32),
            pltpu.VMEM((c1, rows), BF16),
            pltpu.VMEM((n, rows // 128, 128), jnp.int32),
            pltpu.VMEM((c1_wide // 128, rows + 2 * RIM, 128), F32),
            pltpu.VMEM((HALVES, 6, held, c1), BF16),
            pltpu.VMEM((KW, c1, n * c2), BF16),
            pltpu.VMEM((KW, n * c1, c2), BF16),
            pltpu.VMEM((HALVES, 2, held, n * c2), BF16),
            pltpu.VMEM((2, half, c1), BF16),
            pltpu.VMEM((2, half, c1), BF16),
            pltpu.VMEM((rows, rows), BF16),
            pltpu.VMEM((HALVES, 3, 2, held, c2), BF16),
            pltpu.VMEM((HALVES, 2, held, c2), BF16),
            pltpu.VMEM((HALVES, 2, held, c2), F32),
            pltpu.VMEM((held + 2 * SIDE, c2), F32),
            pltpu.VMEM((held, 3 * c2), BF16),
            pltpu.VMEM((HALVES, n, 2, held, c1), BF16),
            pltpu.VMEM((HALVES, 3, 2, held, c1), BF16),
            pltpu.VMEM((HALVES, 2, held, c1), BF16),
            pltpu.VMEM((wide, c1), F32),
            pltpu.VMEM((2, 2, TILE, c1), BF16),
            pltpu.VMEM((2, wide, c1), F32),
            pltpu.VMEM((HALVES, n, 2, held, c1), BF16),
            pltpu.VMEM((3, held + 2 * SIDE, c2), F32),
            pltpu.VMEM((HALVES, 2, own, c2), BF16),
            pltpu.VMEM((HALVES, 2, own // 2, c2), BF16),
            pltpu.VMEM((n, 2, half, c2), BF16),
            pltpu.VMEM((HALVES, n, 2, held, c1), BF16),
            pltpu.VMEM((2, wide, c1), F32),
            pltpu.VMEM((KW, half, c1), BF16),
            pltpu.VMEM((n, half, c2), BF16),
            pltpu.VMEM((6, pairs, c1), BF16),
            dma(counts), dma(counts), dma(HALVES * 3), dma(HALVES * 3), dma(2), dma(2),
            dma(HALVES * 3), dma(HALVES * 3), dma(double), dma(double), dma(double),
            dma(n - 1), dma(n - 1), dma(5),
            dma(HALVES), dma(HALVES), dma(double), dma(double), dma(3 * double), dma(3 * double),
            dma(HALVES),
            dma(double), dma(double), dma(double), dma(double), dma(HALVES),
        ],
        compiler_params=pltpu.CompilerParams(
            collective_id=0, has_side_effects=True, vmem_limit_bytes=VMEM_BYTES
        ),
    )(
        dna_bases.reshape(rows // 128, 128),
        w_stem.transpose(1, 2, 0),
        targets.T,
        w_enc.transpose(1, 2, 0),
        w_dec.transpose(1, 0, 2),
    )
    pred, g_enc, g_dec = store(pred, g_enc, g_dec)
    return (pred.T, g_enc.transpose(2, 0, 1), g_dec.transpose(1, 0, 2))


def shards(dna_bases, w_stem, w_enc, w_dec, targets):
    args = (dna_bases, w_stem, w_enc, w_dec, targets)
    rows, c1, c2 = dna_bases.shape[0], w_stem.shape[0], w_dec.shape[2]
    n = lax.axis_size("seq")
    square = n == 4 and lax.axis_size("chan") == 4
    if square and rows % 512 == 0 and c2 % 128 == 0 and c1 % 64 == 0:
        return square_shards(*args)
    return general_shards(*args)


def solution(mesh):
    return jax.shard_map(
        shards,
        mesh=mesh,
        in_specs=(
            P(("groups", "seq")),
            P("chan", None, None),
            P(None, None, "chan"),
            P(None, None, "chan"),
            P(("groups", "seq"), "chan"),
        ),
        out_specs=(
            P(("groups", "seq"), "chan"),
            P(("groups", "seq"), None, "chan"),
            P(("groups", "seq"), None, "chan"),
        ),
        check_vma=False,
    )
```

```python
import functools
import math

import jax
import jax.numpy as jnp
from jax import lax
from jax.experimental import pallas as pl
from jax.experimental.pallas import tpu as pltpu
from jax.sharding import PartitionSpec as P

KW = 5


SQRT_TWO_PI = 0.7978845608028654
CUBIC = 0.044715


def extended(block, sides, width):
    for axis, dim in sides:
        count = lax.axis_size(axis)
        forward = [(i, i + 1) for i in range(count - 1)]
        backward = [(target, source) for source, target in forward]
        low = lax.ppermute(
            lax.slice_in_dim(block, block.shape[dim] - width, None, axis=dim), axis, forward
        )
        high = lax.ppermute(lax.slice_in_dim(block, 0, width, axis=dim), axis, backward)
        block = jnp.concatenate([low, block, high], axis=dim)
    return block


def gelu_value(value):
    inner = jnp.tanh(SQRT_TWO_PI * (value + CUBIC * value * value * value))
    return 0.5 * value * (1.0 + inner)


def gelu_slope(value):
    inner = jnp.tanh(SQRT_TWO_PI * (value + CUBIC * value * value * value))
    return 0.5 * (1.0 + inner) + 0.5 * value * (1.0 - inner * inner) * SQRT_TWO_PI * (
        1.0 + 3.0 * CUBIC * value * value
    )


def rim_cells(block, margin):
    return extended(block, (("seq", 0),), margin)


def channel_sum(partial_value):
    return lax.psum_scatter(partial_value, "chan", scatter_dimension=1, tiled=True)


def channel_gather(block):
    return lax.all_gather(block, "chan", axis=1, tiled=True)


def conv_rows(padded, weight):
    row_count = padded.shape[0] - 4
    total = jnp.zeros((row_count, weight.shape[0]), jnp.float32)
    for k in range(KW):
        total = total + lax.dot_general(
            padded[k : k + row_count],
            weight[:, k, :],
            (((1,), (1,)), ((), ())),
            preferred_element_type=jnp.float32,
        )
    return total


def grad_taps(picked, padded):
    row_count = picked.shape[0]
    pieces = [
        lax.dot_general(
            picked,
            padded[k : k + row_count],
            (((0,), (0,)), ((), ())),
            preferred_element_type=jnp.float32,
        )
        for k in range(KW)
    ]
    return jnp.stack(pieces, axis=1)


def weight_grad(cotangent, padded):
    rounded = grad_taps(cotangent, padded).astype(jnp.bfloat16)
    return lax.psum_scatter(
        lax.optimization_barrier(rounded).astype(jnp.float32),
        "seq",
        scatter_dimension=0,
        tiled=True,
    )


def general_shards(dna_bases, w_stem, w_enc, w_dec, targets):
    row_count = dna_bases.shape[0]
    devices = lax.axis_size("seq")
    length = row_count * devices
    onehot = (dna_bases[:, None] == jnp.arange(4, dtype=jnp.int32)[None, :]).astype(jnp.bfloat16)
    onehot_pad = rim_cells(onehot, 2)
    stem_out = gelu_value(conv_rows(onehot_pad, w_stem)).astype(jnp.bfloat16)
    stem_pad = rim_cells(stem_out, 2)
    enc_pre = channel_sum(conv_rows(stem_pad, w_enc))
    active = gelu_value(enc_pre).astype(jnp.bfloat16).astype(jnp.float32)
    pooled = (0.5 * active.reshape(row_count // 2, 2, -1).sum(axis=1)).astype(jnp.bfloat16)
    pooled_pad = rim_cells(pooled, 1)
    up_pad = jnp.repeat(pooled_pad, 2, axis=0)
    output = channel_sum(conv_rows(up_pad, w_dec)) + stem_out.astype(jnp.float32)
    pred = output.astype(jnp.bfloat16)
    scale = 1.0 / math.sqrt(length)
    slope_out = ((output - targets.astype(jnp.float32)) * scale).astype(jnp.bfloat16)
    slope_all = channel_gather(slope_out)
    g_dec = weight_grad(slope_all, up_pad)
    slope_pad = rim_cells(slope_all, 2)
    up_grad = jnp.zeros((row_count, w_dec.shape[2]), jnp.float32)
    for k in range(KW):
        up_grad = up_grad + jnp.dot(
            slope_pad[4 - k : 4 - k + row_count], w_dec[:, k, :], preferred_element_type=jnp.float32
        )
    pool_grad = up_grad.reshape(row_count // 2, 2, -1).sum(axis=1)
    act_grad = 0.5 * jnp.repeat(pool_grad, 2, axis=0)
    pre_grad = (act_grad * gelu_slope(enc_pre)).astype(jnp.bfloat16)
    pre_all = channel_gather(pre_grad)
    g_enc = weight_grad(pre_all, stem_pad)
    return (pred, g_enc, g_dec)


MESH_ID = pl.DeviceIdType.MESH
BF16 = jnp.bfloat16
F32 = jnp.float32
TILE = 16
SIDE = 8
RIM = 32
HALVES = 2
VMEM_BYTES = 48 * 1024 * 1024


def send(src, dst, send_sem, recv_sem, seq, chan):
    return pltpu.make_async_remote_copy(
        src_ref=src,
        dst_ref=dst,
        send_sem=send_sem,
        recv_sem=recv_sem,
        device_id={"seq": seq, "chan": chan},
        device_id_type=MESH_ID,
    )


def greet(targets):
    barrier = pltpu.get_barrier_semaphore()
    for seq, chan in targets:
        pl.semaphore_signal(
            barrier, inc=1, device_id={"seq": seq, "chan": chan}, device_id_type=MESH_ID
        )
    pl.semaphore_wait(barrier, len(targets))


def whole_group(n, s, c):
    others = []
    for ds in range(n):
        for dc in range(n):
            if ds or dc:
                others.append((lax.rem(s + ds, n), lax.rem(c + dc, n)))
    return others


def partners(c):
    mate = c + 1 - 2 * lax.rem(c, 2)
    across = lax.rem(c + 2, 4)
    return mate, across, lax.rem(mate + 2, 4)


def span(first, count):
    return pl.ds(first, count)


def tiles(first, count, body):
    @pl.loop(0, count // TILE)
    def _(i):
        body(pl.ds(pl.multiple_of(first + i * TILE, TILE), TILE))


class Part:
    def __init__(self, sem, base):
        self.sem, self.base = sem, base

    @property
    def at(self):
        return self

    def __getitem__(self, index):
        return self.sem.at[self.base + index]


class Turn:
    def __init__(self, n, s, c, h, own, mid, out, sems):
        self.n, self.s, self.c, self.h, self.own, self.mid, self.out = n, s, c, h, own, mid, out
        (self.cross_send, self.cross_recv, self.along_send, self.along_recv,
         self.share_send, self.share_recv, self.local) = sems
        self.count = own.shape[1]
        self.piece = self.count // n
        self.side = c // 2

    def out_rows(self, index):
        first = self.h * self.count + index * self.piece
        return pl.ds(pl.multiple_of(first, self.piece), self.piece)

    def cross(self):
        wide = 2 * self.piece
        at = pl.ds(pl.multiple_of((1 - self.side) * wide, wide), wide)
        return send(self.own.at[:, at], self.mid, self.cross_send.at[0], self.cross_recv.at[0],
                    self.s, partners(self.c)[1])

    def source(self, plane, q):
        if plane:
            first = (q - 2 * self.side) * self.piece
            return self.mid.at[:, pl.ds(pl.multiple_of(first, self.piece), self.piece)]
        return self.own.at[:, pl.ds(pl.multiple_of(q * self.piece, self.piece), self.piece)]

    def along(self, plane, kind, slot):
        mate, across, _ = partners(self.c)
        q = mate if kind else self.c
        return send(self.source(plane, q), self.out.at[self.s, :, self.out_rows(q)],
                    self.along_send.at[2 * plane + kind], self.along_recv.at[slot],
                    across if plane else self.c, q)

    def keep(self, plane):
        return pltpu.make_async_copy(
            self.source(plane, self.c), self.out.at[self.s, :, self.out_rows(self.c)], self.local
        )

    def home(self, plane):
        return self.s == (partners(self.c)[1] if plane else self.c)

    def start(self, plane):
        home = self.home(plane)
        pl.when(jnp.logical_not(home))(lambda: self.along(plane, 0, self.s).start())
        pl.when(home)(lambda: self.keep(plane).start())
        self.along(plane, 1, self.s).start()

    def share(self, slot, kind, part, to):
        spot = self.out.at[slot, :, self.out_rows(part)]
        index = slot * 3 + kind
        return send(spot, spot, self.share_send.at[index], self.share_recv.at[index], self.s, to)

    def forward(self, slot, mine):
        mate, across, _ = partners(self.c)
        if mine:
            pl.when(self.home(0))(lambda: self.keep(0).wait())
            pl.when(self.home(1))(lambda: self.keep(1).wait())
            other = jnp.logical_not(jnp.logical_or(self.home(0), self.home(1)))
            pl.when(other)(lambda: self.along(0, 0, slot).wait_recv())
        else:
            self.along(0, 0, slot).wait_recv()
        self.share(slot, 1, self.c, across).start()
        self.share(slot, 0, self.c, mate).start()

    def relay(self, slot):
        mate, across, _ = partners(self.c)
        self.share(slot, 1, across, across).wait_recv()
        self.share(slot, 2, across, mate).start()

    def finish(self, slot):
        mate, across, far = partners(self.c)
        self.share(slot, 0, mate, mate).wait_recv()
        self.share(slot, 2, far, mate).wait_recv()

    def end(self):
        mate, across, _ = partners(self.c)
        for slot in range(self.n):
            self.share(slot, 0, self.c, mate).wait_send()
            self.share(slot, 1, self.c, across).wait_send()
            self.share(slot, 2, across, mate).wait_send()
        self.cross().wait_send()
        for plane in range(2):
            pl.when(jnp.logical_not(self.home(plane)))(
                functools.partial(lambda plane: self.along(plane, 0, self.s).wait_send(), plane)
            )
            self.along(plane, 1, self.s).wait_send()


class PairSum:
    def __init__(self, block, held, pair, s, c, chunks, sems):
        self.block, self.held, self.pair, self.s, self.c = block, held, pair, s, c
        self.chunks = chunks
        self.send_sem, self.recv_sem = sems

    def hop(self, kind, q):
        mate, across, far = partners(self.c)
        source = (lambda: self.block(mate), lambda: self.block(far), lambda: self.pair)[kind]()
        target = (mate, mate, across)[kind]
        at = span(*self.chunks[q])
        index = kind * len(self.chunks) + q
        return send(source.at[:, at], self.held.at[kind, :, at], self.send_sem.at[index],
                    self.recv_sem.at[index], self.s, target)

    def start(self, kind):
        for q in range(len(self.chunks)):
            self.hop(kind, q).start()

    def cross(self, q):
        _, across, _ = partners(self.c)
        self.hop(1, q).wait_recv()
        block = self.block(across)

        def body(at):
            self.pair[:, at, :] = (
                block[:, at, :].astype(F32) + self.held[1, :, at, :].astype(F32)
            ).astype(BF16)

        tiles(*self.chunks[q], body)
        self.hop(2, q).start()

    def arrive(self, q):
        self.hop(0, q).wait_recv()
        self.hop(2, q).wait_recv()

    def total(self, at):
        mine = self.block(self.c)[:, at, :].astype(F32)
        return mine + self.held[0, :, at, :].astype(F32) + self.held[2, :, at, :].astype(F32)

    def end(self):
        for kind in range(3):
            for q in range(len(self.chunks)):
                self.hop(kind, q).wait_send()


class PoolRelay:
    def __init__(self, n, s, c, h, out, right_send, left_send, recv):
        self.n, self.s, self.c, self.out = n, s, c, out
        self.right_send, self.left_send, self.recv = right_send, left_send, recv
        self.at = span(h * (out.shape[1] // HALVES), out.shape[1] // HALVES)

    def hop(self, slot, step):
        sems = self.right_send if step > 0 else self.left_send
        spot = self.out.at[slot, self.at]
        return send(spot, spot, sems.at[slot], self.recv.at[slot], self.s + step, self.c)

    def start(self):
        pl.when(self.s < self.n - 1)(lambda: self.hop(self.s, 1).start())
        pl.when(self.s > 0)(lambda: self.hop(self.s, -1).start())

    def arrive(self, d):
        low, high = self.s - d, self.s + d

        @pl.when(low >= 0)
        def _():
            self.hop(low, 1).wait_recv()
            pl.when(self.s < self.n - 1)(lambda: self.hop(low, 1).start())

        @pl.when(high < self.n)
        def _():
            self.hop(high, -1).wait_recv()
            pl.when(self.s > 0)(lambda: self.hop(high, -1).start())

    def end(self):
        for slot in range(self.n):
            pl.when(jnp.logical_and(slot <= self.s, self.s < self.n - 1))(
                functools.partial(lambda slot: self.hop(slot, 1).wait_send(), slot)
            )
            pl.when(jnp.logical_and(slot >= self.s, self.s > 0))(
                functools.partial(lambda slot: self.hop(slot, -1).wait_send(), slot)
            )


class SlopeTurn:
    def __init__(self, n, s, c, chan, out, sems):
        self.n, self.s, self.c, self.chan, self.out = n, s, c, chan, out
        (self.send_sem, self.recv_sem, self.cross_send, self.cross_recv,
         self.share_send, self.share_recv, self.local) = sems
        self.plane = c // 2
        self.hub = lax.rem(s, 2) == lax.rem(c, 2)

    def hop(self, to, slot):
        return send(self.chan.at[to, self.plane], self.out.at[self.s, self.plane],
                    self.send_sem.at[to], self.recv_sem.at[slot], to, self.c)

    def mine(self, block):
        return jnp.logical_and(block != self.s, lax.rem(block, 2) == lax.rem(self.c, 2))

    def start(self, block):
        pl.when(self.mine(block))(lambda: self.hop(block, self.s).start())

    def keep(self):
        return pltpu.make_async_copy(self.chan.at[self.s], self.out.at[self.s], self.local)

    def cross(self, slot, plane):
        spot = self.out.at[slot, plane]
        return send(spot, spot, self.cross_send.at[slot], self.cross_recv.at[slot], self.s,
                    partners(self.c)[1])

    def share(self, slot, plane):
        spot = self.out.at[slot, plane]
        return send(spot, spot, self.share_send.at[2 * slot + plane],
                    self.share_recv.at[2 * slot + plane], self.s, partners(self.c)[0])

    def forward(self, slot):
        @pl.when(self.hub)
        def _():
            self.hop(self.s, slot).wait_recv()
            self.cross(slot, self.plane).start()
            self.share(slot, self.plane).start()

    def relay(self, slot):
        @pl.when(self.hub)
        def _():
            self.cross(slot, 1 - self.plane).wait_recv()
            self.share(slot, 1 - self.plane).start()

    def finish(self, slot):
        @pl.when(jnp.logical_not(self.hub))
        def _():
            for plane in range(2):
                self.share(slot, plane).wait_recv()

    def end(self, others):
        for slot in others:
            pl.when(self.mine(slot))(
                functools.partial(lambda slot: self.hop(slot, self.s).wait_send(), slot)
            )

        @pl.when(self.hub)
        def _():
            for slot in others:
                self.cross(slot, self.plane).wait_send()
                for plane in range(2):
                    self.share(slot, plane).wait_send()


def across_rows(left, right):
    return lax.dot_general(left, right, (((0,), (0,)), ((), ())), preferred_element_type=F32)


def by_channels(left, right):
    return lax.dot_general(left, right, (((1,), (1,)), ((), ())), preferred_element_type=F32)


def train_kernel(
    n, scale, enc_chunks, bases_ref, w_stem_hbm, target_hbm, w_enc_ref, w_dec_ref,
    pred_ref, g_enc_ref, g_dec_ref,
    w_stem_small, w_stem_ref, target_in, bases, natural, near, w_enc, w_ref, part, target_ref, pred_pair, split,
    enc_held, enc_pair, bend, pool_wide, pool_near, dec_part, dec_held, dec_pair, q_wide,
    edge, slope, chan, up, pre_own, pre_mid, pre_seq, ab_seq, ab_wide, ab_near, pools, stems,
    enc_send, enc_recv, dec_send, dec_recv, edge_send, edge_recv, row_send, row_recv,
    right_send, left_send, pool_recv, bases_send, bases_recv, local_sem, *turn_sems,
):
    s, c = lax.axis_index("seq"), lax.axis_index("chan")
    mate, across, far = partners(c)
    rows, c2 = pool_near.shape[0], pool_wide.shape[1]
    own = rows - TILE
    pairs = HALVES * own
    c1 = near.shape[3]
    upper = s // 2
    slots = (s, 1 - s + 4 * upper, 2 - upper, 3 - 3 * upper)
    both_halves = range(HALVES)
    weight_copies = [
        pltpu.make_async_copy(w_enc_ref, w_enc, local_sem.at[0]),
        pltpu.make_async_copy(w_dec_ref, w_ref, local_sem.at[1]),
    ]
    small_copies = [
        pltpu.make_async_copy(bases_ref, bases.at[s], local_sem.at[2]),
        pltpu.make_async_copy(w_stem_hbm, w_stem_small, local_sem.at[3]),
        pltpu.make_async_copy(target_hbm, target_in, local_sem.at[4]),
    ]
    for copy in small_copies[:2] + weight_copies[:1] + small_copies[2:] + weight_copies[1:]:
        copy.start()
    greet(whole_group(n, s, c))
    small_copies[0].wait()
    base_copies = [
        send(bases.at[s], bases.at[s], bases_send.at[d - 1], bases_recv.at[d - 1],
             lax.rem(s + d, n), c)
        for d in range(1, n)
    ]
    for copy in base_copies:
        copy.start()

    def column_block(h, j):
        return part.at[h, :, :, pl.ds(pl.multiple_of(j * c2, 128), c2)]

    counts = 3 * len(enc_chunks)
    enc = [
        PairSum(functools.partial(column_block, h), enc_held.at[h], enc_pair.at[h], s, c,
                enc_chunks, (Part(enc_send, h * counts), Part(enc_recv, h * counts)))
        for h in both_halves
    ]
    dec = [
        PairSum(functools.partial(lambda h, j: dec_part.at[h, j], h), dec_held.at[h],
                dec_pair.at[h], s, c, ((0, rows),), (Part(dec_send, h * 3), Part(dec_recv, h * 3)))
        for h in both_halves
    ]
    relay = [
        PoolRelay(n, s, c, h, pools, *[Part(sem, h * n) for sem in (right_send, left_send, pool_recv)])
        for h in both_halves
    ]
    turn = [
        Turn(n, s, c, h, pre_own.at[h], pre_mid.at[h], pre_seq,
             [Part(sem, h * size) for sem, size in zip(turn_sems[:6], (1, 1, n, n, 3 * n, 3 * n))]
             + [turn_sems[6].at[h]])
        for h in both_halves
    ]
    slopes = [
        SlopeTurn(n, s, c, chan.at[h], ab_seq.at[h],
                  [Part(sem, h * n) for sem in turn_sems[7:11]]
                  + [Part(sem, 2 * h * n) for sem in turn_sems[11:13]] + [turn_sems[13].at[h]])
        for h in both_halves
    ]

    def stem_rows(slot):
        before = bases[lax.rem(slot + n - 1, n)]
        here = bases[slot]
        after = bases[lax.rem(slot + 1, n)]
        count = here.shape[0]
        lanes = [jnp.where(slot > 0, before[count - 1 :], -1)]
        lanes += [here[i : i + 1] for i in range(count)]
        lanes += [jnp.where(slot < n - 1, after[:1], -1)]
        line = jnp.concatenate(lanes, axis=1)
        total = line.shape[1]
        line = jnp.broadcast_to(line, (SIDE, total))
        kind = lax.broadcasted_iota(jnp.int32, (SIDE, total), 0)
        onehot = jnp.concatenate(
            [
                jnp.where(pltpu.roll(line, (2 - k) % total, 1) == kind, 1.0, 0.0)
                for k in range(KW)
            ],
            axis=0,
        ).astype(BF16)
        for i in range(count + 2):
            value = across_rows(onehot[:, i * 128 : (i + 1) * 128], w_stem_ref[...].astype(BF16))
            first = 128 * (i - 1) + RIM
            if i == 0:
                first, value = 0, jnp.where(slot > 0, value[128 - RIM :], 0.0)
            if i == count + 1:
                value = jnp.where(slot < n - 1, value[:RIM], 0.0)
            value = gelu_value(value)
            for t in range(natural.shape[0]):
                natural[t, first : first + value.shape[0], :] = value[:, t * 128 : (t + 1) * 128]

    def every_other(t, first, count):
        return natural[t, pl.ds(first, count, stride=2), : min(128, c1 - t * 128)]

    def piece_start(i):
        return RIM + i % 2 + 2 * (i // 2 - 1)

    def lane_span(t):
        return slice(t * 128, min(c1, (t + 1) * 128))

    def near_rows():
        for h in both_halves:
            for i in range(6):
                first = piece_start(i) + 2 * own * h
                for t in range(natural.shape[0]):
                    halo = [every_other(t, first + 2 * own, SIDE), every_other(t, first - 2 * SIDE, SIDE)]
                    near[h, i, 0:TILE, lane_span(t)] = jnp.concatenate(halo, axis=0).astype(BF16)
                    near[h, i, TILE:, lane_span(t)] = every_other(t, first, own).astype(BF16)

    def keep_stems(slot):
        at = pl.ds(pl.multiple_of(slot * pairs, TILE), pairs)
        for i in range(6):
            for t in range(natural.shape[0]):
                stems[i, at, lane_span(t)] = every_other(t, piece_start(i), pairs).astype(BF16)

    def part_block(h, j):
        at = pl.ds(pl.multiple_of(j * c2, 128), c2)
        total = None
        for k in range(KW):
            window = near[h, k : k + 2].reshape(2 * rows, c1)
            term = jnp.dot(window, w_enc[k, :, at], preferred_element_type=F32)
            total = term if total is None else total + term
        part[h, :, :, at] = total.astype(BF16).reshape(2, rows, c2)

    edges = [
        send(target_ref.at[:, pl.ds(pairs - TILE, TILE)], edge.at[0], edge_send.at[0],
             edge_recv.at[0], lax.rem(s + 1, n), c),
        send(target_ref.at[:, pl.ds(0, TILE)], edge.at[1], edge_send.at[1], edge_recv.at[1],
             lax.rem(s + n - 1, n), c),
    ]

    def pair_targets():
        size = 2 * pairs
        for first in range(0, size, 128):
            place = lax.broadcasted_iota(jnp.int32, (128, size), 0) + first % pairs
            wanted = 2 * place + first // pairs
            column = lax.broadcasted_iota(jnp.int32, (128, size), 1)
            split[first : first + 128, :] = jnp.where(column == wanted, 1.0, 0.0).astype(BF16)
        for parity in range(2):
            value = by_channels(split[parity * pairs : (parity + 1) * pairs, :], target_in[...])
            target_ref[parity, :, :] = value.astype(BF16)

    small_copies[1].wait()
    w_stem_ref[...] = jnp.zeros_like(w_stem_ref)
    for k in range(KW):
        w_stem_ref[k * SIDE : k * SIDE + 4, 0:c1] = w_stem_small[k].astype(F32)
    for copy in base_copies:
        copy.wait()
    stem_rows(s)
    near_rows()
    weight_copies[0].wait()
    part_block(0, far)
    enc[0].start(1)
    part_block(0, across)
    part_block(1, far)
    enc[1].start(1)
    for q in range(len(enc_chunks)):
        enc[0].cross(q)
    part_block(1, across)
    for q in range(len(enc_chunks)):
        enc[1].cross(q)
    for h in both_halves:
        part_block(h, mate)
        enc[h].start(0)
        part_block(h, c)
    small_copies[2].wait()
    pair_targets()
    for copy in edges:
        copy.start()
    keep_stems(s)

    @pl.loop(1, n)
    def _(d):
        slot = lax.rem(s + d, n)
        stem_rows(slot)
        keep_stems(slot)

    weight_copies[1].wait()

    row = lax.broadcasted_iota(jnp.int32, (TILE, 1), 0)
    inside = (
        jnp.logical_or(row < SIDE, s > 0),
        jnp.logical_or(row >= SIDE, s < n - 1),
    )

    def enc_rows(h, at):
        total = enc[h].total(at)
        square = total * total
        inner = jnp.tanh(SQRT_TWO_PI * (total + CUBIC * square * total))
        active = (0.5 * total * (1.0 + inner)).astype(BF16).astype(F32)
        pooled = (0.5 * (active[0] + active[1])).astype(BF16).astype(F32)
        pool_wide[pl.ds(pl.multiple_of(at.start + SIDE, SIDE), TILE), :] = pooled
        bend[h, :, at, :] = 0.5 * (
            0.5 * (1.0 + inner)
            + 0.5 * total * (1.0 - inner * inner) * SQRT_TWO_PI * (1.0 + 3.0 * CUBIC * square)
        )

    def conv_block(h, j):
        at = pl.ds(pl.multiple_of(j * c1, TILE), c1)
        before, here, after = (pool_near[:, i * c2 : (i + 1) * c2] for i in range(3))
        shared = by_channels(before, w_ref[0, at, :]) + by_channels(here, w_ref[2, at, :])
        shared = shared + by_channels(after, w_ref[4, at, :])
        single = by_channels(before, w_ref[1, at, :]) + by_channels(here, w_ref[3, at, :])
        q_wide[0:rows, :] = single
        q_wide[rows:, :] = single[0:SIDE]
        dec_part[h, j, 0, :, :] = (shared + single).astype(BF16)
        dec_part[h, j, 1, :, :] = (shared + q_wide[1 : rows + 1, :]).astype(BF16)

    def encode(h):
        for q in range(len(enc_chunks)):
            enc[h].arrive(q)
            tiles(*enc_chunks[q], functools.partial(enc_rows, h))
        halo = pool_wide[SIDE : SIDE + TILE, :]
        pool_wide[SIDE : SIDE + TILE, :] = jnp.where(inside[h], halo, 0.0)
        pool_wide[0:SIDE, :] = pool_wide[rows : rows + SIDE, :]
        pool_wide[rows + SIDE :, :] = pool_wide[SIDE : 2 * SIDE, :]
        for first in range(0, rows, TILE):
            for shift in range(3):
                value = pool_wide[first + SIDE - 1 + shift : first + SIDE - 1 + shift + TILE, :]
                pool_near[first : first + TILE, shift * c2 : (shift + 1) * c2] = value.astype(BF16)
        conv_block(h, far)
        dec[h].start(1)
        pools[s, h * own : (h + 1) * own, :] = pool_near[TILE:, c2 : 2 * c2]
        relay[h].start()
        conv_block(h, across)
        dec[h].cross(0)
        conv_block(h, mate)
        dec[h].start(0)
        conv_block(h, c)

    def slope_tile(h, at, target, keep=None):
        output = dec[h].total(at) + near[h, 2:4, at, :].astype(F32)
        value = (output - target) * scale
        if keep is None:
            own_at = pl.ds(pl.multiple_of(at.start - TILE + h * own, TILE), TILE)
            pred_pair[:, own_at, :] = output.astype(BF16)
        else:
            value = jnp.where(keep[None], value, 0.0)
        slope[:, at, :] = value

    def slope_rows(h, at):
        own_at = pl.ds(pl.multiple_of(at.start - TILE + h * own, TILE), TILE)
        slope_tile(h, at, target_ref[:, own_at, :].astype(F32))

    def row_copy(h, kind, owner, to):
        spot = chan.at[h, owner]
        return send(spot, spot, row_send.at[h * 3 + kind], row_recv.at[h * 3 + kind], s, to)

    def decode(h):
        dec[h].arrive(0)
        high = target_ref[:, own : own + TILE, :] if h == 0 else edge[1]
        low = edge[0] if h == 0 else target_ref[:, own - TILE : own, :]
        target = jnp.where(row[None] < SIDE, high.astype(F32), low.astype(F32))
        slope_tile(h, pl.ds(0, TILE), target, inside[h])
        slope[:, rows:, :] = slope[:, 0:SIDE, :]
        tiles(TILE, own, functools.partial(slope_rows, h))
        for start in range(0, rows, TILE):
            even = slope[0, start : start + TILE, :]
            odd = slope[1, start : start + TILE, :]
            following = slope[0, start + 1 : start + 1 + TILE, :]
            chan[h, c, 0, start : start + TILE, :] = (even + odd).astype(BF16)
            chan[h, c, 1, start : start + TILE, :] = (odd + following).astype(BF16)
        row_copy(h, 1, c, across).start()
        row_copy(h, 0, c, mate).start()

    def up_block(h, j, first):
        at = pl.ds(pl.multiple_of(j * c1, TILE), c1)
        for place, terms in enumerate((((0, 0),), ((1, 1), (0, 2)), ((1, 3), (0, 4)))):
            total = None
            for plane, k in terms:
                term = jnp.dot(chan[h, j, plane], w_ref[k, at, :], preferred_element_type=F32)
                total = term if total is None else total + term
            if not first:
                total = total + up[place, SIDE : SIDE + rows, :]
            up[place, SIDE : SIDE + rows, :] = total

    def bend_back(h):
        up[0, SIDE + rows :, :] = up[0, SIDE : 2 * SIDE, :]
        for first in range(0, own, TILE):
            spot = first + TILE + SIDE
            grad = (
                up[0, spot + 1 : spot + 1 + TILE, :]
                + up[1, spot : spot + TILE, :]
                + up[2, spot - 1 : spot - 1 + TILE, :]
            )
            pre_own[h, :, first : first + TILE, :] = (
                grad[None] * bend[h, :, first + TILE : first + 2 * TILE, :]
            ).astype(BF16)
        turn[h].cross().start()
        turn[h].start(0)

    def near_grad(h):
        if h == 0:
            slopes[h].start(c)
        up_block(h, c, True)
        row_copy(h, 0, mate, mate).wait_recv()
        if h == 0:
            slopes[h].start(mate)
        up_block(h, mate, False)

    def across_grad(h):
        row_copy(h, 1, across, across).wait_recv()
        row_copy(h, 2, across, mate).start()
        up_block(h, across, False)

    def far_grad(h):
        row_copy(h, 2, far, mate).wait_recv()
        up_block(h, far, False)
        bend_back(h)

    def pass_on(h):
        turn[h].cross().wait_recv()
        turn[h].start(1)

    def turn_slopes(h):
        for block in (across, far) if h == 0 else (c, mate, across, far):
            slopes[h].start(block)
        slopes[h].keep().start()

    def decoder_grad(slot):
        for h in both_halves:
            for plane in range(2):
                value = ab_seq[h, slot, plane].astype(F32)
                ab_wide[plane, 0:rows, :] = value
                ab_wide[plane, rows:, :] = value[0:SIDE]
            for k, (plane, shift) in enumerate(((0, 1), (1, 0), (0, 0), (1, -1), (0, -1))):
                ab_near[k, h * own : (h + 1) * own, :] = ab_wide[
                    plane, TILE + shift : rows + shift, :
                ].astype(BF16)
        for k in range(KW):
            g_dec_ref[k, :, :] += across_rows(ab_near[k], pools[slot])

    def encoder_grad(slot):
        at = pl.ds(pl.multiple_of(slot * pairs, TILE), pairs)
        for k in range(KW):
            g_enc_ref[k, :, :] += across_rows(stems[k, at, :], pre_seq[slot, 0]) + across_rows(
                stems[k + 1, at, :], pre_seq[slot, 1]
            )

    encode(0)
    encode(1)
    for copy in edges:
        copy.wait()
    decode(0)
    relay[0].arrive(1)
    near_grad(0)
    decode(1)
    relay[1].arrive(1)
    across_grad(0)
    far_grad(0)
    turn_slopes(0)
    relay[0].arrive(2)
    near_grad(1)
    across_grad(1)
    pass_on(0)
    far_grad(1)
    g_enc_ref[...] = jnp.zeros_like(g_enc_ref)
    g_dec_ref[...] = jnp.zeros_like(g_dec_ref)
    merged = across_rows(pred_pair[0], split[0:pairs, :])
    pred_ref[...] = (merged + across_rows(pred_pair[1], split[pairs:, :])).astype(BF16)
    relay[1].arrive(2)
    pass_on(1)
    turn_slopes(1)
    for h in both_halves:
        slopes[h].keep().wait()
    decoder_grad(s)
    for i in range(n):
        turn[0].forward(slots[i], i == 0)
    relay[0].arrive(3)
    for slot in slots[1:]:
        slopes[0].forward(slot)
    for i in range(n):
        turn[1].forward(slots[i], i == 0)
        turn[0].relay(slots[i])
    for slot in slots[1:]:
        slopes[0].relay(slot)
    relay[1].arrive(3)
    for i in range(n):
        turn[1].relay(slots[i])
        if i:
            slopes[1].forward(slots[i])
            for h in both_halves:
                turn[h].finish(slots[i - 1])
            encoder_grad(slots[i - 1])
    for slot in slots[1:]:
        slopes[1].relay(slot)
    for h in both_halves:
        turn[h].finish(slots[n - 1])
    encoder_grad(slots[n - 1])
    for slot in slots[1:]:
        for h in both_halves:
            slopes[h].finish(slot)
        decoder_grad(slot)

    for h in both_halves:
        enc[h].end()
        dec[h].end()
        row_copy(h, 0, c, mate).wait_send()
        row_copy(h, 1, c, across).wait_send()
        row_copy(h, 2, across, mate).wait_send()
        relay[h].end()
        slopes[h].end(slots[1:])
        turn[h].end()


def store_kernel(*refs):
    count = (len(refs) - 1) // 2
    sems = refs[-1]
    copies = []
    for source, target in zip(refs[:count], refs[count:-1]):
        parts = source.shape[0] if len(source.shape) == 3 else 1
        for i in range(parts):
            pair = (source.at[i], target.at[i]) if len(source.shape) == 3 else (source, target)
            copies.append(pltpu.make_async_copy(*pair, sems.at[len(copies)]))
    for copy in copies:
        copy.start()
    for copy in copies:
        copy.wait()


def store(*values):
    return pl.pallas_call(
        store_kernel,
        out_shape=tuple(jax.ShapeDtypeStruct(value.shape, value.dtype) for value in values),
        in_specs=[pl.BlockSpec(memory_space=pl.ANY)] * len(values),
        out_specs=(pl.BlockSpec(memory_space=pltpu.HBM),) * len(values),
        scratch_shapes=[dma(2 * KW + len(values))],
        compiler_params=pltpu.CompilerParams(vmem_limit_bytes=1024 * 1024),
    )(*values)


def dma(count):
    return pltpu.SemaphoreType.DMA((count,))


def square_shards(dna_bases, w_stem, w_enc, w_dec, targets):
    rows = dna_bases.shape[0]
    n = lax.axis_size("seq")
    half = rows // 2
    length, pairs = rows * n, half * n
    own = half // HALVES
    held = own + TILE
    c1, c2 = w_stem.shape[0], w_dec.shape[2]
    c1_wide = (c1 + 127) // 128 * 128
    struct = jax.ShapeDtypeStruct

    cut = held // TILE // 2 * TILE
    enc_chunks = ((0, cut), (cut, held - cut))
    wide = held + SIDE
    double = HALVES * n
    counts = HALVES * 3 * len(enc_chunks)
    vmem = pl.BlockSpec(memory_space=pltpu.VMEM)
    anywhere = pl.BlockSpec(memory_space=pl.ANY)
    pred, g_enc, g_dec = pl.pallas_call(
        functools.partial(train_kernel, n, 1.0 / math.sqrt(length), enc_chunks),
        out_shape=(
            struct((c1, rows), BF16),
            struct((KW, c1, c2), F32),
            struct((KW, c1, c2), F32),
        ),
        in_specs=[anywhere] * 5,
        out_specs=(vmem, vmem, vmem),
        scratch_shapes=[
            pltpu.VMEM((KW, 4, c1), BF16),
            pltpu.VMEM((KW * SIDE, c1_wide), F32),
            pltpu.VMEM((c1, rows), BF16),
            pltpu.VMEM((n, rows // 128, 128), jnp.int32),
            pltpu.VMEM((c1_wide // 128, rows + 2 * RIM, 128), F32),
            pltpu.VMEM((HALVES, 6, held, c1), BF16),
            pltpu.VMEM((KW, c1, n * c2), BF16),
            pltpu.VMEM((KW, n * c1, c2), BF16),
            pltpu.VMEM((HALVES, 2, held, n * c2), BF16),
            pltpu.VMEM((2, half, c1), BF16),
            pltpu.VMEM((2, half, c1), BF16),
            pltpu.VMEM((rows, rows), BF16),
            pltpu.VMEM((HALVES, 3, 2, held, c2), BF16),
            pltpu.VMEM((HALVES, 2, held, c2), BF16),
            pltpu.VMEM((HALVES, 2, held, c2), F32),
            pltpu.VMEM((held + 2 * SIDE, c2), F32),
            pltpu.VMEM((held, 3 * c2), BF16),
            pltpu.VMEM((HALVES, n, 2, held, c1), BF16),
            pltpu.VMEM((HALVES, 3, 2, held, c1), BF16),
            pltpu.VMEM((HALVES, 2, held, c1), BF16),
            pltpu.VMEM((wide, c1), F32),
            pltpu.VMEM((2, 2, TILE, c1), BF16),
            pltpu.VMEM((2, wide, c1), F32),
            pltpu.VMEM((HALVES, n, 2, held, c1), BF16),
            pltpu.VMEM((3, held + 2 * SIDE, c2), F32),
            pltpu.VMEM((HALVES, 2, own, c2), BF16),
            pltpu.VMEM((HALVES, 2, own // 2, c2), BF16),
            pltpu.VMEM((n, 2, half, c2), BF16),
            pltpu.VMEM((HALVES, n, 2, held, c1), BF16),
            pltpu.VMEM((2, wide, c1), F32),
            pltpu.VMEM((KW, half, c1), BF16),
            pltpu.VMEM((n, half, c2), BF16),
            pltpu.VMEM((6, pairs, c1), BF16),
            dma(counts), dma(counts), dma(HALVES * 3), dma(HALVES * 3), dma(2), dma(2),
            dma(HALVES * 3), dma(HALVES * 3), dma(double), dma(double), dma(double),
            dma(n - 1), dma(n - 1), dma(5),
            dma(HALVES), dma(HALVES), dma(double), dma(double), dma(3 * double), dma(3 * double),
            dma(HALVES),
            dma(double), dma(double), dma(double), dma(double), dma(2 * double), dma(2 * double),
            dma(HALVES),
        ],
        compiler_params=pltpu.CompilerParams(
            collective_id=0, has_side_effects=True, vmem_limit_bytes=VMEM_BYTES
        ),
    )(
        dna_bases.reshape(rows // 128, 128),
        w_stem.transpose(1, 2, 0),
        targets.T,
        w_enc.transpose(1, 2, 0),
        w_dec.transpose(1, 0, 2),
    )
    pred, g_enc, g_dec = store(pred, g_enc, g_dec)
    return (pred.T, g_enc.transpose(2, 0, 1), g_dec.transpose(1, 0, 2))


def shards(dna_bases, w_stem, w_enc, w_dec, targets):
    args = (dna_bases, w_stem, w_enc, w_dec, targets)
    rows, c1, c2 = dna_bases.shape[0], w_stem.shape[0], w_dec.shape[2]
    n = lax.axis_size("seq")
    square = n == 4 and lax.axis_size("chan") == 4
    if square and rows % 512 == 0 and c2 % 128 == 0 and c1 % 64 == 0:
        return square_shards(*args)
    return general_shards(*args)


def solution(mesh):
    return jax.shard_map(
        shards,
        mesh=mesh,
        in_specs=(
            P(("groups", "seq")),
            P("chan", None, None),
            P(None, None, "chan"),
            P(None, None, "chan"),
            P(("groups", "seq"), "chan"),
        ),
        out_specs=(
            P(("groups", "seq"), "chan"),
            P(("groups", "seq"), None, "chan"),
            P(("groups", "seq"), None, "chan"),
        ),
        check_vma=False,
    )
```

```python
import functools
import math

import jax
import jax.numpy as jnp
from jax import lax
from jax.experimental import pallas as pl
from jax.experimental.pallas import tpu as pltpu
from jax.sharding import PartitionSpec as P

KW = 5


SQRT_TWO_PI = 0.7978845608028654
CUBIC = 0.044715


def extended(block, sides, width):
    for axis, dim in sides:
        count = lax.axis_size(axis)
        forward = [(i, i + 1) for i in range(count - 1)]
        backward = [(target, source) for source, target in forward]
        low = lax.ppermute(
            lax.slice_in_dim(block, block.shape[dim] - width, None, axis=dim), axis, forward
        )
        high = lax.ppermute(lax.slice_in_dim(block, 0, width, axis=dim), axis, backward)
        block = jnp.concatenate([low, block, high], axis=dim)
    return block


def gelu_value(value):
    inner = jnp.tanh(SQRT_TWO_PI * (value + CUBIC * value * value * value))
    return 0.5 * value * (1.0 + inner)


def gelu_slope(value):
    inner = jnp.tanh(SQRT_TWO_PI * (value + CUBIC * value * value * value))
    return 0.5 * (1.0 + inner) + 0.5 * value * (1.0 - inner * inner) * SQRT_TWO_PI * (
        1.0 + 3.0 * CUBIC * value * value
    )


def rim_cells(block, margin):
    return extended(block, (("seq", 0),), margin)


def channel_sum(partial_value):
    return lax.psum_scatter(partial_value, "chan", scatter_dimension=1, tiled=True)


def channel_gather(block):
    return lax.all_gather(block, "chan", axis=1, tiled=True)


def conv_rows(padded, weight):
    row_count = padded.shape[0] - 4
    total = jnp.zeros((row_count, weight.shape[0]), jnp.float32)
    for k in range(KW):
        total = total + lax.dot_general(
            padded[k : k + row_count],
            weight[:, k, :],
            (((1,), (1,)), ((), ())),
            preferred_element_type=jnp.float32,
        )
    return total


def grad_taps(picked, padded):
    row_count = picked.shape[0]
    pieces = [
        lax.dot_general(
            picked,
            padded[k : k + row_count],
            (((0,), (0,)), ((), ())),
            preferred_element_type=jnp.float32,
        )
        for k in range(KW)
    ]
    return jnp.stack(pieces, axis=1)


def weight_grad(cotangent, padded):
    rounded = grad_taps(cotangent, padded).astype(jnp.bfloat16)
    return lax.psum_scatter(
        lax.optimization_barrier(rounded).astype(jnp.float32),
        "seq",
        scatter_dimension=0,
        tiled=True,
    )


def general_shards(dna_bases, w_stem, w_enc, w_dec, targets):
    row_count = dna_bases.shape[0]
    devices = lax.axis_size("seq")
    length = row_count * devices
    onehot = (dna_bases[:, None] == jnp.arange(4, dtype=jnp.int32)[None, :]).astype(jnp.bfloat16)
    onehot_pad = rim_cells(onehot, 2)
    stem_out = gelu_value(conv_rows(onehot_pad, w_stem)).astype(jnp.bfloat16)
    stem_pad = rim_cells(stem_out, 2)
    enc_pre = channel_sum(conv_rows(stem_pad, w_enc))
    active = gelu_value(enc_pre).astype(jnp.bfloat16).astype(jnp.float32)
    pooled = (0.5 * active.reshape(row_count // 2, 2, -1).sum(axis=1)).astype(jnp.bfloat16)
    pooled_pad = rim_cells(pooled, 1)
    up_pad = jnp.repeat(pooled_pad, 2, axis=0)
    output = channel_sum(conv_rows(up_pad, w_dec)) + stem_out.astype(jnp.float32)
    pred = output.astype(jnp.bfloat16)
    scale = 1.0 / math.sqrt(length)
    slope_out = ((output - targets.astype(jnp.float32)) * scale).astype(jnp.bfloat16)
    slope_all = channel_gather(slope_out)
    g_dec = weight_grad(slope_all, up_pad)
    slope_pad = rim_cells(slope_all, 2)
    up_grad = jnp.zeros((row_count, w_dec.shape[2]), jnp.float32)
    for k in range(KW):
        up_grad = up_grad + jnp.dot(
            slope_pad[4 - k : 4 - k + row_count], w_dec[:, k, :], preferred_element_type=jnp.float32
        )
    pool_grad = up_grad.reshape(row_count // 2, 2, -1).sum(axis=1)
    act_grad = 0.5 * jnp.repeat(pool_grad, 2, axis=0)
    pre_grad = (act_grad * gelu_slope(enc_pre)).astype(jnp.bfloat16)
    pre_all = channel_gather(pre_grad)
    g_enc = weight_grad(pre_all, stem_pad)
    return (pred, g_enc, g_dec)


MESH_ID = pl.DeviceIdType.MESH
BF16 = jnp.bfloat16
F32 = jnp.float32
TILE = 16
SIDE = 8
RIM = 32
HALVES = 2
VMEM_BYTES = 48 * 1024 * 1024


def send(src, dst, send_sem, recv_sem, seq, chan):
    return pltpu.make_async_remote_copy(
        src_ref=src,
        dst_ref=dst,
        send_sem=send_sem,
        recv_sem=recv_sem,
        device_id={"seq": seq, "chan": chan},
        device_id_type=MESH_ID,
    )


def greet(targets):
    barrier = pltpu.get_barrier_semaphore()
    for seq, chan in targets:
        pl.semaphore_signal(
            barrier, inc=1, device_id={"seq": seq, "chan": chan}, device_id_type=MESH_ID
        )
    pl.semaphore_wait(barrier, len(targets))


def partner_group(n, s, c):
    mate = partners(c)[0]
    others = [(s, lax.rem(c + d, n)) for d in range(1, n)]
    for d in range(1, n):
        others += [(lax.rem(s + d, n), c), (lax.rem(s + d, n), mate)]
    return others


def partners(c):
    mate = c + 1 - 2 * lax.rem(c, 2)
    across = lax.rem(c + 2, 4)
    return mate, across, lax.rem(mate + 2, 4)


def span(first, count):
    return pl.ds(first, count)


def tiles(first, count, body):
    @pl.loop(0, count // TILE)
    def _(i):
        body(pl.ds(pl.multiple_of(first + i * TILE, TILE), TILE))


class Part:
    def __init__(self, sem, base):
        self.sem, self.base = sem, base

    @property
    def at(self):
        return self

    def __getitem__(self, index):
        return self.sem.at[self.base + index]


class Turn:
    def __init__(self, n, s, c, h, own, mid, out, sems):
        self.n, self.s, self.c, self.h, self.own, self.mid, self.out = n, s, c, h, own, mid, out
        (self.cross_send, self.cross_recv, self.along_send, self.along_recv,
         self.share_send, self.share_recv, self.local) = sems
        self.count = own.shape[1]
        self.piece = self.count // n
        self.side = c // 2

    def out_rows(self, index):
        first = self.h * self.count + index * self.piece
        return pl.ds(pl.multiple_of(first, self.piece), self.piece)

    def cross(self):
        wide = 2 * self.piece
        at = pl.ds(pl.multiple_of((1 - self.side) * wide, wide), wide)
        return send(self.own.at[:, at], self.mid, self.cross_send.at[0], self.cross_recv.at[0],
                    self.s, partners(self.c)[1])

    def source(self, plane, q):
        if plane:
            first = (q - 2 * self.side) * self.piece
            return self.mid.at[:, pl.ds(pl.multiple_of(first, self.piece), self.piece)]
        return self.own.at[:, pl.ds(pl.multiple_of(q * self.piece, self.piece), self.piece)]

    def along(self, plane, kind, slot):
        mate, across, _ = partners(self.c)
        q = mate if kind else self.c
        return send(self.source(plane, q), self.out.at[self.s, :, self.out_rows(q)],
                    self.along_send.at[2 * plane + kind], self.along_recv.at[slot],
                    across if plane else self.c, q)

    def keep(self, plane):
        return pltpu.make_async_copy(
            self.source(plane, self.c), self.out.at[self.s, :, self.out_rows(self.c)], self.local
        )

    def home(self, plane):
        return self.s == (partners(self.c)[1] if plane else self.c)

    def start(self, plane):
        home = self.home(plane)
        pl.when(jnp.logical_not(home))(lambda: self.along(plane, 0, self.s).start())
        pl.when(home)(lambda: self.keep(plane).start())
        self.along(plane, 1, self.s).start()

    def share(self, slot, kind, part, to):
        spot = self.out.at[slot, :, self.out_rows(part)]
        index = slot * 3 + kind
        return send(spot, spot, self.share_send.at[index], self.share_recv.at[index], self.s, to)

    def forward(self, slot, mine):
        mate, across, _ = partners(self.c)
        if mine:
            pl.when(self.home(0))(lambda: self.keep(0).wait())
            pl.when(self.home(1))(lambda: self.keep(1).wait())
            other = jnp.logical_not(jnp.logical_or(self.home(0), self.home(1)))
            pl.when(other)(lambda: self.along(0, 0, slot).wait_recv())
        else:
            self.along(0, 0, slot).wait_recv()
        self.share(slot, 1, self.c, across).start()
        self.share(slot, 0, self.c, mate).start()

    def relay(self, slot):
        mate, across, _ = partners(self.c)
        self.share(slot, 1, across, across).wait_recv()
        self.share(slot, 2, across, mate).start()

    def finish(self, slot):
        mate, across, far = partners(self.c)
        self.share(slot, 0, mate, mate).wait_recv()
        self.share(slot, 2, far, mate).wait_recv()

    def end(self):
        mate, across, _ = partners(self.c)
        for slot in range(self.n):
            self.share(slot, 0, self.c, mate).wait_send()
            self.share(slot, 1, self.c, across).wait_send()
            self.share(slot, 2, across, mate).wait_send()
        self.cross().wait_send()
        for plane in range(2):
            pl.when(jnp.logical_not(self.home(plane)))(
                functools.partial(lambda plane: self.along(plane, 0, self.s).wait_send(), plane)
            )
            self.along(plane, 1, self.s).wait_send()


class PairSum:
    def __init__(self, block, held, pair, s, c, chunks, sems):
        self.block, self.held, self.pair, self.s, self.c = block, held, pair, s, c
        self.chunks = chunks
        self.send_sem, self.recv_sem = sems

    def hop(self, kind, q):
        mate, across, far = partners(self.c)
        source = (lambda: self.block(mate), lambda: self.block(far), lambda: self.pair)[kind]()
        target = (mate, mate, across)[kind]
        at = span(*self.chunks[q])
        index = kind * len(self.chunks) + q
        return send(source.at[:, at], self.held.at[kind, :, at], self.send_sem.at[index],
                    self.recv_sem.at[index], self.s, target)

    def start(self, kind):
        for q in range(len(self.chunks)):
            self.hop(kind, q).start()

    def cross(self, q):
        _, across, _ = partners(self.c)
        self.hop(1, q).wait_recv()
        block = self.block(across)

        def body(at):
            self.pair[:, at, :] = (
                block[:, at, :].astype(F32) + self.held[1, :, at, :].astype(F32)
            ).astype(BF16)

        tiles(*self.chunks[q], body)
        self.hop(2, q).start()

    def arrive(self, q):
        self.hop(0, q).wait_recv()
        self.hop(2, q).wait_recv()

    def total(self, at):
        mine = self.block(self.c)[:, at, :].astype(F32)
        return mine + self.held[0, :, at, :].astype(F32) + self.held[2, :, at, :].astype(F32)

    def end(self):
        for kind in range(3):
            for q in range(len(self.chunks)):
                self.hop(kind, q).wait_send()


class PoolRelay:
    def __init__(self, n, s, c, h, out, right_send, left_send, recv):
        self.n, self.s, self.c, self.out = n, s, c, out
        self.right_send, self.left_send, self.recv = right_send, left_send, recv
        self.at = span(h * (out.shape[1] // HALVES), out.shape[1] // HALVES)

    def hop(self, slot, step):
        sems = self.right_send if step > 0 else self.left_send
        spot = self.out.at[slot, self.at]
        return send(spot, spot, sems.at[slot], self.recv.at[slot], self.s + step, self.c)

    def start(self):
        pl.when(self.s < self.n - 1)(lambda: self.hop(self.s, 1).start())
        pl.when(self.s > 0)(lambda: self.hop(self.s, -1).start())

    def arrive(self, d):
        low, high = self.s - d, self.s + d

        @pl.when(low >= 0)
        def _():
            self.hop(low, 1).wait_recv()
            pl.when(self.s < self.n - 1)(lambda: self.hop(low, 1).start())

        @pl.when(high < self.n)
        def _():
            self.hop(high, -1).wait_recv()
            pl.when(self.s > 0)(lambda: self.hop(high, -1).start())

    def end(self):
        for slot in range(self.n):
            pl.when(jnp.logical_and(slot <= self.s, self.s < self.n - 1))(
                functools.partial(lambda slot: self.hop(slot, 1).wait_send(), slot)
            )
            pl.when(jnp.logical_and(slot >= self.s, self.s > 0))(
                functools.partial(lambda slot: self.hop(slot, -1).wait_send(), slot)
            )


class SlopeTurn:
    def __init__(self, n, s, c, chan, out, sems):
        self.n, self.s, self.c, self.chan, self.out = n, s, c, chan, out
        (self.send_sem, self.recv_sem, self.cross_send, self.cross_recv,
         self.share_send, self.share_recv, self.local) = sems
        self.plane = c // 2
        self.hub = lax.rem(s, 2) == lax.rem(c, 2)

    def hop(self, to, slot):
        return send(self.chan.at[to, self.plane], self.out.at[self.s, self.plane],
                    self.send_sem.at[to], self.recv_sem.at[slot], to, self.c)

    def mine(self, block):
        return jnp.logical_and(block != self.s, lax.rem(block, 2) == lax.rem(self.c, 2))

    def start(self, block):
        pl.when(self.mine(block))(lambda: self.hop(block, self.s).start())

    def keep(self):
        return pltpu.make_async_copy(self.chan.at[self.s], self.out.at[self.s], self.local)

    def cross(self, slot, plane):
        spot = self.out.at[slot, plane]
        return send(spot, spot, self.cross_send.at[slot], self.cross_recv.at[slot], self.s,
                    partners(self.c)[1])

    def share(self, slot, plane):
        spot = self.out.at[slot, plane]
        return send(spot, spot, self.share_send.at[2 * slot + plane],
                    self.share_recv.at[2 * slot + plane], self.s, partners(self.c)[0])

    def forward(self, slot):
        @pl.when(self.hub)
        def _():
            self.hop(self.s, slot).wait_recv()
            self.cross(slot, self.plane).start()
            self.share(slot, self.plane).start()

    def relay(self, slot):
        @pl.when(self.hub)
        def _():
            self.cross(slot, 1 - self.plane).wait_recv()
            self.share(slot, 1 - self.plane).start()

    def finish(self, slot):
        @pl.when(jnp.logical_not(self.hub))
        def _():
            for plane in range(2):
                self.share(slot, plane).wait_recv()

    def end(self, others):
        for slot in others:
            pl.when(self.mine(slot))(
                functools.partial(lambda slot: self.hop(slot, self.s).wait_send(), slot)
            )

        @pl.when(self.hub)
        def _():
            for slot in others:
                self.cross(slot, self.plane).wait_send()
                for plane in range(2):
                    self.share(slot, plane).wait_send()


def across_rows(left, right):
    return lax.dot_general(left, right, (((0,), (0,)), ((), ())), preferred_element_type=F32)


def by_channels(left, right):
    return lax.dot_general(left, right, (((1,), (1,)), ((), ())), preferred_element_type=F32)


def train_kernel(
    n, scale, enc_chunks, bases_ref, w_stem_hbm, target_hbm, w_enc_ref, w_dec_ref,
    pred_ref, g_enc_ref, g_dec_ref,
    w_stem_small, w_stem_ref, target_in, bases, natural, near, w_enc, w_ref, part, target_ref, pred_pair, split,
    enc_held, enc_pair, bend, pool_wide, pool_near, dec_part, dec_held, dec_pair, q_wide,
    edge, slope, chan, up, pre_own, pre_mid, pre_seq, ab_seq, ab_wide, ab_near, pools, stems,
    enc_send, enc_recv, dec_send, dec_recv, edge_send, edge_recv, row_send, row_recv,
    right_send, left_send, pool_recv, bases_send, bases_recv, local_sem, *turn_sems,
):
    s, c = lax.axis_index("seq"), lax.axis_index("chan")
    mate, across, far = partners(c)
    rows, c2 = pool_near.shape[0], pool_wide.shape[1]
    own = rows - TILE
    pairs = HALVES * own
    c1 = near.shape[3]
    upper = s // 2
    slots = (s, 1 - s + 4 * upper, 2 - upper, 3 - 3 * upper)
    both_halves = range(HALVES)
    weight_copies = [
        pltpu.make_async_copy(w_enc_ref, w_enc, local_sem.at[0]),
        pltpu.make_async_copy(w_dec_ref, w_ref, local_sem.at[1]),
    ]
    small_copies = [
        pltpu.make_async_copy(bases_ref, bases.at[s], local_sem.at[2]),
        pltpu.make_async_copy(w_stem_hbm, w_stem_small, local_sem.at[3]),
        pltpu.make_async_copy(target_hbm, target_in, local_sem.at[4]),
    ]
    for copy in small_copies[:2] + weight_copies[:1] + small_copies[2:] + weight_copies[1:]:
        copy.start()
    greet(partner_group(n, s, c))
    small_copies[0].wait()
    base_copies = [
        send(bases.at[s], bases.at[s], bases_send.at[d - 1], bases_recv.at[d - 1],
             lax.rem(s + d, n), c)
        for d in range(1, n)
    ]
    for copy in base_copies:
        copy.start()

    def column_block(h, j):
        return part.at[h, :, :, pl.ds(pl.multiple_of(j * c2, 128), c2)]

    counts = 3 * len(enc_chunks)
    enc = [
        PairSum(functools.partial(column_block, h), enc_held.at[h], enc_pair.at[h], s, c,
                enc_chunks, (Part(enc_send, h * counts), Part(enc_recv, h * counts)))
        for h in both_halves
    ]
    dec = [
        PairSum(functools.partial(lambda h, j: dec_part.at[h, j], h), dec_held.at[h],
                dec_pair.at[h], s, c, ((0, rows),), (Part(dec_send, h * 3), Part(dec_recv, h * 3)))
        for h in both_halves
    ]
    relay = [
        PoolRelay(n, s, c, h, pools, *[Part(sem, h * n) for sem in (right_send, left_send, pool_recv)])
        for h in both_halves
    ]
    turn = [
        Turn(n, s, c, h, pre_own.at[h], pre_mid.at[h], pre_seq,
             [Part(sem, h * size) for sem, size in zip(turn_sems[:6], (1, 1, n, n, 3 * n, 3 * n))]
             + [turn_sems[6].at[h]])
        for h in both_halves
    ]
    slopes = [
        SlopeTurn(n, s, c, chan.at[h], ab_seq.at[h],
                  [Part(sem, h * n) for sem in turn_sems[7:11]]
                  + [Part(sem, 2 * h * n) for sem in turn_sems[11:13]] + [turn_sems[13].at[h]])
        for h in both_halves
    ]

    def stem_rows(slot):
        before = bases[lax.rem(slot + n - 1, n)]
        here = bases[slot]
        after = bases[lax.rem(slot + 1, n)]
        count = here.shape[0]
        lanes = [jnp.where(slot > 0, before[count - 1 :], -1)]
        lanes += [here[i : i + 1] for i in range(count)]
        lanes += [jnp.where(slot < n - 1, after[:1], -1)]
        line = jnp.concatenate(lanes, axis=1)
        total = line.shape[1]
        line = jnp.broadcast_to(line, (SIDE, total))
        kind = lax.broadcasted_iota(jnp.int32, (SIDE, total), 0)
        onehot = jnp.concatenate(
            [
                jnp.where(pltpu.roll(line, (2 - k) % total, 1) == kind, 1.0, 0.0)
                for k in range(KW)
            ],
            axis=0,
        ).astype(BF16)
        for i in range(count + 2):
            value = across_rows(onehot[:, i * 128 : (i + 1) * 128], w_stem_ref[...].astype(BF16))
            first = 128 * (i - 1) + RIM
            if i == 0:
                first, value = 0, jnp.where(slot > 0, value[128 - RIM :], 0.0)
            if i == count + 1:
                value = jnp.where(slot < n - 1, value[:RIM], 0.0)
            value = gelu_value(value)
            for t in range(natural.shape[0]):
                natural[t, first : first + value.shape[0], :] = value[:, t * 128 : (t + 1) * 128]

    def every_other(t, first, count):
        return natural[t, pl.ds(first, count, stride=2), : min(128, c1 - t * 128)]

    def piece_start(i):
        return RIM + i % 2 + 2 * (i // 2 - 1)

    def lane_span(t):
        return slice(t * 128, min(c1, (t + 1) * 128))

    def near_rows():
        for h in both_halves:
            for i in range(6):
                first = piece_start(i) + 2 * own * h
                for t in range(natural.shape[0]):
                    halo = [every_other(t, first + 2 * own, SIDE), every_other(t, first - 2 * SIDE, SIDE)]
                    near[h, i, 0:TILE, lane_span(t)] = jnp.concatenate(halo, axis=0).astype(BF16)
                    near[h, i, TILE:, lane_span(t)] = every_other(t, first, own).astype(BF16)

    def keep_stems(slot):
        at = pl.ds(pl.multiple_of(slot * pairs, TILE), pairs)
        for i in range(6):
            for t in range(natural.shape[0]):
                stems[i, at, lane_span(t)] = every_other(t, piece_start(i), pairs).astype(BF16)

    def part_block(h, j):
        at = pl.ds(pl.multiple_of(j * c2, 128), c2)
        total = None
        for k in range(KW):
            window = near[h, k : k + 2].reshape(2 * rows, c1)
            term = jnp.dot(window, w_enc[k, :, at], preferred_element_type=F32)
            total = term if total is None else total + term
        part[h, :, :, at] = total.astype(BF16).reshape(2, rows, c2)

    edges = [
        send(target_ref.at[:, pl.ds(pairs - TILE, TILE)], edge.at[0], edge_send.at[0],
             edge_recv.at[0], lax.rem(s + 1, n), c),
        send(target_ref.at[:, pl.ds(0, TILE)], edge.at[1], edge_send.at[1], edge_recv.at[1],
             lax.rem(s + n - 1, n), c),
    ]

    def pair_targets():
        size = 2 * pairs
        for first in range(0, size, 128):
            place = lax.broadcasted_iota(jnp.int32, (128, size), 0) + first % pairs
            wanted = 2 * place + first // pairs
            column = lax.broadcasted_iota(jnp.int32, (128, size), 1)
            split[first : first + 128, :] = jnp.where(column == wanted, 1.0, 0.0).astype(BF16)
        for parity in range(2):
            value = by_channels(split[parity * pairs : (parity + 1) * pairs, :], target_in[...])
            target_ref[parity, :, :] = value.astype(BF16)

    small_copies[1].wait()
    w_stem_ref[...] = jnp.zeros_like(w_stem_ref)
    for k in range(KW):
        w_stem_ref[k * SIDE : k * SIDE + 4, 0:c1] = w_stem_small[k].astype(F32)
    for copy in base_copies:
        copy.wait()
    stem_rows(s)
    near_rows()
    weight_copies[0].wait()
    part_block(0, far)
    enc[0].start(1)
    part_block(0, across)
    part_block(1, far)
    enc[1].start(1)
    for q in range(len(enc_chunks)):
        enc[0].cross(q)
    part_block(1, across)
    for q in range(len(enc_chunks)):
        enc[1].cross(q)
    for h in both_halves:
        part_block(h, mate)
        enc[h].start(0)
        part_block(h, c)
    small_copies[2].wait()
    pair_targets()
    for copy in edges:
        copy.start()
    keep_stems(s)

    @pl.loop(1, n)
    def _(d):
        slot = lax.rem(s + d, n)
        stem_rows(slot)
        keep_stems(slot)

    weight_copies[1].wait()

    row = lax.broadcasted_iota(jnp.int32, (TILE, 1), 0)
    inside = (
        jnp.logical_or(row < SIDE, s > 0),
        jnp.logical_or(row >= SIDE, s < n - 1),
    )

    def enc_rows(h, at):
        total = enc[h].total(at)
        square = total * total
        inner = jnp.tanh(SQRT_TWO_PI * (total + CUBIC * square * total))
        active = (0.5 * total * (1.0 + inner)).astype(BF16).astype(F32)
        pooled = (0.5 * (active[0] + active[1])).astype(BF16).astype(F32)
        pool_wide[pl.ds(pl.multiple_of(at.start + SIDE, SIDE), TILE), :] = pooled
        bend[h, :, at, :] = 0.5 * (
            0.5 * (1.0 + inner)
            + 0.5 * total * (1.0 - inner * inner) * SQRT_TWO_PI * (1.0 + 3.0 * CUBIC * square)
        )

    def conv_block(h, j):
        at = pl.ds(pl.multiple_of(j * c1, TILE), c1)
        before, here, after = (pool_near[:, i * c2 : (i + 1) * c2] for i in range(3))
        shared = by_channels(before, w_ref[0, at, :]) + by_channels(here, w_ref[2, at, :])
        shared = shared + by_channels(after, w_ref[4, at, :])
        single = by_channels(before, w_ref[1, at, :]) + by_channels(here, w_ref[3, at, :])
        q_wide[0:rows, :] = single
        q_wide[rows:, :] = single[0:SIDE]
        dec_part[h, j, 0, :, :] = (shared + single).astype(BF16)
        dec_part[h, j, 1, :, :] = (shared + q_wide[1 : rows + 1, :]).astype(BF16)

    def encode(h):
        for q in range(len(enc_chunks)):
            enc[h].arrive(q)
            tiles(*enc_chunks[q], functools.partial(enc_rows, h))
        halo = pool_wide[SIDE : SIDE + TILE, :]
        pool_wide[SIDE : SIDE + TILE, :] = jnp.where(inside[h], halo, 0.0)
        pool_wide[0:SIDE, :] = pool_wide[rows : rows + SIDE, :]
        pool_wide[rows + SIDE :, :] = pool_wide[SIDE : 2 * SIDE, :]
        for first in range(0, rows, TILE):
            for shift in range(3):
                value = pool_wide[first + SIDE - 1 + shift : first + SIDE - 1 + shift + TILE, :]
                pool_near[first : first + TILE, shift * c2 : (shift + 1) * c2] = value.astype(BF16)
        conv_block(h, far)
        dec[h].start(1)
        pools[s, h * own : (h + 1) * own, :] = pool_near[TILE:, c2 : 2 * c2]
        relay[h].start()
        conv_block(h, across)
        dec[h].cross(0)
        conv_block(h, mate)
        dec[h].start(0)
        conv_block(h, c)

    def slope_tile(h, at, target, keep=None):
        output = dec[h].total(at) + near[h, 2:4, at, :].astype(F32)
        value = (output - target) * scale
        if keep is None:
            own_at = pl.ds(pl.multiple_of(at.start - TILE + h * own, TILE), TILE)
            pred_pair[:, own_at, :] = output.astype(BF16)
        else:
            value = jnp.where(keep[None], value, 0.0)
        slope[:, at, :] = value

    def slope_rows(h, at):
        own_at = pl.ds(pl.multiple_of(at.start - TILE + h * own, TILE), TILE)
        slope_tile(h, at, target_ref[:, own_at, :].astype(F32))

    def row_copy(h, kind, owner, to):
        spot = chan.at[h, owner]
        return send(spot, spot, row_send.at[h * 3 + kind], row_recv.at[h * 3 + kind], s, to)

    def decode(h):
        dec[h].arrive(0)
        high = target_ref[:, own : own + TILE, :] if h == 0 else edge[1]
        low = edge[0] if h == 0 else target_ref[:, own - TILE : own, :]
        target = jnp.where(row[None] < SIDE, high.astype(F32), low.astype(F32))
        slope_tile(h, pl.ds(0, TILE), target, inside[h])
        slope[:, rows:, :] = slope[:, 0:SIDE, :]
        tiles(TILE, own, functools.partial(slope_rows, h))
        for start in range(0, rows, TILE):
            even = slope[0, start : start + TILE, :]
            odd = slope[1, start : start + TILE, :]
            following = slope[0, start + 1 : start + 1 + TILE, :]
            chan[h, c, 0, start : start + TILE, :] = (even + odd).astype(BF16)
            chan[h, c, 1, start : start + TILE, :] = (odd + following).astype(BF16)
        row_copy(h, 1, c, across).start()
        row_copy(h, 0, c, mate).start()

    def up_block(h, j, first):
        at = pl.ds(pl.multiple_of(j * c1, TILE), c1)
        for place, terms in enumerate((((0, 0),), ((1, 1), (0, 2)), ((1, 3), (0, 4)))):
            total = None
            for plane, k in terms:
                term = jnp.dot(chan[h, j, plane], w_ref[k, at, :], preferred_element_type=F32)
                total = term if total is None else total + term
            if not first:
                total = total + up[place, SIDE : SIDE + rows, :]
            up[place, SIDE : SIDE + rows, :] = total

    def bend_back(h):
        up[0, SIDE + rows :, :] = up[0, SIDE : 2 * SIDE, :]
        for first in range(0, own, TILE):
            spot = first + TILE + SIDE
            grad = (
                up[0, spot + 1 : spot + 1 + TILE, :]
                + up[1, spot : spot + TILE, :]
                + up[2, spot - 1 : spot - 1 + TILE, :]
            )
            pre_own[h, :, first : first + TILE, :] = (
                grad[None] * bend[h, :, first + TILE : first + 2 * TILE, :]
            ).astype(BF16)
        turn[h].cross().start()
        turn[h].start(0)

    def near_grad(h):
        if h == 0:
            slopes[h].start(c)
        up_block(h, c, True)
        row_copy(h, 0, mate, mate).wait_recv()
        if h == 0:
            slopes[h].start(mate)
        up_block(h, mate, False)

    def across_grad(h):
        row_copy(h, 1, across, across).wait_recv()
        row_copy(h, 2, across, mate).start()
        up_block(h, across, False)

    def far_grad(h):
        row_copy(h, 2, far, mate).wait_recv()
        up_block(h, far, False)
        bend_back(h)

    def pass_on(h):
        turn[h].cross().wait_recv()
        turn[h].start(1)

    def turn_slopes(h):
        for block in (across, far) if h == 0 else (c, mate, across, far):
            slopes[h].start(block)
        slopes[h].keep().start()

    def decoder_grad(slot):
        for h in both_halves:
            for plane in range(2):
                value = ab_seq[h, slot, plane].astype(F32)
                ab_wide[plane, 0:rows, :] = value
                ab_wide[plane, rows:, :] = value[0:SIDE]
            for k, (plane, shift) in enumerate(((0, 1), (1, 0), (0, 0), (1, -1), (0, -1))):
                ab_near[k, h * own : (h + 1) * own, :] = ab_wide[
                    plane, TILE + shift : rows + shift, :
                ].astype(BF16)
        for k in range(KW):
            g_dec_ref[k, :, :] += across_rows(ab_near[k], pools[slot])

    def encoder_grad(slot):
        at = pl.ds(pl.multiple_of(slot * pairs, TILE), pairs)
        for k in range(KW):
            g_enc_ref[k, :, :] += across_rows(stems[k, at, :], pre_seq[slot, 0]) + across_rows(
                stems[k + 1, at, :], pre_seq[slot, 1]
            )

    encode(0)
    encode(1)
    for copy in edges:
        copy.wait()
    decode(0)
    relay[0].arrive(1)
    near_grad(0)
    decode(1)
    relay[1].arrive(1)
    across_grad(0)
    far_grad(0)
    turn_slopes(0)
    relay[0].arrive(2)
    near_grad(1)
    across_grad(1)
    pass_on(0)
    far_grad(1)
    g_enc_ref[...] = jnp.zeros_like(g_enc_ref)
    g_dec_ref[...] = jnp.zeros_like(g_dec_ref)
    merged = across_rows(pred_pair[0], split[0:pairs, :])
    pred_ref[...] = (merged + across_rows(pred_pair[1], split[pairs:, :])).astype(BF16)
    relay[1].arrive(2)
    pass_on(1)
    turn_slopes(1)
    for h in both_halves:
        slopes[h].keep().wait()
    decoder_grad(s)
    for i in range(n):
        turn[0].forward(slots[i], i == 0)
    relay[0].arrive(3)
    for slot in slots[1:]:
        slopes[0].forward(slot)
    for i in range(n):
        turn[1].forward(slots[i], i == 0)
        turn[0].relay(slots[i])
    for slot in slots[1:]:
        slopes[0].relay(slot)
    relay[1].arrive(3)
    for i in range(n):
        turn[1].relay(slots[i])
        if i:
            slopes[1].forward(slots[i])
            for h in both_halves:
                turn[h].finish(slots[i - 1])
            encoder_grad(slots[i - 1])
    for slot in slots[1:]:
        slopes[1].relay(slot)
    for h in both_halves:
        turn[h].finish(slots[n - 1])
    encoder_grad(slots[n - 1])
    for slot in slots[1:]:
        for h in both_halves:
            slopes[h].finish(slot)
        decoder_grad(slot)

    for h in both_halves:
        enc[h].end()
        dec[h].end()
        row_copy(h, 0, c, mate).wait_send()
        row_copy(h, 1, c, across).wait_send()
        row_copy(h, 2, across, mate).wait_send()
        relay[h].end()
        slopes[h].end(slots[1:])
        turn[h].end()


def store_kernel(*refs):
    count = (len(refs) - 1) // 2
    sems = refs[-1]
    copies = []
    for source, target in zip(refs[:count], refs[count:-1]):
        parts = source.shape[0] if len(source.shape) == 3 else 1
        for i in range(parts):
            pair = (source.at[i], target.at[i]) if len(source.shape) == 3 else (source, target)
            copies.append(pltpu.make_async_copy(*pair, sems.at[len(copies)]))
    for copy in copies:
        copy.start()
    for copy in copies:
        copy.wait()


def store(*values):
    return pl.pallas_call(
        store_kernel,
        out_shape=tuple(jax.ShapeDtypeStruct(value.shape, value.dtype) for value in values),
        in_specs=[pl.BlockSpec(memory_space=pl.ANY)] * len(values),
        out_specs=(pl.BlockSpec(memory_space=pltpu.HBM),) * len(values),
        scratch_shapes=[dma(2 * KW + len(values))],
        compiler_params=pltpu.CompilerParams(vmem_limit_bytes=1024 * 1024),
    )(*values)


def dma(count):
    return pltpu.SemaphoreType.DMA((count,))


def square_shards(dna_bases, w_stem, w_enc, w_dec, targets):
    rows = dna_bases.shape[0]
    n = lax.axis_size("seq")
    half = rows // 2
    length, pairs = rows * n, half * n
    own = half // HALVES
    held = own + TILE
    c1, c2 = w_stem.shape[0], w_dec.shape[2]
    c1_wide = (c1 + 127) // 128 * 128
    struct = jax.ShapeDtypeStruct

    cut = held // TILE // 3 * TILE
    enc_chunks = ((0, cut), (cut, cut), (2 * cut, held - 2 * cut))
    wide = held + SIDE
    double = HALVES * n
    counts = HALVES * 3 * len(enc_chunks)
    vmem = pl.BlockSpec(memory_space=pltpu.VMEM)
    anywhere = pl.BlockSpec(memory_space=pl.ANY)
    pred, g_enc, g_dec = pl.pallas_call(
        functools.partial(train_kernel, n, 1.0 / math.sqrt(length), enc_chunks),
        out_shape=(
            struct((c1, rows), BF16),
            struct((KW, c1, c2), F32),
            struct((KW, c1, c2), F32),
        ),
        in_specs=[anywhere] * 5,
        out_specs=(vmem, vmem, vmem),
        scratch_shapes=[
            pltpu.VMEM((KW, 4, c1), BF16),
            pltpu.VMEM((KW * SIDE, c1_wide), F32),
            pltpu.VMEM((c1, rows), BF16),
            pltpu.VMEM((n, rows // 128, 128), jnp.int32),
            pltpu.VMEM((c1_wide // 128, rows + 2 * RIM, 128), F32),
            pltpu.VMEM((HALVES, 6, held, c1), BF16),
            pltpu.VMEM((KW, c1, n * c2), BF16),
            pltpu.VMEM((KW, n * c1, c2), BF16),
            pltpu.VMEM((HALVES, 2, held, n * c2), BF16),
            pltpu.VMEM((2, half, c1), BF16),
            pltpu.VMEM((2, half, c1), BF16),
            pltpu.VMEM((rows, rows), BF16),
            pltpu.VMEM((HALVES, 3, 2, held, c2), BF16),
            pltpu.VMEM((HALVES, 2, held, c2), BF16),
            pltpu.VMEM((HALVES, 2, held, c2), F32),
            pltpu.VMEM((held + 2 * SIDE, c2), F32),
            pltpu.VMEM((held, 3 * c2), BF16),
            pltpu.VMEM((HALVES, n, 2, held, c1), BF16),
            pltpu.VMEM((HALVES, 3, 2, held, c1), BF16),
            pltpu.VMEM((HALVES, 2, held, c1), BF16),
            pltpu.VMEM((wide, c1), F32),
            pltpu.VMEM((2, 2, TILE, c1), BF16),
            pltpu.VMEM((2, wide, c1), F32),
            pltpu.VMEM((HALVES, n, 2, held, c1), BF16),
            pltpu.VMEM((3, held + 2 * SIDE, c2), F32),
            pltpu.VMEM((HALVES, 2, own, c2), BF16),
            pltpu.VMEM((HALVES, 2, own // 2, c2), BF16),
            pltpu.VMEM((n, 2, half, c2), BF16),
            pltpu.VMEM((HALVES, n, 2, held, c1), BF16),
            pltpu.VMEM((2, wide, c1), F32),
            pltpu.VMEM((KW, half, c1), BF16),
            pltpu.VMEM((n, half, c2), BF16),
            pltpu.VMEM((6, pairs, c1), BF16),
            dma(counts), dma(counts), dma(HALVES * 3), dma(HALVES * 3), dma(2), dma(2),
            dma(HALVES * 3), dma(HALVES * 3), dma(double), dma(double), dma(double),
            dma(n - 1), dma(n - 1), dma(5),
            dma(HALVES), dma(HALVES), dma(double), dma(double), dma(3 * double), dma(3 * double),
            dma(HALVES),
            dma(double), dma(double), dma(double), dma(double), dma(2 * double), dma(2 * double),
            dma(HALVES),
        ],
        compiler_params=pltpu.CompilerParams(
            collective_id=0, has_side_effects=True, vmem_limit_bytes=VMEM_BYTES
        ),
    )(
        dna_bases.reshape(rows // 128, 128),
        w_stem.transpose(1, 2, 0),
        targets.T,
        w_enc.transpose(1, 2, 0),
        w_dec.transpose(1, 0, 2),
    )
    pred, g_enc, g_dec = store(pred, g_enc, g_dec)
    return (pred.T, g_enc.transpose(2, 0, 1), g_dec.transpose(1, 0, 2))


def shards(dna_bases, w_stem, w_enc, w_dec, targets):
    args = (dna_bases, w_stem, w_enc, w_dec, targets)
    rows, c1, c2 = dna_bases.shape[0], w_stem.shape[0], w_dec.shape[2]
    n = lax.axis_size("seq")
    square = n == 4 and lax.axis_size("chan") == 4
    if square and rows % 512 == 0 and c2 % 128 == 0 and c1 % 64 == 0:
        return square_shards(*args)
    return general_shards(*args)


def solution(mesh):
    return jax.shard_map(
        shards,
        mesh=mesh,
        in_specs=(
            P(("groups", "seq")),
            P("chan", None, None),
            P(None, None, "chan"),
            P(None, None, "chan"),
            P(("groups", "seq"), "chan"),
        ),
        out_specs=(
            P(("groups", "seq"), "chan"),
            P(("groups", "seq"), None, "chan"),
            P(("groups", "seq"), None, "chan"),
        ),
        check_vma=False,
    )
```

```python
import functools
import math

import jax
import jax.numpy as jnp
from jax import lax
from jax.experimental import pallas as pl
from jax.experimental.pallas import tpu as pltpu
from jax.sharding import PartitionSpec as P

KW = 5


SQRT_TWO_PI = 0.7978845608028654
CUBIC = 0.044715


def extended(block, sides, width):
    for axis, dim in sides:
        count = lax.axis_size(axis)
        forward = [(i, i + 1) for i in range(count - 1)]
        backward = [(target, source) for source, target in forward]
        low = lax.ppermute(
            lax.slice_in_dim(block, block.shape[dim] - width, None, axis=dim), axis, forward
        )
        high = lax.ppermute(lax.slice_in_dim(block, 0, width, axis=dim), axis, backward)
        block = jnp.concatenate([low, block, high], axis=dim)
    return block


def gelu_value(value):
    inner = jnp.tanh(SQRT_TWO_PI * (value + CUBIC * value * value * value))
    return 0.5 * value * (1.0 + inner)


def gelu_slope(value):
    inner = jnp.tanh(SQRT_TWO_PI * (value + CUBIC * value * value * value))
    return 0.5 * (1.0 + inner) + 0.5 * value * (1.0 - inner * inner) * SQRT_TWO_PI * (
        1.0 + 3.0 * CUBIC * value * value
    )


def rim_cells(block, margin):
    return extended(block, (("seq", 0),), margin)


def channel_sum(partial_value):
    return lax.psum_scatter(partial_value, "chan", scatter_dimension=1, tiled=True)


def channel_gather(block):
    return lax.all_gather(block, "chan", axis=1, tiled=True)


def conv_rows(padded, weight):
    row_count = padded.shape[0] - 4
    total = jnp.zeros((row_count, weight.shape[0]), jnp.float32)
    for k in range(KW):
        total = total + lax.dot_general(
            padded[k : k + row_count],
            weight[:, k, :],
            (((1,), (1,)), ((), ())),
            preferred_element_type=jnp.float32,
        )
    return total


def grad_taps(picked, padded):
    row_count = picked.shape[0]
    pieces = [
        lax.dot_general(
            picked,
            padded[k : k + row_count],
            (((0,), (0,)), ((), ())),
            preferred_element_type=jnp.float32,
        )
        for k in range(KW)
    ]
    return jnp.stack(pieces, axis=1)


def weight_grad(cotangent, padded):
    rounded = grad_taps(cotangent, padded).astype(jnp.bfloat16)
    return lax.psum_scatter(
        lax.optimization_barrier(rounded).astype(jnp.float32),
        "seq",
        scatter_dimension=0,
        tiled=True,
    )


def general_shards(dna_bases, w_stem, w_enc, w_dec, targets):
    row_count = dna_bases.shape[0]
    devices = lax.axis_size("seq")
    length = row_count * devices
    onehot = (dna_bases[:, None] == jnp.arange(4, dtype=jnp.int32)[None, :]).astype(jnp.bfloat16)
    onehot_pad = rim_cells(onehot, 2)
    stem_out = gelu_value(conv_rows(onehot_pad, w_stem)).astype(jnp.bfloat16)
    stem_pad = rim_cells(stem_out, 2)
    enc_pre = channel_sum(conv_rows(stem_pad, w_enc))
    active = gelu_value(enc_pre).astype(jnp.bfloat16).astype(jnp.float32)
    pooled = (0.5 * active.reshape(row_count // 2, 2, -1).sum(axis=1)).astype(jnp.bfloat16)
    pooled_pad = rim_cells(pooled, 1)
    up_pad = jnp.repeat(pooled_pad, 2, axis=0)
    output = channel_sum(conv_rows(up_pad, w_dec)) + stem_out.astype(jnp.float32)
    pred = output.astype(jnp.bfloat16)
    scale = 1.0 / math.sqrt(length)
    slope_out = ((output - targets.astype(jnp.float32)) * scale).astype(jnp.bfloat16)
    slope_all = channel_gather(slope_out)
    g_dec = weight_grad(slope_all, up_pad)
    slope_pad = rim_cells(slope_all, 2)
    up_grad = jnp.zeros((row_count, w_dec.shape[2]), jnp.float32)
    for k in range(KW):
        up_grad = up_grad + jnp.dot(
            slope_pad[4 - k : 4 - k + row_count], w_dec[:, k, :], preferred_element_type=jnp.float32
        )
    pool_grad = up_grad.reshape(row_count // 2, 2, -1).sum(axis=1)
    act_grad = 0.5 * jnp.repeat(pool_grad, 2, axis=0)
    pre_grad = (act_grad * gelu_slope(enc_pre)).astype(jnp.bfloat16)
    pre_all = channel_gather(pre_grad)
    g_enc = weight_grad(pre_all, stem_pad)
    return (pred, g_enc, g_dec)


MESH_ID = pl.DeviceIdType.MESH
BF16 = jnp.bfloat16
F32 = jnp.float32
TILE = 16
SIDE = 8
RIM = 32
HALVES = 2
VMEM_BYTES = 48 * 1024 * 1024


def send(src, dst, send_sem, recv_sem, seq, chan):
    return pltpu.make_async_remote_copy(
        src_ref=src,
        dst_ref=dst,
        send_sem=send_sem,
        recv_sem=recv_sem,
        device_id={"seq": seq, "chan": chan},
        device_id_type=MESH_ID,
    )


def greet(targets):
    barrier = pltpu.get_barrier_semaphore()
    for seq, chan in targets:
        pl.semaphore_signal(
            barrier, inc=1, device_id={"seq": seq, "chan": chan}, device_id_type=MESH_ID
        )
    pl.semaphore_wait(barrier, len(targets))


def partner_group(n, s, c):
    mate = partners(c)[0]
    others = [(s, lax.rem(c + d, n)) for d in range(1, n)]
    for d in range(1, n):
        others += [(lax.rem(s + d, n), c), (lax.rem(s + d, n), mate)]
    return others


def partners(c):
    mate = c + 1 - 2 * lax.rem(c, 2)
    across = lax.rem(c + 2, 4)
    return mate, across, lax.rem(mate + 2, 4)


def span(first, count):
    return pl.ds(first, count)


def tiles(first, count, body):
    @pl.loop(0, count // TILE)
    def _(i):
        body(pl.ds(pl.multiple_of(first + i * TILE, TILE), TILE))


class Part:
    def __init__(self, sem, base):
        self.sem, self.base = sem, base

    @property
    def at(self):
        return self

    def __getitem__(self, index):
        return self.sem.at[self.base + index]


class Turn:
    def __init__(self, n, s, c, h, own, mid, out, sems):
        self.n, self.s, self.c, self.h, self.own, self.mid, self.out = n, s, c, h, own, mid, out
        (self.cross_send, self.cross_recv, self.along_send, self.along_recv,
         self.share_send, self.share_recv, self.local) = sems
        self.count = own.shape[1]
        self.piece = self.count // n
        self.side = c // 2

    def out_rows(self, index):
        first = self.h * self.count + index * self.piece
        return pl.ds(pl.multiple_of(first, self.piece), self.piece)

    def cross(self):
        wide = 2 * self.piece
        at = pl.ds(pl.multiple_of((1 - self.side) * wide, wide), wide)
        return send(self.own.at[:, at], self.mid, self.cross_send.at[0], self.cross_recv.at[0],
                    self.s, partners(self.c)[1])

    def source(self, plane, q):
        if plane:
            first = (q - 2 * self.side) * self.piece
            return self.mid.at[:, pl.ds(pl.multiple_of(first, self.piece), self.piece)]
        return self.own.at[:, pl.ds(pl.multiple_of(q * self.piece, self.piece), self.piece)]

    def along(self, plane, kind, slot):
        mate, across, _ = partners(self.c)
        q = mate if kind else self.c
        return send(self.source(plane, q), self.out.at[self.s, :, self.out_rows(q)],
                    self.along_send.at[2 * plane + kind], self.along_recv.at[slot],
                    across if plane else self.c, q)

    def keep(self, plane):
        return pltpu.make_async_copy(
            self.source(plane, self.c), self.out.at[self.s, :, self.out_rows(self.c)], self.local
        )

    def home(self, plane):
        return self.s == (partners(self.c)[1] if plane else self.c)

    def start(self, plane):
        home = self.home(plane)
        pl.when(jnp.logical_not(home))(lambda: self.along(plane, 0, self.s).start())
        pl.when(home)(lambda: self.keep(plane).start())
        self.along(plane, 1, self.s).start()

    def share(self, slot, kind, part, to):
        spot = self.out.at[slot, :, self.out_rows(part)]
        index = slot * 3 + kind
        return send(spot, spot, self.share_send.at[index], self.share_recv.at[index], self.s, to)

    def forward(self, slot, mine):
        mate, across, _ = partners(self.c)
        if mine:
            pl.when(self.home(0))(lambda: self.keep(0).wait())
            pl.when(self.home(1))(lambda: self.keep(1).wait())
            other = jnp.logical_not(jnp.logical_or(self.home(0), self.home(1)))
            pl.when(other)(lambda: self.along(0, 0, slot).wait_recv())
        else:
            self.along(0, 0, slot).wait_recv()
        self.share(slot, 1, self.c, across).start()
        self.share(slot, 0, self.c, mate).start()

    def relay(self, slot):
        mate, across, _ = partners(self.c)
        self.share(slot, 1, across, across).wait_recv()
        self.share(slot, 2, across, mate).start()

    def finish(self, slot):
        mate, across, far = partners(self.c)
        self.share(slot, 0, mate, mate).wait_recv()
        self.share(slot, 2, far, mate).wait_recv()

    def end(self):
        mate, across, _ = partners(self.c)
        for slot in range(self.n):
            self.share(slot, 0, self.c, mate).wait_send()
            self.share(slot, 1, self.c, across).wait_send()
            self.share(slot, 2, across, mate).wait_send()
        self.cross().wait_send()
        for plane in range(2):
            pl.when(jnp.logical_not(self.home(plane)))(
                functools.partial(lambda plane: self.along(plane, 0, self.s).wait_send(), plane)
            )
            self.along(plane, 1, self.s).wait_send()


class PairSum:
    def __init__(self, block, held, pair, s, c, chunks, sems):
        self.block, self.held, self.pair, self.s, self.c = block, held, pair, s, c
        self.chunks = chunks
        self.send_sem, self.recv_sem = sems

    def hop(self, kind, q):
        mate, across, far = partners(self.c)
        source = (lambda: self.block(mate), lambda: self.block(far), lambda: self.pair)[kind]()
        target = (mate, mate, across)[kind]
        at = span(*self.chunks[q])
        index = kind * len(self.chunks) + q
        return send(source.at[:, at], self.held.at[kind, :, at], self.send_sem.at[index],
                    self.recv_sem.at[index], self.s, target)

    def start(self, kind):
        for q in range(len(self.chunks)):
            self.hop(kind, q).start()

    def cross(self, q):
        _, across, _ = partners(self.c)
        self.hop(1, q).wait_recv()
        block = self.block(across)

        def body(at):
            self.pair[:, at, :] = (
                block[:, at, :].astype(F32) + self.held[1, :, at, :].astype(F32)
            ).astype(BF16)

        tiles(*self.chunks[q], body)
        self.hop(2, q).start()

    def arrive(self, q):
        self.hop(0, q).wait_recv()
        self.hop(2, q).wait_recv()

    def total(self, at):
        mine = self.block(self.c)[:, at, :].astype(F32)
        return mine + self.held[0, :, at, :].astype(F32) + self.held[2, :, at, :].astype(F32)

    def end(self):
        for kind in range(3):
            for q in range(len(self.chunks)):
                self.hop(kind, q).wait_send()


class PoolRelay:
    def __init__(self, n, s, c, h, out, right_send, left_send, recv):
        self.n, self.s, self.c, self.out = n, s, c, out
        self.right_send, self.left_send, self.recv = right_send, left_send, recv
        self.at = span(h * (out.shape[1] // HALVES), out.shape[1] // HALVES)

    def hop(self, slot, step):
        sems = self.right_send if step > 0 else self.left_send
        spot = self.out.at[slot, self.at]
        return send(spot, spot, sems.at[slot], self.recv.at[slot], self.s + step, self.c)

    def start(self):
        pl.when(self.s < self.n - 1)(lambda: self.hop(self.s, 1).start())
        pl.when(self.s > 0)(lambda: self.hop(self.s, -1).start())

    def arrive(self, d):
        low, high = self.s - d, self.s + d

        @pl.when(low >= 0)
        def _():
            self.hop(low, 1).wait_recv()
            pl.when(self.s < self.n - 1)(lambda: self.hop(low, 1).start())

        @pl.when(high < self.n)
        def _():
            self.hop(high, -1).wait_recv()
            pl.when(self.s > 0)(lambda: self.hop(high, -1).start())

    def end(self):
        for slot in range(self.n):
            pl.when(jnp.logical_and(slot <= self.s, self.s < self.n - 1))(
                functools.partial(lambda slot: self.hop(slot, 1).wait_send(), slot)
            )
            pl.when(jnp.logical_and(slot >= self.s, self.s > 0))(
                functools.partial(lambda slot: self.hop(slot, -1).wait_send(), slot)
            )


class SlopeTurn:
    def __init__(self, n, s, c, chan, out, sems):
        self.n, self.s, self.c, self.chan, self.out = n, s, c, chan, out
        (self.send_sem, self.recv_sem, self.cross_send, self.cross_recv,
         self.share_send, self.share_recv, self.local) = sems
        self.plane = c // 2
        self.hub = lax.rem(s, 2) == lax.rem(c, 2)

    def hop(self, to, slot):
        return send(self.chan.at[to, self.plane], self.out.at[self.s, self.plane],
                    self.send_sem.at[to], self.recv_sem.at[slot], to, self.c)

    def mine(self, block):
        return jnp.logical_and(block != self.s, lax.rem(block, 2) == lax.rem(self.c, 2))

    def start(self, block):
        pl.when(self.mine(block))(lambda: self.hop(block, self.s).start())

    def keep(self):
        return pltpu.make_async_copy(self.chan.at[self.s], self.out.at[self.s], self.local)

    def cross(self, slot, plane):
        spot = self.out.at[slot, plane]
        return send(spot, spot, self.cross_send.at[slot], self.cross_recv.at[slot], self.s,
                    partners(self.c)[1])

    def share(self, slot, plane):
        spot = self.out.at[slot, plane]
        return send(spot, spot, self.share_send.at[2 * slot + plane],
                    self.share_recv.at[2 * slot + plane], self.s, partners(self.c)[0])

    def forward(self, slot):
        @pl.when(self.hub)
        def _():
            self.hop(self.s, slot).wait_recv()
            self.cross(slot, self.plane).start()
            self.share(slot, self.plane).start()

    def relay(self, slot):
        @pl.when(self.hub)
        def _():
            self.cross(slot, 1 - self.plane).wait_recv()
            self.share(slot, 1 - self.plane).start()

    def finish(self, slot):
        @pl.when(jnp.logical_not(self.hub))
        def _():
            for plane in range(2):
                self.share(slot, plane).wait_recv()

    def end(self, others):
        for slot in others:
            pl.when(self.mine(slot))(
                functools.partial(lambda slot: self.hop(slot, self.s).wait_send(), slot)
            )

        @pl.when(self.hub)
        def _():
            for slot in others:
                self.cross(slot, self.plane).wait_send()
                for plane in range(2):
                    self.share(slot, plane).wait_send()


def across_rows(left, right):
    return lax.dot_general(left, right, (((0,), (0,)), ((), ())), preferred_element_type=F32)


def by_channels(left, right):
    return lax.dot_general(left, right, (((1,), (1,)), ((), ())), preferred_element_type=F32)


def train_kernel(
    n, scale, enc_chunks, bases_ref, w_stem_hbm, target_hbm, w_enc_ref, w_dec_ref,
    pred_ref, g_enc_ref, g_dec_ref,
    w_stem_small, w_stem_ref, target_in, bases, natural, near, w_enc, w_ref, part, target_ref, pred_pair, split,
    enc_held, enc_pair, bend, pool_wide, pool_near, dec_part, dec_held, dec_pair, q_wide,
    edge, slope, chan, up, pre_own, pre_mid, pre_seq, ab_seq, ab_wide, ab_near, pools, stems,
    enc_send, enc_recv, dec_send, dec_recv, edge_send, edge_recv, row_send, row_recv,
    right_send, left_send, pool_recv, bases_send, bases_recv, local_sem, *turn_sems,
):
    s, c = lax.axis_index("seq"), lax.axis_index("chan")
    mate, across, far = partners(c)
    rows, c2 = pool_near.shape[0], pool_wide.shape[1]
    own = rows - TILE
    pairs = HALVES * own
    c1 = near.shape[3]
    upper = s // 2
    slots = (s, 1 - s + 4 * upper, 2 - upper, 3 - 3 * upper)
    both_halves = range(HALVES)
    weight_copies = [
        pltpu.make_async_copy(w_enc_ref, w_enc, local_sem.at[0]),
        pltpu.make_async_copy(w_dec_ref, w_ref, local_sem.at[1]),
    ]
    small_copies = [
        pltpu.make_async_copy(bases_ref, bases.at[s], local_sem.at[2]),
        pltpu.make_async_copy(w_stem_hbm, w_stem_small, local_sem.at[3]),
        pltpu.make_async_copy(target_hbm, target_in, local_sem.at[4]),
    ]
    for copy in small_copies[:2] + weight_copies[:1] + small_copies[2:] + weight_copies[1:]:
        copy.start()
    greet(partner_group(n, s, c))
    small_copies[0].wait()
    base_copies = [
        send(bases.at[s], bases.at[s], bases_send.at[d - 1], bases_recv.at[d - 1],
             lax.rem(s + d, n), c)
        for d in range(1, n)
    ]
    for copy in base_copies:
        copy.start()

    def column_block(h, j):
        return part.at[h, :, :, pl.ds(pl.multiple_of(j * c2, 128), c2)]

    counts = 3 * len(enc_chunks)
    enc = [
        PairSum(functools.partial(column_block, h), enc_held.at[h], enc_pair.at[h], s, c,
                enc_chunks, (Part(enc_send, h * counts), Part(enc_recv, h * counts)))
        for h in both_halves
    ]
    dec = [
        PairSum(functools.partial(lambda h, j: dec_part.at[h, j], h), dec_held.at[h],
                dec_pair.at[h], s, c, ((0, rows),), (Part(dec_send, h * 3), Part(dec_recv, h * 3)))
        for h in both_halves
    ]
    relay = [
        PoolRelay(n, s, c, h, pools, *[Part(sem, h * n) for sem in (right_send, left_send, pool_recv)])
        for h in both_halves
    ]
    turn = [
        Turn(n, s, c, h, pre_own.at[h], pre_mid.at[h], pre_seq,
             [Part(sem, h * size) for sem, size in zip(turn_sems[:6], (1, 1, n, n, 3 * n, 3 * n))]
             + [turn_sems[6].at[h]])
        for h in both_halves
    ]
    slopes = [
        SlopeTurn(n, s, c, chan.at[h], ab_seq.at[h],
                  [Part(sem, h * n) for sem in turn_sems[7:11]]
                  + [Part(sem, 2 * h * n) for sem in turn_sems[11:13]] + [turn_sems[13].at[h]])
        for h in both_halves
    ]

    def stem_rows(slot):
        before = bases[lax.rem(slot + n - 1, n)]
        here = bases[slot]
        after = bases[lax.rem(slot + 1, n)]
        count = here.shape[0]
        lanes = [jnp.where(slot > 0, before[count - 1 :], -1)]
        lanes += [here[i : i + 1] for i in range(count)]
        lanes += [jnp.where(slot < n - 1, after[:1], -1)]
        line = jnp.concatenate(lanes, axis=1)
        total = line.shape[1]
        line = jnp.broadcast_to(line, (SIDE, total))
        kind = lax.broadcasted_iota(jnp.int32, (SIDE, total), 0)
        onehot = jnp.concatenate(
            [
                jnp.where(pltpu.roll(line, (2 - k) % total, 1) == kind, 1.0, 0.0)
                for k in range(KW)
            ],
            axis=0,
        ).astype(BF16)
        for i in range(count + 2):
            value = across_rows(onehot[:, i * 128 : (i + 1) * 128], w_stem_ref[...].astype(BF16))
            first = 128 * (i - 1) + RIM
            if i == 0:
                first, value = 0, jnp.where(slot > 0, value[128 - RIM :], 0.0)
            if i == count + 1:
                value = jnp.where(slot < n - 1, value[:RIM], 0.0)
            value = gelu_value(value)
            for t in range(natural.shape[0]):
                natural[t, first : first + value.shape[0], :] = value[:, t * 128 : (t + 1) * 128]

    def every_other(t, first, count):
        return natural[t, pl.ds(first, count, stride=2), : min(128, c1 - t * 128)]

    def piece_start(i):
        return RIM + i % 2 + 2 * (i // 2 - 1)

    def lane_span(t):
        return slice(t * 128, min(c1, (t + 1) * 128))

    def near_rows():
        for h in both_halves:
            for i in range(6):
                first = piece_start(i) + 2 * own * h
                for t in range(natural.shape[0]):
                    halo = [every_other(t, first + 2 * own, SIDE), every_other(t, first - 2 * SIDE, SIDE)]
                    near[h, i, 0:TILE, lane_span(t)] = jnp.concatenate(halo, axis=0).astype(BF16)
                    near[h, i, TILE:, lane_span(t)] = every_other(t, first, own).astype(BF16)

    def keep_stems(slot):
        at = pl.ds(pl.multiple_of(slot * pairs, TILE), pairs)
        for i in range(6):
            for t in range(natural.shape[0]):
                stems[i, at, lane_span(t)] = every_other(t, piece_start(i), pairs).astype(BF16)

    def part_block(h, j):
        at = pl.ds(pl.multiple_of(j * c2, 128), c2)
        total = None
        for k in range(KW):
            window = near[h, k : k + 2].reshape(2 * rows, c1)
            term = jnp.dot(window, w_enc[k, :, at], preferred_element_type=F32)
            total = term if total is None else total + term
        part[h, :, :, at] = total.astype(BF16).reshape(2, rows, c2)

    edges = [
        send(target_ref.at[:, pl.ds(pairs - TILE, TILE)], edge.at[0], edge_send.at[0],
             edge_recv.at[0], lax.rem(s + 1, n), c),
        send(target_ref.at[:, pl.ds(0, TILE)], edge.at[1], edge_send.at[1], edge_recv.at[1],
             lax.rem(s + n - 1, n), c),
    ]

    def pair_targets():
        size = 2 * pairs
        for first in range(0, size, 128):
            place = lax.broadcasted_iota(jnp.int32, (128, size), 0) + first % pairs
            wanted = 2 * place + first // pairs
            column = lax.broadcasted_iota(jnp.int32, (128, size), 1)
            split[first : first + 128, :] = jnp.where(column == wanted, 1.0, 0.0).astype(BF16)
        for parity in range(2):
            value = by_channels(split[parity * pairs : (parity + 1) * pairs, :], target_in[...])
            target_ref[parity, :, :] = value.astype(BF16)

    small_copies[1].wait()
    w_stem_ref[...] = jnp.zeros_like(w_stem_ref)
    for k in range(KW):
        w_stem_ref[k * SIDE : k * SIDE + 4, 0:c1] = w_stem_small[k].astype(F32)
    for copy in base_copies:
        copy.wait()
    stem_rows(s)
    near_rows()
    weight_copies[0].wait()
    part_block(0, far)
    enc[0].start(1)
    part_block(0, across)
    part_block(1, far)
    enc[1].start(1)
    for q in range(len(enc_chunks)):
        enc[0].cross(q)
    part_block(1, across)
    for q in range(len(enc_chunks)):
        enc[1].cross(q)
    for h in both_halves:
        part_block(h, mate)
        enc[h].start(0)
        part_block(h, c)
    small_copies[2].wait()
    pair_targets()
    for copy in edges:
        copy.start()
    keep_stems(s)

    @pl.loop(1, n)
    def _(d):
        slot = lax.rem(s + d, n)
        stem_rows(slot)
        keep_stems(slot)

    weight_copies[1].wait()

    row = lax.broadcasted_iota(jnp.int32, (TILE, 1), 0)
    inside = (
        jnp.logical_or(row < SIDE, s > 0),
        jnp.logical_or(row >= SIDE, s < n - 1),
    )

    def enc_rows(h, at):
        total = enc[h].total(at)
        square = total * total
        inner = jnp.tanh(SQRT_TWO_PI * (total + CUBIC * square * total))
        active = (0.5 * total * (1.0 + inner)).astype(BF16).astype(F32)
        pooled = (0.5 * (active[0] + active[1])).astype(BF16).astype(F32)
        pool_wide[pl.ds(pl.multiple_of(at.start + SIDE, SIDE), TILE), :] = pooled
        bend[h, :, at, :] = 0.5 * (
            0.5 * (1.0 + inner)
            + 0.5 * total * (1.0 - inner * inner) * SQRT_TWO_PI * (1.0 + 3.0 * CUBIC * square)
        )

    def conv_block(h, j):
        at = pl.ds(pl.multiple_of(j * c1, TILE), c1)
        before, here, after = (pool_near[:, i * c2 : (i + 1) * c2] for i in range(3))
        shared = by_channels(before, w_ref[0, at, :]) + by_channels(here, w_ref[2, at, :])
        shared = shared + by_channels(after, w_ref[4, at, :])
        single = by_channels(before, w_ref[1, at, :]) + by_channels(here, w_ref[3, at, :])
        q_wide[0:rows, :] = single
        q_wide[rows:, :] = single[0:SIDE]
        dec_part[h, j, 0, :, :] = (shared + single).astype(BF16)
        dec_part[h, j, 1, :, :] = (shared + q_wide[1 : rows + 1, :]).astype(BF16)

    def encode(h):
        for q in range(len(enc_chunks)):
            enc[h].arrive(q)
            tiles(*enc_chunks[q], functools.partial(enc_rows, h))
        halo = pool_wide[SIDE : SIDE + TILE, :]
        pool_wide[SIDE : SIDE + TILE, :] = jnp.where(inside[h], halo, 0.0)
        pool_wide[0:SIDE, :] = pool_wide[rows : rows + SIDE, :]
        pool_wide[rows + SIDE :, :] = pool_wide[SIDE : 2 * SIDE, :]
        for first in range(0, rows, TILE):
            for shift in range(3):
                value = pool_wide[first + SIDE - 1 + shift : first + SIDE - 1 + shift + TILE, :]
                pool_near[first : first + TILE, shift * c2 : (shift + 1) * c2] = value.astype(BF16)
        conv_block(h, far)
        dec[h].start(1)
        pools[s, h * own : (h + 1) * own, :] = pool_near[TILE:, c2 : 2 * c2]
        relay[h].start()
        conv_block(h, across)
        dec[h].cross(0)
        conv_block(h, mate)
        dec[h].start(0)
        conv_block(h, c)

    def slope_tile(h, at, target, keep=None):
        output = dec[h].total(at) + near[h, 2:4, at, :].astype(F32)
        value = (output - target) * scale
        if keep is None:
            own_at = pl.ds(pl.multiple_of(at.start - TILE + h * own, TILE), TILE)
            pred_pair[:, own_at, :] = output.astype(BF16)
        else:
            value = jnp.where(keep[None], value, 0.0)
        slope[:, at, :] = value

    def slope_rows(h, at):
        own_at = pl.ds(pl.multiple_of(at.start - TILE + h * own, TILE), TILE)
        slope_tile(h, at, target_ref[:, own_at, :].astype(F32))

    def row_copy(h, kind, owner, to):
        spot = chan.at[h, owner]
        return send(spot, spot, row_send.at[h * 3 + kind], row_recv.at[h * 3 + kind], s, to)

    def decode(h):
        dec[h].arrive(0)
        high = target_ref[:, own : own + TILE, :] if h == 0 else edge[1]
        low = edge[0] if h == 0 else target_ref[:, own - TILE : own, :]
        target = jnp.where(row[None] < SIDE, high.astype(F32), low.astype(F32))
        slope_tile(h, pl.ds(0, TILE), target, inside[h])
        slope[:, rows:, :] = slope[:, 0:SIDE, :]
        tiles(TILE, own, functools.partial(slope_rows, h))
        for start in range(0, rows, TILE):
            even = slope[0, start : start + TILE, :]
            odd = slope[1, start : start + TILE, :]
            following = slope[0, start + 1 : start + 1 + TILE, :]
            chan[h, c, 0, start : start + TILE, :] = (even + odd).astype(BF16)
            chan[h, c, 1, start : start + TILE, :] = (odd + following).astype(BF16)
        row_copy(h, 1, c, across).start()
        row_copy(h, 0, c, mate).start()

    def up_block(h, j, first):
        at = pl.ds(pl.multiple_of(j * c1, TILE), c1)
        for place, terms in enumerate((((0, 0),), ((1, 1), (0, 2)), ((1, 3), (0, 4)))):
            total = None
            for plane, k in terms:
                term = jnp.dot(chan[h, j, plane], w_ref[k, at, :], preferred_element_type=F32)
                total = term if total is None else total + term
            if not first:
                total = total + up[place, SIDE : SIDE + rows, :]
            up[place, SIDE : SIDE + rows, :] = total

    def bend_back(h):
        up[0, SIDE + rows :, :] = up[0, SIDE : 2 * SIDE, :]
        for first in range(0, own, TILE):
            spot = first + TILE + SIDE
            grad = (
                up[0, spot + 1 : spot + 1 + TILE, :]
                + up[1, spot : spot + TILE, :]
                + up[2, spot - 1 : spot - 1 + TILE, :]
            )
            pre_own[h, :, first : first + TILE, :] = (
                grad[None] * bend[h, :, first + TILE : first + 2 * TILE, :]
            ).astype(BF16)
        turn[h].cross().start()
        turn[h].start(0)

    def near_grad(h):
        if h == 0:
            slopes[h].start(c)
        up_block(h, c, True)
        row_copy(h, 0, mate, mate).wait_recv()
        if h == 0:
            slopes[h].start(mate)
        up_block(h, mate, False)

    def across_grad(h):
        row_copy(h, 1, across, across).wait_recv()
        row_copy(h, 2, across, mate).start()
        up_block(h, across, False)

    def far_grad(h):
        row_copy(h, 2, far, mate).wait_recv()
        up_block(h, far, False)
        bend_back(h)

    def pass_on(h):
        turn[h].cross().wait_recv()
        turn[h].start(1)

    def turn_slopes(h):
        for block in (across, far) if h == 0 else (c, mate, across, far):
            slopes[h].start(block)
        slopes[h].keep().start()

    def decoder_grad(slot):
        for h in both_halves:
            for plane in range(2):
                value = ab_seq[h, slot, plane].astype(F32)
                ab_wide[plane, 0:rows, :] = value
                ab_wide[plane, rows:, :] = value[0:SIDE]
            for k, (plane, shift) in enumerate(((0, 1), (1, 0), (0, 0), (1, -1), (0, -1))):
                ab_near[k, h * own : (h + 1) * own, :] = ab_wide[
                    plane, TILE + shift : rows + shift, :
                ].astype(BF16)
        for k in range(KW):
            g_dec_ref[k, :, :] += across_rows(ab_near[k], pools[slot])

    def encoder_grad(slot):
        at = pl.ds(pl.multiple_of(slot * pairs, TILE), pairs)
        for k in range(KW):
            g_enc_ref[k, :, :] += across_rows(stems[k, at, :], pre_seq[slot, 0]) + across_rows(
                stems[k + 1, at, :], pre_seq[slot, 1]
            )

    encode(0)
    encode(1)
    for copy in edges:
        copy.wait()
    decode(0)
    relay[0].arrive(1)
    near_grad(0)
    decode(1)
    relay[1].arrive(1)
    across_grad(0)
    far_grad(0)
    turn_slopes(0)
    relay[0].arrive(2)
    near_grad(1)
    across_grad(1)
    pass_on(0)
    far_grad(1)
    g_enc_ref[...] = jnp.zeros_like(g_enc_ref)
    g_dec_ref[...] = jnp.zeros_like(g_dec_ref)
    merged = across_rows(pred_pair[0], split[0:pairs, :])
    pred_ref[...] = (merged + across_rows(pred_pair[1], split[pairs:, :])).astype(BF16)
    relay[1].arrive(2)
    pass_on(1)
    turn_slopes(1)
    for h in both_halves:
        slopes[h].keep().wait()
    for i in range(n):
        turn[0].forward(slots[i], i == 0)
    decoder_grad(s)
    relay[0].arrive(3)
    for slot in slots[1:]:
        slopes[0].forward(slot)
    for i in range(n):
        turn[1].forward(slots[i], i == 0)
        turn[0].relay(slots[i])
    for slot in slots[1:]:
        slopes[0].relay(slot)
    relay[1].arrive(3)
    for i in range(n):
        turn[1].relay(slots[i])
        if i:
            slopes[1].forward(slots[i])
            for h in both_halves:
                turn[h].finish(slots[i - 1])
            encoder_grad(slots[i - 1])
    for slot in slots[1:]:
        slopes[1].relay(slot)
    for h in both_halves:
        turn[h].finish(slots[n - 1])
    encoder_grad(slots[n - 1])
    for slot in slots[1:]:
        for h in both_halves:
            slopes[h].finish(slot)
        decoder_grad(slot)

    for h in both_halves:
        enc[h].end()
        dec[h].end()
        row_copy(h, 0, c, mate).wait_send()
        row_copy(h, 1, c, across).wait_send()
        row_copy(h, 2, across, mate).wait_send()
        relay[h].end()
        slopes[h].end(slots[1:])
        turn[h].end()


def store_kernel(*refs):
    count = (len(refs) - 1) // 2
    sems = refs[-1]
    copies = []
    for source, target in zip(refs[:count], refs[count:-1]):
        parts = source.shape[0] if len(source.shape) == 3 else 1
        for i in range(parts):
            pair = (source.at[i], target.at[i]) if len(source.shape) == 3 else (source, target)
            copies.append(pltpu.make_async_copy(*pair, sems.at[len(copies)]))
    for copy in copies:
        copy.start()
    for copy in copies:
        copy.wait()


def store(*values):
    return pl.pallas_call(
        store_kernel,
        out_shape=tuple(jax.ShapeDtypeStruct(value.shape, value.dtype) for value in values),
        in_specs=[pl.BlockSpec(memory_space=pl.ANY)] * len(values),
        out_specs=(pl.BlockSpec(memory_space=pltpu.HBM),) * len(values),
        scratch_shapes=[dma(2 * KW + len(values))],
        compiler_params=pltpu.CompilerParams(vmem_limit_bytes=1024 * 1024),
    )(*values)


def dma(count):
    return pltpu.SemaphoreType.DMA((count,))


def square_shards(dna_bases, w_stem, w_enc, w_dec, targets):
    rows = dna_bases.shape[0]
    n = lax.axis_size("seq")
    half = rows // 2
    length, pairs = rows * n, half * n
    own = half // HALVES
    held = own + TILE
    c1, c2 = w_stem.shape[0], w_dec.shape[2]
    c1_wide = (c1 + 127) // 128 * 128
    struct = jax.ShapeDtypeStruct

    cut = held // TILE // 3 * TILE
    enc_chunks = ((0, cut), (cut, cut), (2 * cut, held - 2 * cut))
    wide = held + SIDE
    double = HALVES * n
    counts = HALVES * 3 * len(enc_chunks)
    vmem = pl.BlockSpec(memory_space=pltpu.VMEM)
    anywhere = pl.BlockSpec(memory_space=pl.ANY)
    pred, g_enc, g_dec = pl.pallas_call(
        functools.partial(train_kernel, n, 1.0 / math.sqrt(length), enc_chunks),
        out_shape=(
            struct((c1, rows), BF16),
            struct((KW, c1, c2), F32),
            struct((KW, c1, c2), F32),
        ),
        in_specs=[anywhere] * 5,
        out_specs=(vmem, vmem, vmem),
        scratch_shapes=[
            pltpu.VMEM((KW, 4, c1), BF16),
            pltpu.VMEM((KW * SIDE, c1_wide), F32),
            pltpu.VMEM((c1, rows), BF16),
            pltpu.VMEM((n, rows // 128, 128), jnp.int32),
            pltpu.VMEM((c1_wide // 128, rows + 2 * RIM, 128), F32),
            pltpu.VMEM((HALVES, 6, held, c1), BF16),
            pltpu.VMEM((KW, c1, n * c2), BF16),
            pltpu.VMEM((KW, n * c1, c2), BF16),
            pltpu.VMEM((HALVES, 2, held, n * c2), BF16),
            pltpu.VMEM((2, half, c1), BF16),
            pltpu.VMEM((2, half, c1), BF16),
            pltpu.VMEM((rows, rows), BF16),
            pltpu.VMEM((HALVES, 3, 2, held, c2), BF16),
            pltpu.VMEM((HALVES, 2, held, c2), BF16),
            pltpu.VMEM((HALVES, 2, held, c2), F32),
            pltpu.VMEM((held + 2 * SIDE, c2), F32),
            pltpu.VMEM((held, 3 * c2), BF16),
            pltpu.VMEM((HALVES, n, 2, held, c1), BF16),
            pltpu.VMEM((HALVES, 3, 2, held, c1), BF16),
            pltpu.VMEM((HALVES, 2, held, c1), BF16),
            pltpu.VMEM((wide, c1), F32),
            pltpu.VMEM((2, 2, TILE, c1), BF16),
            pltpu.VMEM((2, wide, c1), F32),
            pltpu.VMEM((HALVES, n, 2, held, c1), BF16),
            pltpu.VMEM((3, held + 2 * SIDE, c2), F32),
            pltpu.VMEM((HALVES, 2, own, c2), BF16),
            pltpu.VMEM((HALVES, 2, own // 2, c2), BF16),
            pltpu.VMEM((n, 2, half, c2), BF16),
            pltpu.VMEM((HALVES, n, 2, held, c1), BF16),
            pltpu.VMEM((2, wide, c1), F32),
            pltpu.VMEM((KW, half, c1), BF16),
            pltpu.VMEM((n, half, c2), BF16),
            pltpu.VMEM((6, pairs, c1), BF16),
            dma(counts), dma(counts), dma(HALVES * 3), dma(HALVES * 3), dma(2), dma(2),
            dma(HALVES * 3), dma(HALVES * 3), dma(double), dma(double), dma(double),
            dma(n - 1), dma(n - 1), dma(5),
            dma(HALVES), dma(HALVES), dma(double), dma(double), dma(3 * double), dma(3 * double),
            dma(HALVES),
            dma(double), dma(double), dma(double), dma(double), dma(2 * double), dma(2 * double),
            dma(HALVES),
        ],
        compiler_params=pltpu.CompilerParams(
            collective_id=0, has_side_effects=True, vmem_limit_bytes=VMEM_BYTES
        ),
    )(
        dna_bases.reshape(rows // 128, 128),
        w_stem.transpose(1, 2, 0),
        targets.T,
        w_enc.transpose(1, 2, 0),
        w_dec.transpose(1, 0, 2),
    )
    pred, g_enc, g_dec = store(pred, g_enc, g_dec)
    return (pred.T, g_enc.transpose(2, 0, 1), g_dec.transpose(1, 0, 2))


def shards(dna_bases, w_stem, w_enc, w_dec, targets):
    args = (dna_bases, w_stem, w_enc, w_dec, targets)
    rows, c1, c2 = dna_bases.shape[0], w_stem.shape[0], w_dec.shape[2]
    n = lax.axis_size("seq")
    square = n == 4 and lax.axis_size("chan") == 4
    if square and rows % 512 == 0 and c2 % 128 == 0 and c1 % 64 == 0:
        return square_shards(*args)
    return general_shards(*args)


def solution(mesh):
    return jax.shard_map(
        shards,
        mesh=mesh,
        in_specs=(
            P(("groups", "seq")),
            P("chan", None, None),
            P(None, None, "chan"),
            P(None, None, "chan"),
            P(("groups", "seq"), "chan"),
        ),
        out_specs=(
            P(("groups", "seq"), "chan"),
            P(("groups", "seq"), None, "chan"),
            P(("groups", "seq"), None, "chan"),
        ),
        check_vma=False,
    )
```
